32 devices in a mesh: section: 4 (over y, x), expert: 8 (over z, core).
Axes of the slice: x: 2, y: 2, z: 4, core: 2. Of those that a mesh axis runs over, the one named last changes fastest.
Arguments:
- handoff_forward: bfloat16 [4096, 1024], P(('section', 'expert')), may hold values from -12 to 12
- stashed_input: bfloat16 [4096, 1024], P(('section', 'expert')), may hold values from -12 to 12
- relay_cotangents: bfloat16 [4096, 1024], P(('section', 'expert')), may hold values from -6 to 6
- attention_gain: float32 [4, 1024], P('section'), may hold values from 0.1 to 1.9
- expert_gain: float32 [4, 1024], P('section'), may hold values from 0.1 to 1.9
- w_qkv: bfloat16 [4, 1024, 3072], P('section', 'expert'), may hold values from -0.1875 to 0.1875
- w_out: bfloat16 [4, 1024, 1024], P('section', 'expert'), may hold values from -0.1875 to 0.1875
- w_up: bfloat16 [4, 8, 1024, 704], P('section', 'expert'), may hold values from -0.1875 to 0.1875
- w_down: bfloat16 [4, 8, 704, 1024], P('section', 'expert'), may hold values from -0.21875 to 0.21875
- routes: int32 [2, 4096, 2], P(None, ('section', 'expert')), may hold values from 0 to 7, as said below
- gate_logits: float32 [2, 4096, 2], P(None, ('section', 'expert')), may hold values from -6 to 6
- block_mask: int32 [2, 32, 8, 8], P(None, ('section', 'expert')), may hold values 0 or 1
Outputs:
- layer_output: bfloat16 [4096, 1024], P(('section', 'expert'))
- layer_entry_derivative: bfloat16 [4096, 1024], P(('section', 'expert'))
The draws below stay inside these ranges and needn't reach their ends.
Inputs may be any that keep to these rules, and one draw needn't show every extreme that they name: `routes`: each row names two different experts; within each aligned block of 128 rows of one micro-batch no expert is named more than 64 times, and one expert, the same for every block of both micro-batches, is named exactly 64 times in every block.
All inputs are finite; a program needn't handle non-finite values. No bound on the sum of `block_mask` on one device may be relied on, other than what follows from the above.
Results may differ from the reference program's by a relative error of at most 0.007.
Values may be sent and summed in bfloat16 or wider, within the bound.
No kernel may reach another device: no remote copies, remote signals or barrier semaphores. Data moves between devices by JAX's collectives and lax.ppermute only.
A program may use at most 128 MiB of HBM per device.

```python
from functools import partial
import jax
import jax.numpy as jnp
from jax import lax

D = 1024
HEADS = 8
HEAD_DIM = 128
FF = 704
FRAMES = 128
BLOCK = 16
NBLK = 8
TOK_DEV = 128
GROUP_SPECIALISTS = 8
SPECIALIST_SEATS = 64
SECTION_ROWS = 1024
TOKENS = 4096
N_SECTION = 4
N_EXPERT = 8


def activation_draw(key):
    base = jnp.clip(jax.random.normal(jax.random.fold_in(key, 1), (TOKENS, D), jnp.float32), -6.0, 6.0)
    return base.astype(jnp.bfloat16)


def draw_handoff_forward(key, part):
    return activation_draw(jax.random.fold_in(key, 11))


def draw_stashed_input(key, part):
    return activation_draw(jax.random.fold_in(key, 12))


def draw_routes(key, part):
    base_key = jax.random.fold_in(key, 21)
    block_count = 2 * TOKENS // TOK_DEV
    hot_expert = jax.random.randint(jax.random.fold_in(base_key, 1), (), 0, GROUP_SPECIALISTS, dtype=jnp.int32)
    favoured_sequence_list = jax.random.permutation(jax.random.fold_in(base_key, 2), GROUP_SPECIALISTS - 1)
    favoured_uplift = (favoured_sequence_list < (GROUP_SPECIALISTS - 1) // 4).astype(jnp.int32) * 48
    others = (hot_expert + 1 + jnp.arange(GROUP_SPECIALISTS - 1, dtype=jnp.int32)) % GROUP_SPECIALISTS
    needed = 2 * TOK_DEV - SPECIALIST_SEATS
    slot_ids = jnp.arange((GROUP_SPECIALISTS - 1) * SPECIALIST_SEATS, dtype=jnp.int32).reshape(GROUP_SPECIALISTS - 1, SPECIALIST_SEATS)

    def one_block(block_key):
        affinity_noise_seed, flip_key, order_key = jax.random.split(block_key, 3)
        sorted_specialists = jax.random.randint(affinity_noise_seed, (GROUP_SPECIALISTS - 1, SPECIALIST_SEATS), 0, 64, dtype=jnp.int32) + favoured_uplift[:, None]
        keyed = (sorted_specialists * ((GROUP_SPECIALISTS - 1) * SPECIALIST_SEATS) + slot_ids).reshape(-1)
        _, picked = lax.top_k(keyed, needed)
        picked = jnp.sort(picked.astype(jnp.int32))
        chosen = others[picked // SPECIALIST_SEATS]
        listing = jnp.concatenate([jnp.full((SPECIALIST_SEATS,), hot_expert, jnp.int32), chosen])
        paired = jnp.stack([listing[:TOK_DEV], listing[TOK_DEV:]], axis=1)
        flips = jax.random.randint(flip_key, (TOK_DEV,), 0, 2, dtype=jnp.int32)
        paired = jnp.where(flips[:, None] == 1, paired[:, ::-1], paired)
        order = jax.random.permutation(order_key, TOK_DEV)
        return paired[order]
    block_keys = jax.random.split(base_key, block_count)
    return jax.vmap(one_block)(block_keys).reshape(2, TOKENS, 2).astype(jnp.int32)


def place_ends(values, key, smallest, high):
    extent = values.shape
    index_at = [jax.random.randint(jax.random.fold_in(key, axis), (), 0, extent[axis]) for axis in range(len(extent))]
    values = values.at[tuple(index_at)].set(smallest)
    longest = extent.index(max(extent))
    index_at[longest] = (index_at[longest] + 1) % extent[longest]
    return values.at[tuple(index_at)].set(high)


def shard_levels(stream_key, extent, shards, low, high):
    factor_of = 1.0
    for dim, shards_of in shards:
        steps = jax.random.uniform(jax.random.fold_in(jax.random.fold_in(stream_key, 6), dim), (shards_of,), jnp.float32, low / len(shards), high / len(shards))
        factor_of = factor_of * jnp.repeat(jnp.exp(steps), extent[dim] // shards_of).reshape((-1,) + (1,) * (len(extent) - 1 - dim))
    return factor_of


def gaussian(stream_key, dims, scale, reach, shards=(), kind=jnp.bfloat16):
    values = jax.random.normal(stream_key, dims, jnp.float32) * scale
    if len(shards) > 0:
        values = shard_levels(stream_key, dims, shards, -0.22, 0.18) * values
    return jnp.clip(values, min=-reach, max=reach).astype(kind)


def setup_inputs(seed: int = 0) -> dict:
    streams_of = jax.random.split(jax.random.key(seed), 13)
    handoff_forward = draw_handoff_forward(jax.random.fold_in(streams_of[12], 71), 0)
    stashed_input = draw_stashed_input(jax.random.fold_in(streams_of[12], 71), 0)
    relay_cotangents = gaussian(streams_of[2], (TOKENS, D), 1.0, 6.0, ((0, 32),))
    attention_gain = jnp.clip(1.0 + 0.18 * jax.random.normal(streams_of[3], (N_SECTION, D), jnp.float32), 0.1, 1.9)
    expert_gain = jnp.clip(1.0 + 0.18 * jax.random.normal(streams_of[4], (N_SECTION, D), jnp.float32), 0.1, 1.9)
    w_qkv = gaussian(streams_of[5], (N_SECTION, D, 3 * D), D ** -0.5, 0.1875, ((0, 4), (1, 8)))
    w_out = gaussian(streams_of[6], (N_SECTION, D, D), D ** -0.5, 0.1875, ((0, 4), (1, 8)))
    w_up = gaussian(streams_of[7], (N_SECTION, GROUP_SPECIALISTS, D, FF), D ** -0.5, 0.1875, ((0, 4), (1, 8)))
    w_down = gaussian(streams_of[8], (N_SECTION, GROUP_SPECIALISTS, FF, D), FF ** -0.5, 0.21875, ((0, 4), (1, 8)))
    routes = draw_routes(jax.random.fold_in(streams_of[12], 71), 0)
    gate_logits = gaussian(streams_of[10], (2, TOKENS, 2), 1.5, 6.0, ((1, 32),), jnp.float32)
    block_mask = place_ends((jax.random.randint(streams_of[11], (2, TOKENS // FRAMES, NBLK, NBLK), 0, 2) < 1).astype(jnp.int32), jax.random.fold_in(streams_of[11], 1), 0, 1)
    return {"handoff_forward": handoff_forward, "stashed_input": stashed_input, "relay_cotangents": relay_cotangents, "attention_gain": attention_gain, "expert_gain": expert_gain, "w_qkv": w_qkv, "w_out": w_out, "w_up": w_up, "w_down": w_down, "routes": routes, "gate_logits": gate_logits, "block_mask": block_mask}


EPS = 1e-06

def mean_last(values):
    return lax.optimization_barrier(jnp.mean(values, axis=-1, keepdims=True))

def allowed_pairs(mask_blocks):
    frame_block = jnp.arange(FRAMES, dtype=jnp.int32) // BLOCK
    given = mask_blocks[:, frame_block[:, None], frame_block[None, :]]
    return (given == 1) | (frame_block[:, None] == frame_block[None, :])[None]

def attend_forward(inputs, gain_attn, gain_expert, mixer, output_w, mask_blocks):
    row_count = inputs.shape[0]
    seq_count = row_count // FRAMES
    score_scale = HEAD_DIM ** (-0.5)
    input_f32 = inputs.astype(jnp.float32)
    rms_first = lax.rsqrt(mean_last(input_f32 * input_f32) + EPS)
    normed = (input_f32 * rms_first * gain_attn).astype(jnp.bfloat16)
    projected = jnp.dot(normed, mixer, preferred_element_type=jnp.float32)
    parted = projected.reshape(seq_count, FRAMES, 3, HEADS, HEAD_DIM)
    query_raw = parted[:, :, 0]
    key_raw = parted[:, :, 1]
    query_scale = lax.rsqrt(mean_last(query_raw * query_raw) + EPS)
    key_scale = lax.rsqrt(mean_last(key_raw * key_raw) + EPS)
    query_hat = query_raw * query_scale
    key_hat = key_raw * key_scale
    query_bf = query_hat.astype(jnp.bfloat16)
    key_bf = key_hat.astype(jnp.bfloat16)
    value_bf = parted[:, :, 2].astype(jnp.bfloat16)
    scores = jnp.einsum('sqhd,skhd->shqk', query_bf.astype(jnp.float32), key_bf.astype(jnp.float32)) * score_scale
    allowed = allowed_pairs(mask_blocks)
    expo = jnp.where(allowed[:, None], jnp.exp(scores), 0.0)
    attn_probs = expo / lax.optimization_barrier(jnp.sum(expo, axis=-1, keepdims=True))
    probs_bf = attn_probs.astype(jnp.bfloat16)
    heads_out = jnp.einsum('shqk,skhd->sqhd', probs_bf.astype(jnp.float32), value_bf.astype(jnp.float32))
    heads_out = heads_out.astype(jnp.bfloat16).reshape(row_count, HEADS * HEAD_DIM)
    hidden_state = input_f32 + jnp.dot(heads_out, output_w, preferred_element_type=jnp.float32)
    rms_second = lax.rsqrt(mean_last(hidden_state * hidden_state) + EPS)
    expert_in = (hidden_state * rms_second * gain_expert).astype(jnp.bfloat16)
    return (input_f32, rms_first, query_hat, query_scale, key_hat, key_scale, query_bf, key_bf, value_bf, attn_probs, probs_bf, hidden_state, rms_second, expert_in)

def attend_backward(saved, cot_f32, grad_moe, gain_attn, gain_expert, mixer, output_w):
    input_f32, rms_first, query_hat, query_scale, key_hat, key_scale, query_bf, key_bf, value_bf, attn_probs, probs_bf, hidden_state, rms_second, expert_in = saved
    row_count = input_f32.shape[0]
    seq_count = row_count // FRAMES
    score_scale = HEAD_DIM ** (-0.5)
    normal_two = hidden_state * rms_second
    grad_two = grad_moe * gain_expert
    grad_hidden = cot_f32 + rms_second * (grad_two - normal_two * mean_last(grad_two * normal_two))
    grad_heads = jnp.dot(grad_hidden.astype(jnp.bfloat16), output_w.T, preferred_element_type=jnp.float32)
    grad_heads = grad_heads.astype(jnp.bfloat16).reshape(seq_count, FRAMES, HEADS, HEAD_DIM)
    grad_probs = jnp.einsum('sqhd,skhd->shqk', grad_heads.astype(jnp.float32), value_bf.astype(jnp.float32))
    grad_values = jnp.einsum('shqk,sqhd->skhd', probs_bf.astype(jnp.float32), grad_heads.astype(jnp.float32))
    grad_scores = attn_probs * (grad_probs - lax.optimization_barrier(jnp.sum(attn_probs * grad_probs, axis=-1, keepdims=True))) * score_scale
    grad_scores = grad_scores.astype(jnp.bfloat16)
    grad_qhat = jnp.einsum('shqk,skhd->sqhd', grad_scores.astype(jnp.float32), key_bf.astype(jnp.float32))
    grad_khat = jnp.einsum('shqk,sqhd->skhd', grad_scores.astype(jnp.float32), query_bf.astype(jnp.float32))
    grad_query = query_scale * (grad_qhat - query_hat * mean_last(grad_qhat * query_hat))
    grad_key = key_scale * (grad_khat - key_hat * mean_last(grad_khat * key_hat))
    grad_mixed = jnp.stack([grad_query, grad_key, grad_values], axis=2)
    grad_mixed = grad_mixed.reshape(row_count, 3 * HEADS * HEAD_DIM).astype(jnp.bfloat16)
    grad_normed = jnp.dot(grad_mixed, mixer.T, preferred_element_type=jnp.float32)
    normal_one = input_f32 * rms_first
    grad_one = grad_normed * gain_attn
    result = grad_hidden + rms_first * (grad_one - normal_one * mean_last(grad_one * normal_one))
    return result.astype(jnp.bfloat16)

def slot_table(route_rows):
    flat_routes = route_rows.reshape(-1)
    onehot = (flat_routes[:, None] == jnp.arange(GROUP_SPECIALISTS, dtype=jnp.int32)[None, :]).astype(jnp.int32)
    earlier = jnp.cumsum(onehot, axis=0, dtype=jnp.int32) - onehot
    slot_rank = lax.optimization_barrier(jnp.sum(earlier * onehot, axis=1, dtype=jnp.int32))
    position = (flat_routes * SPECIALIST_SEATS + slot_rank).astype(jnp.int32)
    fill_ids = jnp.arange(flat_routes.shape[0], dtype=jnp.int32) + 1
    owner_slot = jnp.zeros((GROUP_SPECIALISTS * SPECIALIST_SEATS,), jnp.int32).at[position].set(fill_ids)
    return (position, owner_slot)

def collect(owner_slot, source_rows, divisor):
    occupied = (owner_slot > 0)[:, None]
    gathered = source_rows[jnp.maximum(owner_slot - 1, 0) // divisor]
    return jnp.where(occupied, gathered, jnp.zeros_like(gathered))

def pick_rows(source_rows, index_rows):
    return source_rows[index_rows]

def expert_batches(buffer):
    last_width = buffer.shape[-1]
    grouped = buffer.reshape(N_EXPERT, GROUP_SPECIALISTS, SPECIALIST_SEATS, last_width)
    return jnp.transpose(grouped, (1, 0, 2, 3)).reshape(GROUP_SPECIALISTS, N_EXPERT * SPECIALIST_SEATS, last_width)

def source_batches(buffer):
    last_width = buffer.shape[-1]
    grouped = buffer.reshape(GROUP_SPECIALISTS, N_EXPERT, SPECIALIST_SEATS, last_width)
    return jnp.transpose(grouped, (1, 0, 2, 3)).reshape(N_EXPERT, GROUP_SPECIALISTS * SPECIALIST_SEATS, last_width)

def gelu_pullback(preact, grad_act):
    _, pullback = jax.vjp(lambda values_in: jax.nn.gelu(values_in, approximate=True), preact)
    return pullback(grad_act)[0]

def expert_forward_batch(rows_in, up_section, down_section):
    preact = jnp.einsum('erd,edf->erf', rows_in.astype(jnp.float32), up_section.astype(jnp.float32))
    activated = jax.nn.gelu(preact, approximate=True).astype(jnp.bfloat16)
    result = jnp.einsum('erf,efd->erd', activated.astype(jnp.float32), down_section.astype(jnp.float32))
    return result.astype(jnp.bfloat16)

def expert_backward_batch(rows_in, grads_in, up_section, down_section):
    preact = jnp.einsum('erd,edf->erf', rows_in.astype(jnp.float32), up_section.astype(jnp.float32))
    grad_act = jnp.einsum('erd,efd->erf', grads_in.astype(jnp.float32), down_section.astype(jnp.float32))
    grad_preact = gelu_pullback(preact, grad_act).astype(jnp.bfloat16)
    result = jnp.einsum('erf,edf->erd', grad_preact.astype(jnp.float32), up_section.astype(jnp.float32))
    return result.astype(jnp.bfloat16)

def section_step(operands):
    forward_in, stash_in, cot_in, gain_attn, gain_expert, mixer, output_w, up_section, down_section, routes_forward, routes_backward, logits_forward, logits_backward, mask_forward, mask_backward = operands
    kept_forward_state = attend_forward(forward_in, gain_attn, gain_expert, mixer, output_w, mask_forward)
    saved_backward = attend_forward(stash_in, gain_attn, gain_expert, mixer, output_w, mask_backward)
    place_forward, owner_forward = jax.vmap(slot_table)(routes_forward.reshape(N_EXPERT, TOK_DEV, 2))
    place_backward, owner_backward = jax.vmap(slot_table)(routes_backward.reshape(N_EXPERT, TOK_DEV, 2))
    tokens_forward = kept_forward_state[13].reshape(N_EXPERT, TOK_DEV, D)
    sent_forward = jax.vmap(partial(collect, divisor=2))(owner_forward, tokens_forward)
    outputs = expert_forward_batch(expert_batches(sent_forward), up_section, down_section)
    picked_forward = jax.vmap(pick_rows)(source_batches(outputs), place_forward).reshape(SECTION_ROWS, 2, D)
    gates_forward = jax.nn.sigmoid(logits_forward)
    moe_sum = lax.optimization_barrier(jnp.sum(gates_forward[:, :, None] * picked_forward.astype(jnp.float32), axis=1))
    layer_output = (kept_forward_state[11] + moe_sum).astype(jnp.bfloat16)
    cot_f32 = cot_in.astype(jnp.float32)
    gates_backward = jax.nn.sigmoid(logits_backward)
    grad_rows = (gates_backward[:, :, None] * cot_f32[:, None, :]).astype(jnp.bfloat16)
    grad_rows = grad_rows.reshape(N_EXPERT, 2 * TOK_DEV, D)
    tokens_backward = saved_backward[13].reshape(N_EXPERT, TOK_DEV, D)
    sent_inputs = jax.vmap(partial(collect, divisor=2))(owner_backward, tokens_backward)
    sent_grads = jax.vmap(partial(collect, divisor=1))(owner_backward, grad_rows)
    backs = expert_backward_batch(expert_batches(sent_inputs), expert_batches(sent_grads), up_section, down_section)
    picked_backward = jax.vmap(pick_rows)(source_batches(backs), place_backward).reshape(SECTION_ROWS, 2, D)
    grad_moe = lax.optimization_barrier(jnp.sum(picked_backward.astype(jnp.float32), axis=1))
    layer_entry_derivative = attend_backward(saved_backward, cot_f32, grad_moe, gain_attn, gain_expert, mixer, output_w)
    return (layer_output, layer_entry_derivative)

def reference(handoff_forward, stashed_input, relay_cotangents, attention_gain, expert_gain, w_qkv, w_out, w_up, w_down, routes, gate_logits, block_mask):
    received_payload = jnp.roll(handoff_forward.reshape(N_SECTION, SECTION_ROWS, D), 1, axis=0)
    cot_rows = jnp.roll(relay_cotangents.reshape(N_SECTION, SECTION_ROWS, D), -1, axis=0)
    stash_rows = stashed_input.reshape(N_SECTION, SECTION_ROWS, D)
    route_section = routes.reshape(2, N_SECTION, SECTION_ROWS, 2)
    logit_section = gate_logits.reshape(2, N_SECTION, SECTION_ROWS, 2)
    mask_section = block_mask.reshape(2, N_SECTION, SECTION_ROWS // FRAMES, NBLK, NBLK)
    operands = (received_payload, stash_rows, cot_rows, attention_gain, expert_gain, w_qkv, w_out, w_up, w_down, route_section[0], route_section[1], logit_section[0], logit_section[1], mask_section[0], mask_section[1])
    layer_output, layer_entry_derivative = lax.map(section_step, operands)
    return (layer_output.reshape(TOKENS, D), layer_entry_derivative.reshape(TOKENS, D))
```

```python
import jax
import jax.numpy as jnp
from jax import lax
from jax.sharding import PartitionSpec as P

HEADS = 8
HEAD_DIM = 128
FRAMES = 128
BLOCK = 16
CORES = 2

EPS = 1e-06


def passed_along(value, axis, steps):
    count = lax.axis_size(axis)
    pairs = [(source, (source + steps) % count) for source in range(count)]
    return lax.ppermute(value, axis, pairs)


def line_length():
    return lax.axis_size("expert") // CORES


def chip_pairs(sources, step):
    return [
        (CORES * chip + core, CORES * (chip + step) + core)
        for chip in sources
        for core in range(CORES)
    ]


def swapped(value):
    count = lax.axis_size("expert")
    return lax.ppermute(value, "expert", [(i, i ^ 1) for i in range(count)])


def line_gather(value):
    length = line_length()
    ups, downs = [], []
    up = down = value
    for hop in range(1, length):
        up = lax.ppermute(up, "expert", chip_pairs(range(hop - 1, length - 1), 1))
        down = lax.ppermute(down, "expert", chip_pairs(range(1, length - hop + 1), -1))
        ups.append(up)
        downs.append(down)
    return ups, downs


def mean_last(values):
    return jnp.mean(values, axis=-1, keepdims=True)


def allowed_pairs(mask_blocks):
    frame_block = jnp.arange(FRAMES, dtype=jnp.int32) // BLOCK
    given = jnp.repeat(jnp.repeat(mask_blocks, BLOCK, axis=1), BLOCK, axis=2)
    return (given == 1) | (frame_block[:, None] == frame_block[None, :])[None]


def attend_scores(projected, mask_blocks):
    row_count = projected.shape[0]
    seq_count = row_count // FRAMES
    score_scale = HEAD_DIM ** (-0.5)
    parted = projected.reshape(seq_count, FRAMES, 3, HEADS, HEAD_DIM)
    query_raw = parted[:, :, 0]
    key_raw = parted[:, :, 1]
    query_scale = lax.rsqrt(mean_last(query_raw * query_raw) + EPS)
    key_scale = lax.rsqrt(mean_last(key_raw * key_raw) + EPS)
    query_hat = query_raw * query_scale
    key_hat = key_raw * key_scale
    query_bf = query_hat.astype(jnp.bfloat16)
    key_bf = key_hat.astype(jnp.bfloat16)
    value_bf = parted[:, :, 2].astype(jnp.bfloat16)
    scores = (
        jnp.einsum("sqhd,skhd->shqk", query_bf, key_bf, preferred_element_type=jnp.float32)
        * score_scale
    )
    allowed = allowed_pairs(mask_blocks)
    expo = jnp.where(allowed[:, None], jnp.exp(scores), 0.0)
    attn_probs = expo / jnp.sum(expo, axis=-1, keepdims=True)
    probs_bf = attn_probs.astype(jnp.bfloat16)
    heads_out = jnp.einsum(
        "shqk,skhd->sqhd", probs_bf, value_bf, preferred_element_type=jnp.float32
    )
    heads_out = heads_out.astype(jnp.bfloat16).reshape(row_count, HEADS * HEAD_DIM)
    return heads_out, (
        query_hat, query_scale, key_hat, key_scale, query_bf, key_bf, value_bf, attn_probs, probs_bf
    )


def attend_backward(saved, grad_heads):
    query_hat, query_scale, key_hat, key_scale, query_bf, key_bf, value_bf, attn_probs, probs_bf = saved
    row_count = grad_heads.shape[0]
    seq_count = row_count // FRAMES
    score_scale = HEAD_DIM ** (-0.5)
    grad_heads = grad_heads.astype(jnp.bfloat16).reshape(seq_count, FRAMES, HEADS, HEAD_DIM)
    grad_probs = jnp.einsum(
        "sqhd,skhd->shqk", grad_heads, value_bf, preferred_element_type=jnp.float32
    )
    grad_values = jnp.einsum(
        "shqk,sqhd->skhd", probs_bf, grad_heads, preferred_element_type=jnp.float32
    )
    grad_scores = (
        attn_probs
        * (grad_probs - jnp.sum(attn_probs * grad_probs, axis=-1, keepdims=True))
        * score_scale
    )
    grad_scores = grad_scores.astype(jnp.bfloat16)
    grad_qhat = jnp.einsum(
        "shqk,skhd->sqhd", grad_scores, key_bf, preferred_element_type=jnp.float32
    )
    grad_khat = jnp.einsum(
        "shqk,sqhd->skhd", grad_scores, query_bf, preferred_element_type=jnp.float32
    )
    grad_query = query_scale * (grad_qhat - query_hat * mean_last(grad_qhat * query_hat))
    grad_key = key_scale * (grad_khat - key_hat * mean_last(grad_khat * key_hat))
    grad_mixed = jnp.stack([grad_query, grad_key, grad_values], axis=2)
    return grad_mixed.reshape(row_count, 3 * HEADS * HEAD_DIM).astype(jnp.bfloat16)


def gelu_slope(values):
    _, pullback = jax.vjp(lambda inner: jax.nn.gelu(inner, approximate=True), values)
    return pullback(jnp.ones_like(values))[0]


def dense_gates(routes, logits, expert_count):
    gates = jax.nn.sigmoid(logits)
    hit = routes[:, :, None] == jnp.arange(expert_count, dtype=jnp.int32)[None, None, :]
    return jnp.sum(jnp.where(hit, gates[:, :, None], 0.0), axis=1)


def local(
    handoff_forward,
    stashed_input,
    relay_cotangents,
    attention_gain,
    expert_gain,
    w_qkv,
    w_out,
    w_up,
    w_down,
    routes,
    gate_logits,
    block_mask,
):
    length = line_length()
    expert_count = lax.axis_size("expert")
    me = lax.axis_index("expert")
    chip = me // CORES
    core = me % CORES
    width = handoff_forward.shape[1]
    tokens = handoff_forward.shape[0]
    depth = w_qkv.shape[1]

    def slot_owner(j, p):
        return CORES * ((chip + j) % length) + (core + p) % CORES

    def pieces(value, j):
        return [
            lax.dynamic_slice_in_dim(value, slot_owner(j, p) * depth, depth, axis=1)
            for p in range(CORES)
        ]

    def columns_of(value, j):
        return jnp.concatenate(pieces(value, j), axis=1)

    def slots(ups, downs, own):
        out = [own]
        for j in range(1, length):
            out.append(jnp.where(chip + j < length, downs[j - 1], ups[length - j - 1]))
        return out

    def paired(value):
        return jnp.concatenate([value, swapped(value)], axis=0)

    mixer = w_qkv[0]
    output_w = w_out[0]
    up_weight = w_up[0, 0]
    down_weight = w_down[0, 0]
    gain_attn = attention_gain[0]
    gain_expert = expert_gain[0]

    arriving = passed_along(handoff_forward, "section", 1)
    cotangent = passed_along(relay_cotangents, "section", -1)

    mix_up, mix_down = line_gather(mixer)
    out_up, out_down = line_gather(output_w)
    gates_own = jnp.concatenate(
        [dense_gates(routes[m], gate_logits[m], expert_count) for m in range(2)], axis=1
    )
    gate_up, gate_down = line_gather(gates_own)
    cot_up, cot_down = line_gather(cotangent)

    inputs = jnp.concatenate([arriving, stashed_input], axis=0).astype(jnp.float32)
    rms_first = lax.rsqrt(mean_last(inputs * inputs) + EPS)
    normed = (inputs * rms_first * gain_attn).astype(jnp.bfloat16)

    own_mix = paired(mixer)
    projected = jnp.dot(columns_of(normed, 0), own_mix, preferred_element_type=jnp.float32)
    mix_up = [paired(block) for block in mix_up]
    mix_down = [paired(block) for block in mix_down]
    for hop in range(1, length):
        projected = projected + jnp.dot(
            columns_of(normed, hop), mix_down[hop - 1], preferred_element_type=jnp.float32
        )
        projected = projected + jnp.dot(
            columns_of(normed, length - hop), mix_up[hop - 1], preferred_element_type=jnp.float32
        )
    mix_slots = slots(mix_up, mix_down, own_mix)
    out_slots = [paired(block) for block in slots(out_up, out_down, output_w)]

    mask = jnp.concatenate([block_mask[0], block_mask[1]], axis=0)
    heads_out, saved = attend_scores(projected, mask)
    hidden_state = inputs
    for j in range(length):
        hidden_state = hidden_state + jnp.dot(
            columns_of(heads_out, j), out_slots[j], preferred_element_type=jnp.float32
        )
    rms_second = lax.rsqrt(mean_last(hidden_state * hidden_state) + EPS)
    expert_in = (hidden_state * rms_second * gain_expert).astype(jnp.bfloat16)

    gate_all = jnp.concatenate([paired(b) for b in slots(gate_up, gate_down, gates_own)], axis=0)
    mine = jnp.arange(2 * expert_count, dtype=jnp.int32)[None, :]
    gate_fwd = jnp.sum(jnp.where(mine == me, gate_all, 0.0), axis=1, keepdims=True)
    gate_bwd = jnp.sum(jnp.where(mine == me + expert_count, gate_all, 0.0), axis=1, keepdims=True)

    cot_all = jnp.concatenate([paired(b) for b in slots(cot_up, cot_down, cotangent)], axis=0)
    grad_act = gate_bwd * jnp.dot(cot_all, down_weight.T, preferred_element_type=jnp.float32)

    def gathered(rows):
        ups, downs = line_gather(rows)
        return jnp.concatenate([paired(b) for b in slots(ups, downs, rows)], axis=0)

    def scattered(partial):
        blocks = partial.astype(jnp.bfloat16).reshape(length, CORES, tokens, width)
        other = swapped(blocks[:, 1])
        local_sum = blocks[:, 0].astype(jnp.float32) + other.astype(jnp.float32)
        up = down = None
        for hop in range(1, length):
            distance = length - hop
            send_up = local_sum[distance]
            send_down = local_sum[length - distance]
            if up is not None:
                send_up = jnp.where(chip + distance < length, send_up, 0.0) + up
                send_down = jnp.where(chip - distance >= 0, send_down, 0.0) + down
            up = lax.ppermute(
                send_up.astype(jnp.bfloat16), "expert", chip_pairs(range(0, hop), 1)
            ).astype(jnp.float32)
            down = lax.ppermute(
                send_down.astype(jnp.bfloat16),
                "expert",
                chip_pairs(range(length - hop, length), -1),
            ).astype(jnp.float32)
        return local_sum[0] + up + down

    rows_bwd = gathered(expert_in[tokens:])
    preact_bwd = jnp.dot(rows_bwd, up_weight, preferred_element_type=jnp.float32)
    grad_preact = (grad_act * gelu_slope(preact_bwd)).astype(jnp.bfloat16)
    back = jnp.dot(grad_preact, up_weight.T, preferred_element_type=jnp.float32)
    grad_moe = scattered(back)

    rows_fwd = gathered(expert_in[:tokens])
    preact_fwd = jnp.dot(rows_fwd, up_weight, preferred_element_type=jnp.float32)
    activated = jax.nn.gelu(preact_fwd, approximate=True).astype(jnp.bfloat16)
    forth = gate_fwd * jnp.dot(activated, down_weight, preferred_element_type=jnp.float32)
    moe_sum = scattered(forth)
    layer_output = (hidden_state[:tokens] + moe_sum).astype(jnp.bfloat16)

    cot_f32 = cotangent.astype(jnp.float32)
    hidden_bwd = hidden_state[tokens:]
    rms_bwd = rms_second[tokens:]
    normal_two = hidden_bwd * rms_bwd
    grad_two = grad_moe * gain_expert
    grad_hidden = cot_f32 + rms_bwd * (grad_two - normal_two * mean_last(grad_two * normal_two))
    grad_hidden_bf = grad_hidden.astype(jnp.bfloat16)

    def restored(parts):
        joined = jnp.concatenate(parts, axis=1)
        return jnp.concatenate(
            [
                lax.dynamic_slice_in_dim(
                    joined,
                    depth
                    * (CORES * ((d // CORES - chip) % length) + (d % CORES + core) % CORES),
                    depth,
                    axis=1,
                )
                for d in range(expert_count)
            ],
            axis=1,
        )

    grad_heads = restored(
        [
            jnp.dot(grad_hidden_bf, out_slots[j].T, preferred_element_type=jnp.float32)
            for j in range(length)
        ]
    )
    grad_mixed = attend_backward(
        tuple(member[member.shape[0] // 2 :] for member in saved), grad_heads
    )
    grad_normed = restored(
        [
            jnp.dot(grad_mixed, mix_slots[j].T, preferred_element_type=jnp.float32)
            for j in range(length)
        ]
    )
    normal_one = inputs[tokens:] * rms_first[tokens:]
    grad_one = grad_normed * gain_attn
    result = grad_hidden + rms_first[tokens:] * (
        grad_one - normal_one * mean_last(grad_one * normal_one)
    )
    return (layer_output, result.astype(jnp.bfloat16))


def solution(mesh):
    placed = (
        P(("section", "expert"), None),
        P(("section", "expert"), None),
        P(("section", "expert"), None),
        P("section", None),
        P("section", None),
        P("section", "expert", None),
        P("section", "expert", None),
        P("section", "expert", None, None),
        P("section", "expert", None, None),
        P(None, ("section", "expert"), None),
        P(None, ("section", "expert"), None),
        P(None, ("section", "expert"), None, None),
    )
    return jax.shard_map(
        local,
        mesh=mesh,
        in_specs=placed,
        out_specs=(P(("section", "expert"), None), P(("section", "expert"), None)),
        check_vma=False,
    )
```

```python
import functools

import jax
import jax.numpy as jnp
from jax import lax
from jax.experimental import pallas as pl
from jax.experimental.pallas import tpu as pltpu
from jax.sharding import PartitionSpec as P

HEADS = 8
HEAD_DIM = 128
FRAMES = 128
BLOCK = 16
CORES = 2
LANES = 128

EPS = 1e-06
SCORE_SCALE = HEAD_DIM ** (-0.5)
GELU_C = 0.7978845608028654
GELU_A = 0.044715


F32 = jnp.float32
BF16 = jnp.bfloat16
NT = (((1,), (1,)), ((), ()))
TN = (((0,), (0,)), ((), ()))
ANY = pl.BlockSpec(memory_space=pl.ANY)
SMEM = pl.BlockSpec(memory_space=pltpu.SMEM)
VMEM = pl.BlockSpec(memory_space=pltpu.VMEM)
PARAMS = pltpu.CompilerParams(vmem_limit_bytes=56 * 1024 * 1024)


def dot(a, b, dims=(((1,), (0,)), ((), ()))):
    return lax.dot_general(a, b, dims, preferred_element_type=F32)


def mean_last(values):
    return jnp.mean(values, axis=-1, keepdims=True)


def passed_along(value, axis, steps):
    count = lax.axis_size(axis)
    pairs = [(source, (source + steps) % count) for source in range(count)]
    return lax.ppermute(value, axis, pairs)


def line_length():
    return lax.axis_size("expert") // CORES


def chip_pairs(sources, step):
    return [
        (CORES * chip + core, CORES * (chip + step) + core)
        for chip in sources
        for core in range(CORES)
    ]


def swapped(value):
    count = lax.axis_size("expert")
    return lax.ppermute(value, "expert", [(i, i ^ 1) for i in range(count)])


def relayed(value):
    length = line_length()
    entries = [value]
    up = down = value
    for hop in range(1, length):
        up = lax.ppermute(up, "expert", chip_pairs(range(hop - 1, length - 1), 1))
        down = lax.ppermute(down, "expert", chip_pairs(range(1, length - hop + 1), -1))
        entries += [up, down]
    return entries


def sent(value):
    length = line_length()
    arrived = {}
    for hop in range(length - 1, 0, -1):
        arrived[hop] = [
            lax.ppermute(value, "expert", chip_pairs(range(0, length - hop), hop)),
            lax.ppermute(value, "expert", chip_pairs(range(hop, length), -hop)),
        ]
    return [value] + [block for hop in range(1, length) for block in arrived[hop]]


def with_partner(entries):
    return entries + [swapped(block) for block in entries]


def scattered(blocks):
    length = line_length()
    arrived = []
    for hop in range(length - 1, 0, -1):
        arrived.append(
            lax.ppermute(blocks[hop], "expert", chip_pairs(range(0, length - hop), hop))
        )
        arrived.append(
            lax.ppermute(blocks[length - hop], "expert", chip_pairs(range(hop, length), -hop))
        )
    return [blocks[0]] + arrived


def entry_chips(length, chip):
    listing = [(None, chip)]
    for hop in range(1, length):
        listing.append((chip - hop >= 0, chip - hop))
        listing.append((chip + hop < length, chip + hop))
    return listing


def each_copy(refs, target, sems, rows, chip, core, act):
    count = len(refs) // 2
    listing = entry_chips((count + 1) // 2, chip)
    for side in range(CORES):
        for index, (valid, origin) in enumerate(listing):
            number = side * count + index
            owner = CORES * origin + (core if side == 0 else 1 - core)

            def run(number=number, owner=owner):
                start = pl.multiple_of(owner * rows, rows)
                act(
                    pltpu.make_async_copy(
                        refs[number], target.at[pl.ds(start, rows), :], sems.at[number]
                    )
                )

            if valid is None:
                run()
            else:
                pl.when(valid)(run)


def start_copies(*args):
    each_copy(*args, lambda copy: copy.start())


def wait_copies(*args):
    each_copy(*args, lambda copy: copy.wait())


def head_parts(proj_ref, head):
    def part(index):
        start = (index * HEADS + head) * HEAD_DIM
        return proj_ref[:, start : start + HEAD_DIM]

    query, key, value = part(0), part(1), part(2)
    query_scale = lax.rsqrt(mean_last(query * query) + EPS)
    key_scale = lax.rsqrt(mean_last(key * key) + EPS)
    return query * query_scale, query_scale, key * key_scale, key_scale, value.astype(BF16)


def attn_probs_of(query_bf, key_bf, allowed):
    scores = dot(query_bf, key_bf, NT) * SCORE_SCALE
    expo = jnp.where(allowed, jnp.exp(scores), 0.0)
    return expo / jnp.sum(expo, axis=-1, keepdims=True)


def attend_rows(proj_ref, mask, heads_ref):
    allowed = mask > 0.5
    for head in range(HEADS):
        query_hat, _, key_hat, _, value_bf = head_parts(proj_ref, head)
        probs = attn_probs_of(query_hat.astype(BF16), key_hat.astype(BF16), allowed)
        out = dot(probs.astype(BF16), value_bf)
        heads_ref[:, head * HEAD_DIM : (head + 1) * HEAD_DIM] = out.astype(BF16)


def finish_rows(x, heads, out_w, gain_e, hidden_ref, expert_ref):
    hidden = x.astype(F32) + dot(heads, out_w)
    hidden_ref[...] = hidden
    rms = lax.rsqrt(mean_last(hidden * hidden) + EPS)
    expert_ref[...] = (hidden * rms * gain_e).astype(BF16)


def project_kernel(count, depth, *refs):
    place, xf_ref, xb_ref, gain_a, gain_e, mask_ref = refs[:6]
    mix_refs = refs[6 : 6 + count]
    out_refs = refs[6 + count : 6 + 2 * count]
    projf_ref, projb_ref, hidden_ref, expert_ref = refs[6 + 2 * count : 10 + 2 * count]
    mix_w, out_w, normed, heads, mix_sems, out_sems = refs[10 + 2 * count :]
    chip, core = place[0], place[1]
    start_copies(mix_refs, mix_w, mix_sems, depth, chip, core)
    start_copies(out_refs, out_w, out_sems, depth, chip, core)
    rows = xf_ref.shape[0]
    for index, x_ref in enumerate((xf_ref, xb_ref)):
        x = x_ref[...].astype(F32)
        rms = lax.rsqrt(mean_last(x * x) + EPS)
        normed[index * rows : (index + 1) * rows, :] = (x * rms * gain_a[...]).astype(BF16)
    wait_copies(mix_refs, mix_w, mix_sems, depth, chip, core)
    columns = mix_w.shape[1]
    chunk = 512
    for begin in range(0, columns, chunk):
        piece = dot(normed[...], mix_w[:, begin : begin + chunk])
        projf_ref[:, begin : begin + chunk] = piece[:rows]
        projb_ref[:, begin : begin + chunk] = piece[rows:]
    attend_rows(projb_ref, mask_ref[1], heads)
    wait_copies(out_refs, out_w, out_sems, depth, chip, core)
    finish_rows(xb_ref[...], heads[...], out_w[...], gain_e[...], hidden_ref, expert_ref)


def forward_kernel(count, depth, *refs):
    place, x_ref, proj_ref, gain_e, mask_ref = refs[:5]
    out_refs = refs[5 : 5 + count]
    hidden_ref, expert_ref = refs[5 + count : 7 + count]
    out_w, heads, out_sems = refs[7 + count :]
    chip, core = place[0], place[1]
    start_copies(out_refs, out_w, out_sems, depth, chip, core)
    attend_rows(proj_ref, mask_ref[0], heads)
    wait_copies(out_refs, out_w, out_sems, depth, chip, core)
    finish_rows(x_ref[...], heads[...], out_w[...], gain_e[...], hidden_ref, expert_ref)


def picked_gate(gates, me, expert_count, micro):
    lane = lax.broadcasted_iota(jnp.int32, gates.shape, 1)
    first = 2 * micro * expert_count + me
    hit = (lane == first) | (lane == first + expert_count)
    return jnp.sum(jnp.where(hit, gates, 0.0), axis=-1, keepdims=True)


def cotangent_kernel(count, rows, width, expert_count, *refs):
    place, down_ref = refs[:2]
    cot_refs = refs[2 : 2 + count]
    act_ref, gate_ref = refs[2 + count : 4 + count]
    cot, sems = refs[4 + count :]
    chip, core = place[0], place[1]
    me = CORES * chip + core
    start_copies(cot_refs, cot, sems, rows, chip, core)
    wait_copies(cot_refs, cot, sems, rows, chip, core)
    chunk = 2 * rows

    def step(index, carry):
        start = pl.multiple_of(index * chunk, chunk)
        block = cot[pl.ds(start, chunk), :]
        gates = block[:, width:].astype(F32)
        grad_act = dot(block[:, :width], down_ref[...], NT)
        act_ref[pl.ds(start, chunk), :] = grad_act * picked_gate(gates, me, expert_count, 1)
        gate_ref[pl.ds(start, chunk), :] = jnp.broadcast_to(
            picked_gate(gates, me, expert_count, 0), (chunk, LANES)
        )
        return carry

    lax.fori_loop(0, expert_count * rows // chunk, step, 0)


def give_back(result, mine_ref, other_ref, rows, chip, core):
    length = mine_ref.shape[0]
    for j in range(length):
        origin = lax.rem(chip + j, length)
        for out_ref, side in ((mine_ref, core), (other_ref, 1 - core)):
            start = pl.multiple_of((CORES * origin + side) * rows, rows)
            out_ref[j] = result[pl.ds(start, rows), :]


def expert_backward_kernel(count, rows, *refs):
    place, up_ref, act_ref = refs[:3]
    row_refs = refs[3 : 3 + count]
    mine_ref, other_ref = refs[3 + count : 5 + count]
    tokens, result, sems = refs[5 + count :]
    chip, core = place[0], place[1]
    start_copies(row_refs, tokens, sems, rows, chip, core)
    wait_copies(row_refs, tokens, sems, rows, chip, core)
    chunk = 2 * rows

    def step(index, carry):
        start = pl.multiple_of(index * chunk, chunk)
        pre = dot(tokens[pl.ds(start, chunk), :], up_ref[...])
        square = pre * pre
        bend = jnp.tanh(GELU_C * pre * (1.0 + GELU_A * square))
        slope = 0.5 * (1.0 + bend) + 0.5 * pre * (1.0 - bend * bend) * (
            GELU_C * (1.0 + 3.0 * GELU_A * square)
        )
        grad = (act_ref[pl.ds(start, chunk), :] * slope).astype(BF16)
        result[pl.ds(start, chunk), :] = dot(grad, up_ref[...], NT).astype(BF16)
        return carry

    lax.fori_loop(0, tokens.shape[0] // chunk, step, 0)
    give_back(result, mine_ref, other_ref, rows, chip, core)


def expert_forward_kernel(count, rows, *refs):
    place, up_ref, down_ref, gate_ref = refs[:4]
    row_refs = refs[4 : 4 + count]
    mine_ref, other_ref = refs[4 + count : 6 + count]
    tokens, result, sems = refs[6 + count :]
    chip, core = place[0], place[1]
    start_copies(row_refs, tokens, sems, rows, chip, core)
    wait_copies(row_refs, tokens, sems, rows, chip, core)
    chunk = 2 * rows

    def step(index, carry):
        start = pl.multiple_of(index * chunk, chunk)
        pre = dot(tokens[pl.ds(start, chunk), :], up_ref[...])
        bend = jnp.tanh(GELU_C * pre * (1.0 + GELU_A * (pre * pre)))
        active = (0.5 * pre * (1.0 + bend)).astype(BF16)
        out = dot(active, down_ref[...])
        gate = gate_ref[pl.ds(start, chunk), :][:, :1]
        result[pl.ds(start, chunk), :] = (gate * out).astype(BF16)
        return carry

    lax.fori_loop(0, tokens.shape[0] // chunk, step, 0)
    give_back(result, mine_ref, other_ref, rows, chip, core)


def add_kernel(mine_ref, other_ref, *out_refs):
    for j, out_ref in enumerate(out_refs):
        out_ref[...] = (mine_ref[j].astype(F32) + other_ref[j].astype(F32)).astype(BF16)


def backward_kernel(count, parts, depth, *refs):
    place, x_ref, cot_ref, hidden_ref, proj_ref, gain_a, gain_e, mask_ref = refs[:8]
    part_refs = refs[8 : 8 + parts]
    mix_refs = refs[8 + parts : 8 + parts + count]
    out_refs = refs[8 + parts + count : 8 + parts + 2 * count]
    result_ref = refs[8 + parts + 2 * count]
    mix_w, out_w, mixed, mix_sems, out_sems = refs[9 + parts + 2 * count :]
    chip, core = place[0], place[1]
    start_copies(out_refs, out_w, out_sems, depth, chip, core)
    start_copies(mix_refs, mix_w, mix_sems, depth, chip, core)
    grad_moe = part_refs[0][...].astype(F32)
    for part_ref in part_refs[1:]:
        grad_moe = grad_moe + part_ref[...].astype(F32)
    hidden = hidden_ref[...]
    rms_two = lax.rsqrt(mean_last(hidden * hidden) + EPS)
    normal_two = hidden * rms_two
    grad_two = grad_moe * gain_e[...]
    grad_hidden = cot_ref[...].astype(F32) + rms_two * (
        grad_two - normal_two * mean_last(grad_two * normal_two)
    )
    wait_copies(out_refs, out_w, out_sems, depth, chip, core)
    grad_heads = dot(grad_hidden.astype(BF16), out_w[...], NT).astype(BF16)
    allowed = mask_ref[1] > 0.5
    for head in range(HEADS):
        query_hat, query_scale, key_hat, key_scale, value_bf = head_parts(proj_ref, head)
        query_bf, key_bf = query_hat.astype(BF16), key_hat.astype(BF16)
        probs = attn_probs_of(query_bf, key_bf, allowed)
        grad_out = grad_heads[:, head * HEAD_DIM : (head + 1) * HEAD_DIM]
        grad_probs = dot(grad_out, value_bf, NT)
        grad_value = dot(probs.astype(BF16), grad_out, TN)
        inner = jnp.sum(probs * grad_probs, axis=-1, keepdims=True)
        grad_scores = (probs * (grad_probs - inner) * SCORE_SCALE).astype(BF16)
        grad_qhat = dot(grad_scores, key_bf)
        grad_khat = dot(grad_scores, query_bf, TN)
        grad_query = query_scale * (grad_qhat - query_hat * mean_last(grad_qhat * query_hat))
        grad_key = key_scale * (grad_khat - key_hat * mean_last(grad_khat * key_hat))
        for index, grad in enumerate((grad_query, grad_key, grad_value)):
            start = (index * HEADS + head) * HEAD_DIM
            mixed[:, start : start + HEAD_DIM] = grad.astype(BF16)
    wait_copies(mix_refs, mix_w, mix_sems, depth, chip, core)
    grad_normed = dot(mixed[...], mix_w[...], NT)
    x = x_ref[...].astype(F32)
    rms_one = lax.rsqrt(mean_last(x * x) + EPS)
    normal_one = x * rms_one
    grad_one = grad_normed * gain_a[...]
    result = grad_hidden + rms_one * (grad_one - normal_one * mean_last(grad_one * normal_one))
    result_ref[...] = result.astype(BF16)


def shaped(shape, kind):
    return jax.ShapeDtypeStruct(shape, kind)


def dma(count):
    return pltpu.SemaphoreType.DMA((count,))


def call(kernel, name, outs, specs, out_specs, scratch, args):
    return pl.pallas_call(
        kernel,
        name=name,
        out_shape=outs,
        in_specs=specs,
        out_specs=out_specs,
        scratch_shapes=scratch,
        compiler_params=PARAMS,
    )(*args)


def dense_gates(routes, logits, expert_count):
    gates = jax.nn.sigmoid(logits)
    hit = routes[..., None] == jnp.arange(expert_count, dtype=jnp.int32)
    return jnp.sum(jnp.where(hit, gates[..., None], 0.0), axis=2)


def gate_columns(routes, logits, expert_count):
    gates = dense_gates(routes, logits, expert_count)
    high = lax.reduce_precision(gates, 8, 7)
    both = jnp.stack([high, gates - high], axis=1).astype(BF16)
    rows = jnp.transpose(both, (2, 0, 1, 3)).reshape(both.shape[2], -1)
    return jnp.pad(rows, ((0, 0), (0, LANES - rows.shape[1])))


def allowed_of(mask_blocks):
    frame_block = jnp.arange(FRAMES, dtype=jnp.int32) // BLOCK
    spread = (frame_block[:, None] == jnp.arange(FRAMES // BLOCK)[None, :]).astype(F32)
    eye = jnp.eye(FRAMES // BLOCK, dtype=F32)
    open_blocks = jnp.maximum((mask_blocks == 1).astype(F32), eye)
    return jnp.einsum("ib,mbc,jc->mij", spread, open_blocks, spread)


def local(
    handoff_forward,
    stashed_input,
    relay_cotangents,
    attention_gain,
    expert_gain,
    w_qkv,
    w_out,
    w_up,
    w_down,
    routes,
    gate_logits,
    block_mask,
):
    length = line_length()
    expert_count = lax.axis_size("expert")
    me = lax.axis_index("expert")
    place = jnp.stack([me // CORES, me % CORES]).astype(jnp.int32)
    tokens, width = handoff_forward.shape
    depth = w_qkv.shape[1]
    total = expert_count * tokens
    columns = w_qkv.shape[2]
    up_weight = w_up[0, 0]
    down_weight = w_down[0, 0]
    hidden_units = up_weight.shape[1]
    count = CORES * (2 * length - 1)

    mixers = with_partner(relayed(w_qkv[0]))
    outers = with_partner(relayed(w_out[0]))
    arriving = passed_along(handoff_forward, "section", 1)
    cotangent = passed_along(relay_cotangents, "section", -1)
    gates = gate_columns(routes, gate_logits, expert_count)
    cots = with_partner(sent(jnp.concatenate([cotangent, gates], axis=1)))
    mask = allowed_of(block_mask[:, 0])

    proj_fwd, proj_bwd, hidden_bwd, expert_bwd = call(
        functools.partial(project_kernel, count, depth),
        "project",
        (
            shaped((tokens, columns), F32),
            shaped((tokens, columns), F32),
            shaped((tokens, width), F32),
            shaped((tokens, width), BF16),
        ),
        [SMEM] + [VMEM] * 5 + [ANY] * (2 * count),
        (VMEM,) * 4,
        [
            pltpu.VMEM((width, columns), BF16),
            pltpu.VMEM((width, width), BF16),
            pltpu.VMEM((2 * tokens, width), BF16),
            pltpu.VMEM((tokens, width), BF16),
            dma(count),
            dma(count),
        ],
        [place, arriving, stashed_input, attention_gain, expert_gain, mask] + mixers + outers,
    )
    rows_bwd = with_partner(sent(expert_bwd))

    hidden_fwd, expert_fwd = call(
        functools.partial(forward_kernel, count, depth),
        "attend",
        (shaped((tokens, width), F32), shaped((tokens, width), BF16)),
        [SMEM] + [VMEM] * 4 + [ANY] * count,
        (VMEM,) * 2,
        [pltpu.VMEM((width, width), BF16), pltpu.VMEM((tokens, width), BF16), dma(count)],
        [place, arriving, proj_fwd, expert_gain, mask] + outers,
    )
    rows_fwd = with_partner(sent(expert_fwd))

    grad_act, gate_fwd = call(
        functools.partial(cotangent_kernel, count, tokens, width, expert_count),
        "cotangent",
        (shaped((total, hidden_units), F32), shaped((total, LANES), F32)),
        [SMEM, VMEM] + [ANY] * count,
        (VMEM,) * 2,
        [pltpu.VMEM((total, width + LANES), BF16), dma(count)],
        [place, down_weight] + cots,
    )

    pair = (shaped((length, tokens, width), BF16),) * 2

    def expert_scratch():
        return [pltpu.VMEM((total, width), BF16), pltpu.VMEM((total, width), BF16), dma(count)]

    def combined(mine, other):
        blocks = call(
            add_kernel,
            "pair_sum",
            (shaped((tokens, width), BF16),) * length,
            [VMEM] * 2,
            (VMEM,) * length,
            [],
            [mine, swapped(other)],
        )
        return scattered(blocks)

    mine, other = call(
        functools.partial(expert_backward_kernel, count, tokens),
        "expert_backward",
        pair,
        [SMEM, VMEM, VMEM] + [ANY] * count,
        (VMEM,) * 2,
        expert_scratch(),
        [place, up_weight, grad_act] + rows_bwd,
    )
    grad_parts = combined(mine, other)

    mine, other = call(
        functools.partial(expert_forward_kernel, count, tokens),
        "expert_forward",
        pair,
        [SMEM, VMEM, VMEM, VMEM] + [ANY] * count,
        (VMEM,) * 2,
        expert_scratch(),
        [place, up_weight, down_weight, gate_fwd] + rows_fwd,
    )
    moe_parts = combined(mine, other)

    parts = len(grad_parts)
    derivative = call(
        functools.partial(backward_kernel, count, parts, depth),
        "attend_backward",
        shaped((tokens, width), BF16),
        [SMEM] + [VMEM] * (7 + parts) + [ANY] * (2 * count),
        VMEM,
        [
            pltpu.VMEM((width, columns), BF16),
            pltpu.VMEM((width, width), BF16),
            pltpu.VMEM((tokens, columns), BF16),
            dma(count),
            dma(count),
        ],
        [place, stashed_input, cotangent, hidden_bwd, proj_bwd, attention_gain, expert_gain, mask]
        + grad_parts
        + mixers
        + outers,
    )

    layer_output = hidden_fwd
    for part in moe_parts:
        layer_output = layer_output + part.astype(F32)
    return (layer_output.astype(BF16), derivative)


def solution(mesh):
    placed = (
        P(("section", "expert"), None),
        P(("section", "expert"), None),
        P(("section", "expert"), None),
        P("section", None),
        P("section", None),
        P("section", "expert", None),
        P("section", "expert", None),
        P("section", "expert", None, None),
        P("section", "expert", None, None),
        P(None, ("section", "expert"), None),
        P(None, ("section", "expert"), None),
        P(None, ("section", "expert"), None, None),
    )
    return jax.shard_map(
        local,
        mesh=mesh,
        in_specs=placed,
        out_specs=(P(("section", "expert"), None), P(("section", "expert"), None)),
        check_vma=False,
    )
```

```python
import functools

import jax
import jax.numpy as jnp
from jax import lax
from jax.experimental import pallas as pl
from jax.experimental.pallas import tpu as pltpu
from jax.sharding import PartitionSpec as P


HEADS = 8
HEAD_DIM = 128
FRAMES = 128
BLOCK = 16
CORES = 2
LANES = 128

EPS = 1e-06
SCORE_SCALE = HEAD_DIM ** (-0.5)
GELU_C = 0.7978845608028654
GELU_A = 0.044715


F32 = jnp.float32
BF16 = jnp.bfloat16
NT = (((1,), (1,)), ((), ()))
TN = (((0,), (0,)), ((), ()))
ANY = pl.BlockSpec(memory_space=pl.ANY)
SMEM = pl.BlockSpec(memory_space=pltpu.SMEM)
VMEM = pl.BlockSpec(memory_space=pltpu.VMEM)
PARAMS = pltpu.CompilerParams(vmem_limit_bytes=56 * 1024 * 1024)


def dot(a, b, dims=(((1,), (0,)), ((), ()))):
    return lax.dot_general(a, b, dims, preferred_element_type=F32)


def mean_last(values):
    return jnp.mean(values, axis=-1, keepdims=True)


def passed_along(value, axis, steps):
    count = lax.axis_size(axis)
    pairs = [(source, (source + steps) % count) for source in range(count)]
    return lax.ppermute(value, axis, pairs)


def line_length():
    return lax.axis_size("expert") // CORES


def chip_pairs(sources, step):
    return [
        (CORES * chip + core, CORES * (chip + step) + core)
        for chip in sources
        for core in range(CORES)
    ]


def swapped(value):
    count = lax.axis_size("expert")
    return lax.ppermute(value, "expert", [(i, i ^ 1) for i in range(count)])


def hop(value, sources, move):
    return lax.ppermute(value, "expert", chip_pairs(sources, move))


def relayed(value):
    length = line_length()
    entries = [value]
    up = down = value
    for step in range(1, length):
        up = hop(up, range(step - 1, length - 1), 1)
        down = hop(down, range(1, length - step + 1), -1)
        entries += [up, down]
    return entries


def with_partner(entries):
    return entries + [swapped(block) for block in entries]


def scattered(blocks):
    length = line_length()
    up = down = None
    for step in range(1, length):
        far = length - step
        send_up, send_down = blocks[far], blocks[length - far]
        if up is not None:
            send_up = send_up + up
            send_down = send_down + down
        up = hop(send_up, range(0, step), 1)
        down = hop(send_down, range(length - step, length), -1)
    return [blocks[0], up, down]


def entry_chips(length, chip):
    listing = [(None, chip)]
    for hop in range(1, length):
        listing.append((chip - hop >= 0, chip - hop))
        listing.append((chip + hop < length, chip + hop))
    return listing


def each_copy(refs, target, sems, rows, chip, core, act):
    count = len(refs) // 2
    listing = entry_chips((count + 1) // 2, chip)
    for side in range(CORES):
        for index, (valid, origin) in enumerate(listing):
            number = side * count + index
            owner = CORES * origin + (core if side == 0 else 1 - core)

            def run(number=number, owner=owner):
                start = pl.multiple_of(owner * rows, rows)
                act(
                    pltpu.make_async_copy(
                        refs[number], target.at[pl.ds(start, rows), :], sems.at[number]
                    )
                )

            if valid is None:
                run()
            else:
                pl.when(valid)(run)


def start_copies(*args):
    each_copy(*args, lambda copy: copy.start())


def wait_copies(*args):
    each_copy(*args, lambda copy: copy.wait())


def head_parts(proj_ref, head):
    def part(index):
        start = (index * HEADS + head) * HEAD_DIM
        return proj_ref[:, start : start + HEAD_DIM]

    query, key, value = part(0), part(1), part(2)
    query_scale = lax.rsqrt(mean_last(query * query) + EPS)
    key_scale = lax.rsqrt(mean_last(key * key) + EPS)
    return query * query_scale, query_scale, key * key_scale, key_scale, value.astype(BF16)


def attn_probs_of(query_bf, key_bf, allowed):
    scores = dot(query_bf, key_bf, NT) * SCORE_SCALE
    expo = jnp.where(allowed, jnp.exp(scores), 0.0)
    return expo / jnp.sum(expo, axis=-1, keepdims=True)


def attend_rows(proj_ref, mask, heads_ref):
    allowed = mask > 0.5
    for head in range(HEADS):
        query_hat, _, key_hat, _, value_bf = head_parts(proj_ref, head)
        probs = attn_probs_of(query_hat.astype(BF16), key_hat.astype(BF16), allowed)
        out = dot(probs.astype(BF16), value_bf)
        heads_ref[:, head * HEAD_DIM : (head + 1) * HEAD_DIM] = out.astype(BF16)


def finish_rows(x, heads, out_w, gain_e, hidden_ref, expert_ref):
    hidden = x.astype(F32) + dot(heads, out_w)
    hidden_ref[...] = hidden
    rms = lax.rsqrt(mean_last(hidden * hidden) + EPS)
    expert_ref[...] = (hidden * rms * gain_e).astype(BF16)


def project_kernel(count, depth, *refs):
    place, xf_ref, xb_ref, gain_a, gain_e, mask_ref = refs[:6]
    mix_refs = refs[6 : 6 + count]
    out_refs = refs[6 + count : 6 + 2 * count]
    projf_ref, projb_ref, hidden_ref, expert_ref = refs[6 + 2 * count : 10 + 2 * count]
    mix_w, out_w, normed, heads, mix_sems, out_sems = refs[10 + 2 * count :]
    chip, core = place[0], place[1]
    start_copies(mix_refs, mix_w, mix_sems, depth, chip, core)
    start_copies(out_refs, out_w, out_sems, depth, chip, core)
    rows = xf_ref.shape[0]
    for index, x_ref in enumerate((xf_ref, xb_ref)):
        x = x_ref[...].astype(F32)
        rms = lax.rsqrt(mean_last(x * x) + EPS)
        normed[index * rows : (index + 1) * rows, :] = (x * rms * gain_a[...]).astype(BF16)
    wait_copies(mix_refs, mix_w, mix_sems, depth, chip, core)
    columns = mix_w.shape[1]
    chunk = 512
    for begin in range(0, columns, chunk):
        piece = dot(normed[...], mix_w[:, begin : begin + chunk])
        projf_ref[:, begin : begin + chunk] = piece[:rows]
        projb_ref[:, begin : begin + chunk] = piece[rows:]
    attend_rows(projb_ref, mask_ref[1], heads)
    wait_copies(out_refs, out_w, out_sems, depth, chip, core)
    finish_rows(xb_ref[...], heads[...], out_w[...], gain_e[...], hidden_ref, expert_ref)


def forward_kernel(count, depth, *refs):
    place, x_ref, proj_ref, gain_e, mask_ref = refs[:5]
    out_refs = refs[5 : 5 + count]
    hidden_ref, expert_ref = refs[5 + count : 7 + count]
    out_w, heads, out_sems = refs[7 + count :]
    chip, core = place[0], place[1]
    start_copies(out_refs, out_w, out_sems, depth, chip, core)
    attend_rows(proj_ref, mask_ref[0], heads)
    wait_copies(out_refs, out_w, out_sems, depth, chip, core)
    finish_rows(x_ref[...], heads[...], out_w[...], gain_e[...], hidden_ref, expert_ref)


def picked_gate(gates, me, expert_count, micro):
    lane = lax.broadcasted_iota(jnp.int32, gates.shape, 1)
    first = 2 * micro * expert_count + me
    hit = (lane == first) | (lane == first + expert_count)
    return jnp.sum(jnp.where(hit, gates, 0.0), axis=-1, keepdims=True)


def cotangent_kernel(count, rows, width, expert_count, *refs):
    place, down_ref = refs[:2]
    cot_refs = refs[2 : 2 + count]
    act_ref, gate_ref = refs[2 + count : 4 + count]
    cot, sems = refs[4 + count :]
    chip, core = place[0], place[1]
    me = CORES * chip + core
    start_copies(cot_refs, cot, sems, rows, chip, core)
    wait_copies(cot_refs, cot, sems, rows, chip, core)
    chunk = 2 * rows

    def step(index, carry):
        start = pl.multiple_of(index * chunk, chunk)
        block = cot[pl.ds(start, chunk), :]
        gates = block[:, width:].astype(F32)
        grad_act = dot(block[:, :width], down_ref[...], NT)
        act_ref[pl.ds(start, chunk), :] = grad_act * picked_gate(gates, me, expert_count, 1)
        gate_ref[pl.ds(start, chunk), :] = jnp.broadcast_to(
            picked_gate(gates, me, expert_count, 0), (chunk, LANES)
        )
        return carry

    lax.fori_loop(0, expert_count * rows // chunk, step, 0)


def give_back(result, mine_ref, other_ref, rows, chip, core):
    length = mine_ref.shape[0]
    for j in range(length):
        origin = lax.rem(chip + j, length)
        for out_ref, side in ((mine_ref, core), (other_ref, 1 - core)):
            start = pl.multiple_of((CORES * origin + side) * rows, rows)
            out_ref[j] = result[pl.ds(start, rows), :]


def expert_backward_kernel(count, rows, *refs):
    place, up_ref, act_ref = refs[:3]
    row_refs = refs[3 : 3 + count]
    mine_ref, other_ref = refs[3 + count : 5 + count]
    tokens, result, sems = refs[5 + count :]
    chip, core = place[0], place[1]
    start_copies(row_refs, tokens, sems, rows, chip, core)
    wait_copies(row_refs, tokens, sems, rows, chip, core)
    chunk = 2 * rows

    def step(index, carry):
        start = pl.multiple_of(index * chunk, chunk)
        pre = dot(tokens[pl.ds(start, chunk), :], up_ref[...])
        square = pre * pre
        bend = jnp.tanh(GELU_C * pre * (1.0 + GELU_A * square))
        slope = 0.5 * (1.0 + bend) + 0.5 * pre * (1.0 - bend * bend) * (
            GELU_C * (1.0 + 3.0 * GELU_A * square)
        )
        grad = (act_ref[pl.ds(start, chunk), :] * slope).astype(BF16)
        result[pl.ds(start, chunk), :] = dot(grad, up_ref[...], NT).astype(BF16)
        return carry

    lax.fori_loop(0, tokens.shape[0] // chunk, step, 0)
    give_back(result, mine_ref, other_ref, rows, chip, core)


def expert_forward_kernel(count, rows, *refs):
    place, up_ref, down_ref, gate_ref = refs[:4]
    row_refs = refs[4 : 4 + count]
    mine_ref, other_ref = refs[4 + count : 6 + count]
    tokens, result, sems = refs[6 + count :]
    chip, core = place[0], place[1]
    start_copies(row_refs, tokens, sems, rows, chip, core)
    wait_copies(row_refs, tokens, sems, rows, chip, core)
    chunk = 2 * rows

    def step(index, carry):
        start = pl.multiple_of(index * chunk, chunk)
        pre = dot(tokens[pl.ds(start, chunk), :], up_ref[...])
        bend = jnp.tanh(GELU_C * pre * (1.0 + GELU_A * (pre * pre)))
        active = (0.5 * pre * (1.0 + bend)).astype(BF16)
        out = dot(active, down_ref[...])
        gate = gate_ref[pl.ds(start, chunk), :][:, :1]
        result[pl.ds(start, chunk), :] = (gate * out).astype(BF16)
        return carry

    lax.fori_loop(0, tokens.shape[0] // chunk, step, 0)
    give_back(result, mine_ref, other_ref, rows, chip, core)


def add_kernel(mine_ref, other_ref, *out_refs):
    for j, out_ref in enumerate(out_refs):
        out_ref[...] = (mine_ref[j].astype(F32) + other_ref[j].astype(F32)).astype(BF16)


def backward_kernel(count, parts, depth, *refs):
    place, x_ref, cot_ref, hidden_ref, proj_ref, gain_a, gain_e, mask_ref = refs[:8]
    part_refs = refs[8 : 8 + parts]
    mix_refs = refs[8 + parts : 8 + parts + count]
    out_refs = refs[8 + parts + count : 8 + parts + 2 * count]
    result_ref = refs[8 + parts + 2 * count]
    mix_w, out_w, mixed, mix_sems, out_sems = refs[9 + parts + 2 * count :]
    chip, core = place[0], place[1]
    start_copies(out_refs, out_w, out_sems, depth, chip, core)
    start_copies(mix_refs, mix_w, mix_sems, depth, chip, core)
    grad_moe = part_refs[0][...].astype(F32)
    for part_ref in part_refs[1:]:
        grad_moe = grad_moe + part_ref[...].astype(F32)
    hidden = hidden_ref[...]
    rms_two = lax.rsqrt(mean_last(hidden * hidden) + EPS)
    normal_two = hidden * rms_two
    grad_two = grad_moe * gain_e[...]
    grad_hidden = cot_ref[...].astype(F32) + rms_two * (
        grad_two - normal_two * mean_last(grad_two * normal_two)
    )
    wait_copies(out_refs, out_w, out_sems, depth, chip, core)
    grad_heads = dot(grad_hidden.astype(BF16), out_w[...], NT).astype(BF16)
    allowed = mask_ref[1] > 0.5
    for head in range(HEADS):
        query_hat, query_scale, key_hat, key_scale, value_bf = head_parts(proj_ref, head)
        query_bf, key_bf = query_hat.astype(BF16), key_hat.astype(BF16)
        probs = attn_probs_of(query_bf, key_bf, allowed)
        grad_out = grad_heads[:, head * HEAD_DIM : (head + 1) * HEAD_DIM]
        grad_probs = dot(grad_out, value_bf, NT)
        grad_value = dot(probs.astype(BF16), grad_out, TN)
        inner = jnp.sum(probs * grad_probs, axis=-1, keepdims=True)
        grad_scores = (probs * (grad_probs - inner) * SCORE_SCALE).astype(BF16)
        grad_qhat = dot(grad_scores, key_bf)
        grad_khat = dot(grad_scores, query_bf, TN)
        grad_query = query_scale * (grad_qhat - query_hat * mean_last(grad_qhat * query_hat))
        grad_key = key_scale * (grad_khat - key_hat * mean_last(grad_khat * key_hat))
        for index, grad in enumerate((grad_query, grad_key, grad_value)):
            start = (index * HEADS + head) * HEAD_DIM
            mixed[:, start : start + HEAD_DIM] = grad.astype(BF16)
    wait_copies(mix_refs, mix_w, mix_sems, depth, chip, core)
    grad_normed = dot(mixed[...], mix_w[...], NT)
    x = x_ref[...].astype(F32)
    rms_one = lax.rsqrt(mean_last(x * x) + EPS)
    normal_one = x * rms_one
    grad_one = grad_normed * gain_a[...]
    result = grad_hidden + rms_one * (grad_one - normal_one * mean_last(grad_one * normal_one))
    result_ref[...] = result.astype(BF16)


def shaped(shape, kind):
    return jax.ShapeDtypeStruct(shape, kind)


def dma(count):
    return pltpu.SemaphoreType.DMA((count,))


def call(kernel, outs, specs, out_specs, scratch, args):
    return pl.pallas_call(
        kernel,
        out_shape=outs,
        in_specs=specs,
        out_specs=out_specs,
        scratch_shapes=scratch,
        compiler_params=PARAMS,
    )(*args)


def dense_gates(routes, logits, expert_count):
    gates = jax.nn.sigmoid(logits)
    hit = routes[..., None] == jnp.arange(expert_count, dtype=jnp.int32)
    return jnp.sum(jnp.where(hit, gates[..., None], 0.0), axis=2)


def gate_columns(routes, logits, expert_count):
    gates = dense_gates(routes, logits, expert_count)
    high = lax.reduce_precision(gates, 8, 7)
    both = jnp.stack([high, gates - high], axis=1).astype(BF16)
    rows = jnp.transpose(both, (2, 0, 1, 3)).reshape(both.shape[2], -1)
    return jnp.pad(rows, ((0, 0), (0, LANES - rows.shape[1])))


def allowed_of(mask_blocks):
    frame_block = jnp.arange(FRAMES, dtype=jnp.int32) // BLOCK
    spread = (frame_block[:, None] == jnp.arange(FRAMES // BLOCK)[None, :]).astype(F32)
    eye = jnp.eye(FRAMES // BLOCK, dtype=F32)
    open_blocks = jnp.maximum((mask_blocks == 1).astype(F32), eye)
    return jnp.einsum("ib,mbc,jc->mij", spread, open_blocks, spread)


def local(
    handoff_forward,
    stashed_input,
    relay_cotangents,
    attention_gain,
    expert_gain,
    w_qkv,
    w_out,
    w_up,
    w_down,
    routes,
    gate_logits,
    block_mask,
):
    length = line_length()
    expert_count = lax.axis_size("expert")
    me = lax.axis_index("expert")
    place = jnp.stack([me // CORES, me % CORES]).astype(jnp.int32)
    tokens, width = handoff_forward.shape
    depth = w_qkv.shape[1]
    total = expert_count * tokens
    columns = w_qkv.shape[2]
    up_weight = w_up[0, 0]
    down_weight = w_down[0, 0]
    hidden_units = up_weight.shape[1]
    count = CORES * (2 * length - 1)

    mixers = with_partner(relayed(w_qkv[0]))
    outers = with_partner(relayed(w_out[0]))
    arriving = passed_along(handoff_forward, "section", 1)
    cotangent = passed_along(relay_cotangents, "section", -1)
    gates = gate_columns(routes, gate_logits, expert_count)
    cots = with_partner(relayed(jnp.concatenate([cotangent, gates], axis=1)))
    mask = allowed_of(block_mask[:, 0])

    proj_fwd, proj_bwd, hidden_bwd, expert_bwd = call(
        functools.partial(project_kernel, count, depth),
        (
            shaped((tokens, columns), F32),
            shaped((tokens, columns), F32),
            shaped((tokens, width), F32),
            shaped((tokens, width), BF16),
        ),
        [SMEM] + [VMEM] * 5 + [ANY] * (2 * count),
        (VMEM,) * 4,
        [
            pltpu.VMEM((width, columns), BF16),
            pltpu.VMEM((width, width), BF16),
            pltpu.VMEM((2 * tokens, width), BF16),
            pltpu.VMEM((tokens, width), BF16),
            dma(count),
            dma(count),
        ],
        [place, arriving, stashed_input, attention_gain, expert_gain, mask] + mixers + outers,
    )
    rows_bwd = with_partner(relayed(expert_bwd))

    hidden_fwd, expert_fwd = call(
        functools.partial(forward_kernel, count, depth),
        (shaped((tokens, width), F32), shaped((tokens, width), BF16)),
        [SMEM] + [VMEM] * 4 + [ANY] * count,
        (VMEM,) * 2,
        [pltpu.VMEM((width, width), BF16), pltpu.VMEM((tokens, width), BF16), dma(count)],
        [place, arriving, proj_fwd, expert_gain, mask] + outers,
    )
    rows_fwd = with_partner(relayed(expert_fwd))

    grad_act, gate_fwd = call(
        functools.partial(cotangent_kernel, count, tokens, width, expert_count),
        (shaped((total, hidden_units), F32), shaped((total, LANES), F32)),
        [SMEM, VMEM] + [ANY] * count,
        (VMEM,) * 2,
        [pltpu.VMEM((total, width + LANES), BF16), dma(count)],
        [place, down_weight] + cots,
    )

    pair = (shaped((length, tokens, width), BF16),) * 2

    def expert_scratch():
        return [pltpu.VMEM((total, width), BF16), pltpu.VMEM((total, width), BF16), dma(count)]

    def combined(mine, other):
        blocks = call(
            add_kernel,
            (shaped((tokens, width), BF16),) * length,
            [VMEM] * 2,
            (VMEM,) * length,
            [],
            [mine, swapped(other)],
        )
        return scattered(blocks)

    mine, other = call(
        functools.partial(expert_backward_kernel, count, tokens),
        pair,
        [SMEM, VMEM, VMEM] + [ANY] * count,
        (VMEM,) * 2,
        expert_scratch(),
        [place, up_weight, grad_act] + rows_bwd,
    )
    grad_parts = combined(mine, other)

    mine, other = call(
        functools.partial(expert_forward_kernel, count, tokens),
        pair,
        [SMEM, VMEM, VMEM, VMEM] + [ANY] * count,
        (VMEM,) * 2,
        expert_scratch(),
        [place, up_weight, down_weight, gate_fwd] + rows_fwd,
    )
    moe_parts = combined(mine, other)

    parts = len(grad_parts)
    derivative = call(
        functools.partial(backward_kernel, count, parts, depth),
        shaped((tokens, width), BF16),
        [SMEM] + [VMEM] * (7 + parts) + [ANY] * (2 * count),
        VMEM,
        [
            pltpu.VMEM((width, columns), BF16),
            pltpu.VMEM((width, width), BF16),
            pltpu.VMEM((tokens, columns), BF16),
            dma(count),
            dma(count),
        ],
        [place, stashed_input, cotangent, hidden_bwd, proj_bwd, attention_gain, expert_gain, mask]
        + grad_parts
        + mixers
        + outers,
    )

    layer_output = hidden_fwd
    for part in moe_parts:
        layer_output = layer_output + part.astype(F32)
    return (layer_output.astype(BF16), derivative)


def solution(mesh):
    placed = (
        P(("section", "expert"), None),
        P(("section", "expert"), None),
        P(("section", "expert"), None),
        P("section", None),
        P("section", None),
        P("section", "expert", None),
        P("section", "expert", None),
        P("section", "expert", None, None),
        P("section", "expert", None, None),
        P(None, ("section", "expert"), None),
        P(None, ("section", "expert"), None),
        P(None, ("section", "expert"), None, None),
    )

    return jax.shard_map(
        local,
        mesh=mesh,
        in_specs=placed,
        out_specs=(P(("section", "expert"), None), P(("section", "expert"), None)),
        check_vma=False,
    )
```

```python
import functools

import jax
import jax.numpy as jnp
from jax import lax
from jax.experimental import pallas as pl
from jax.experimental.pallas import tpu as pltpu
from jax.sharding import PartitionSpec as P


HEADS = 8
HEAD_DIM = 128
FRAMES = 128
BLOCK = 16
CORES = 2
LANES = 128

EPS = 1e-06
SCORE_SCALE = HEAD_DIM ** (-0.5)
GELU_C = 0.7978845608028654
GELU_A = 0.044715


F32 = jnp.float32
BF16 = jnp.bfloat16
NT = (((1,), (1,)), ((), ()))
TN = (((0,), (0,)), ((), ()))
ANY = pl.BlockSpec(memory_space=pl.ANY)
SMEM = pl.BlockSpec(memory_space=pltpu.SMEM)
VMEM = pl.BlockSpec(memory_space=pltpu.VMEM)
PARAMS = pltpu.CompilerParams(vmem_limit_bytes=56 * 1024 * 1024)


def dot(a, b, dims=(((1,), (0,)), ((), ()))):
    return lax.dot_general(a, b, dims, preferred_element_type=F32)


def mean_last(values):
    return jnp.mean(values, axis=-1, keepdims=True)


def passed_along(value, axis, steps):
    count = lax.axis_size(axis)
    pairs = [(source, (source + steps) % count) for source in range(count)]
    return lax.ppermute(value, axis, pairs)


def line_length():
    return lax.axis_size("expert") // CORES


def chip_pairs(sources, step):
    return [
        (CORES * chip + core, CORES * (chip + step) + core)
        for chip in sources
        for core in range(CORES)
    ]


def swapped(value):
    count = lax.axis_size("expert")
    return lax.ppermute(value, "expert", [(i, i ^ 1) for i in range(count)])


def hop(value, sources, move):
    return lax.ppermute(value, "expert", chip_pairs(sources, move))


def relayed(value):
    length = line_length()
    entries = [value]
    up = down = value
    for step in range(1, length):
        up = hop(up, range(step - 1, length - 1), 1)
        down = hop(down, range(1, length - step + 1), -1)
        entries += [up, down]
    return entries


def with_partner(entries):
    return entries + [swapped(block) for block in entries]


def scattered(blocks):
    length = line_length()
    up = down = None
    for step in range(1, length):
        far = length - step
        send_up, send_down = blocks[far], blocks[length - far]
        if up is not None:
            send_up = send_up + up
            send_down = send_down + down
        up = hop(send_up, range(0, step), 1)
        down = hop(send_down, range(length - step, length), -1)
    return [blocks[0], up, down]


def entry_chips(hops, chip):
    length = line_length()
    listing = [(None, chip)]
    for hop in range(1, hops + 1):
        listing.append((chip - hop >= 0, chip - hop))
        listing.append((chip + hop < length, chip + hop))
    return listing


def each_copy(refs, target, sems, rows, chip, core, act):
    count = len(refs) // 2
    listing = entry_chips(count // 2, chip)
    for side in range(CORES):
        for index, (valid, origin) in enumerate(listing):
            number = side * count + index
            owner = CORES * origin + (core if side == 0 else 1 - core)

            def run(number=number, owner=owner):
                start = pl.multiple_of(owner * rows, rows)
                act(
                    pltpu.make_async_copy(
                        refs[number], target.at[pl.ds(start, rows), :], sems.at[number]
                    )
                )

            if valid is None:
                run()
            else:
                pl.when(valid)(run)


def start_copies(*args):
    each_copy(*args, lambda copy: copy.start())


def wait_copies(*args):
    each_copy(*args, lambda copy: copy.wait())


def head_parts(proj_ref, head):
    def part(index):
        start = (index * HEADS + head) * HEAD_DIM
        return proj_ref[:, start : start + HEAD_DIM]

    query, key, value = part(0), part(1), part(2)
    query_scale = lax.rsqrt(mean_last(query * query) + EPS)
    key_scale = lax.rsqrt(mean_last(key * key) + EPS)
    return query * query_scale, query_scale, key * key_scale, key_scale, value.astype(BF16)


def attn_probs_of(query_bf, key_bf, allowed):
    scores = dot(query_bf, key_bf, NT) * SCORE_SCALE
    expo = jnp.where(allowed, jnp.exp(scores), 0.0)
    return expo / jnp.sum(expo, axis=-1, keepdims=True)


def attend_rows(proj_ref, mask, heads_ref):
    allowed = mask > 0.5
    for head in range(HEADS):
        query_hat, _, key_hat, _, value_bf = head_parts(proj_ref, head)
        probs = attn_probs_of(query_hat.astype(BF16), key_hat.astype(BF16), allowed)
        out = dot(probs.astype(BF16), value_bf)
        heads_ref[:, head * HEAD_DIM : (head + 1) * HEAD_DIM] = out.astype(BF16)


def finish_rows(x, heads, out_w, gain_e, hidden_ref, expert_ref):
    hidden = x.astype(F32) + dot(heads, out_w)
    hidden_ref[...] = hidden
    rms = lax.rsqrt(mean_last(hidden * hidden) + EPS)
    expert_ref[...] = (hidden * rms * gain_e).astype(BF16)


def early_kernel(count, depth, *refs):
    place, xf_ref, xb_ref, gain_a = refs[:4]
    mix_refs = refs[4 : 4 + count]
    sumf_ref, sumb_ref, normed_ref = refs[4 + count : 7 + count]
    mix_w, mix_sems = refs[7 + count :]
    chip, core = place[0], place[1]
    mix_w[...] = jnp.zeros_like(mix_w)
    start_copies(mix_refs, mix_w, mix_sems, depth, chip, core)
    rows = xf_ref.shape[0]
    for index, x_ref in enumerate((xf_ref, xb_ref)):
        x = x_ref[...].astype(F32)
        rms = lax.rsqrt(mean_last(x * x) + EPS)
        normed_ref[index * rows : (index + 1) * rows, :] = (x * rms * gain_a[...]).astype(BF16)
    wait_copies(mix_refs, mix_w, mix_sems, depth, chip, core)
    columns = mix_w.shape[1]
    chunk = 512
    for begin in range(0, columns, chunk):
        piece = dot(normed_ref[...], mix_w[:, begin : begin + chunk])
        sumf_ref[:, begin : begin + chunk] = piece[:rows]
        sumb_ref[:, begin : begin + chunk] = piece[rows:]


def last_copies(mix_refs, mix_w, sems, depth, length, chip, core, act):
    for which, end in ((0, length - 1), (1, 0)):

        @pl.when(chip == end)
        def _():
            for side in range(CORES):
                start = pl.multiple_of((core if side == 0 else 1 - core) * depth, depth)
                act(
                    pltpu.make_async_copy(
                        mix_refs[2 * side + which],
                        mix_w.at[pl.ds(start, depth), :],
                        sems.at[2 * side + which],
                    )
                )


def project_kernel(count, depth, length, *refs):
    place, sumf_ref, sumb_ref, normed_ref, xb_ref, gain_e, mask_ref = refs[:7]
    mix_refs = refs[7:11]
    out_refs = refs[11 : 11 + count]
    projf_ref, projb_ref, hidden_ref, expert_ref = refs[11 + count : 15 + count]
    mix_w, out_w, heads, mix_sems, out_sems = refs[15 + count :]
    chip, core = place[0], place[1]
    last_copies(mix_refs, mix_w, mix_sems, depth, length, chip, core, lambda copy: copy.start())
    start_copies(out_refs, out_w, out_sems, depth, chip, core)
    last_copies(mix_refs, mix_w, mix_sems, depth, length, chip, core, lambda copy: copy.wait())
    rows = xb_ref.shape[0]
    columns = mix_w.shape[1]
    chunk = 512
    block = CORES * depth
    for end in (0, length - 1):

        @pl.when(chip == end)
        def _():
            far = (length - 1 - end) * block
            for begin in range(0, columns, chunk):
                span = slice(begin, begin + chunk)
                piece = dot(normed_ref[:, far : far + block], mix_w[:, span])
                projf_ref[:, span] = sumf_ref[:, span] + piece[:rows]
                projb_ref[:, span] = sumb_ref[:, span] + piece[rows:]

    @pl.when((chip > 0) & (chip < length - 1))
    def _():
        projf_ref[...] = sumf_ref[...]
        projb_ref[...] = sumb_ref[...]

    attend_rows(projb_ref, mask_ref[1], heads)
    wait_copies(out_refs, out_w, out_sems, depth, chip, core)
    finish_rows(xb_ref[...], heads[...], out_w[...], gain_e[...], hidden_ref, expert_ref)


def forward_kernel(count, depth, *refs):
    place, x_ref, proj_ref, gain_e, mask_ref = refs[:5]
    out_refs = refs[5 : 5 + count]
    hidden_ref, expert_ref = refs[5 + count : 7 + count]
    out_w, heads, out_sems = refs[7 + count :]
    chip, core = place[0], place[1]
    start_copies(out_refs, out_w, out_sems, depth, chip, core)
    attend_rows(proj_ref, mask_ref[0], heads)
    wait_copies(out_refs, out_w, out_sems, depth, chip, core)
    finish_rows(x_ref[...], heads[...], out_w[...], gain_e[...], hidden_ref, expert_ref)


def picked_gate(gates, me, expert_count, micro):
    lane = lax.broadcasted_iota(jnp.int32, gates.shape, 1)
    first = 2 * micro * expert_count + me
    hit = (lane == first) | (lane == first + expert_count)
    return jnp.sum(jnp.where(hit, gates, 0.0), axis=-1, keepdims=True)


def cotangent_kernel(count, rows, width, expert_count, *refs):
    place, down_ref = refs[:2]
    cot_refs = refs[2 : 2 + count]
    act_ref, gate_ref = refs[2 + count : 4 + count]
    cot, sems = refs[4 + count :]
    chip, core = place[0], place[1]
    me = CORES * chip + core
    start_copies(cot_refs, cot, sems, rows, chip, core)
    wait_copies(cot_refs, cot, sems, rows, chip, core)
    chunk = 2 * rows

    def step(index, carry):
        start = chunk_start(index, chunk)
        block = cot[pl.ds(start, chunk), :]
        gates = block[:, width:].astype(F32)
        grad_act = dot(block[:, :width], down_ref[...], NT)
        act_ref[pl.ds(start, chunk), :] = grad_act * picked_gate(gates, me, expert_count, 1)
        gate_ref[pl.ds(start, chunk), :] = jnp.broadcast_to(
            picked_gate(gates, me, expert_count, 0), (chunk, LANES)
        )
        return carry

    each_chunk(expert_count * rows // chunk, step)


def each_chunk(number, step):
    if number <= 4:
        for index in range(number):
            step(index, 0)
    else:
        lax.fori_loop(0, number, step, 0)


def chunk_start(index, chunk):
    return index * chunk if isinstance(index, int) else pl.multiple_of(index * chunk, chunk)


def give_back(result, mine_ref, other_ref, rows, chip, core):
    length = mine_ref.shape[0]
    for j in range(length):
        origin = lax.rem(chip + j, length)
        for out_ref, side in ((mine_ref, core), (other_ref, 1 - core)):
            start = pl.multiple_of((CORES * origin + side) * rows, rows)
            out_ref[j] = result[pl.ds(start, rows), :]


def expert_backward_kernel(count, rows, *refs):
    place, up_ref, act_ref = refs[:3]
    row_refs = refs[3 : 3 + count]
    mine_ref, other_ref = refs[3 + count : 5 + count]
    tokens, result, sems = refs[5 + count :]
    chip, core = place[0], place[1]
    start_copies(row_refs, tokens, sems, rows, chip, core)
    wait_copies(row_refs, tokens, sems, rows, chip, core)
    chunk = 2 * rows

    def step(index, carry):
        start = chunk_start(index, chunk)
        pre = dot(tokens[pl.ds(start, chunk), :], up_ref[...])
        square = pre * pre
        bend = jnp.tanh(GELU_C * pre * (1.0 + GELU_A * square))
        slope = 0.5 * (1.0 + bend) + 0.5 * pre * (1.0 - bend * bend) * (
            GELU_C * (1.0 + 3.0 * GELU_A * square)
        )
        grad = (act_ref[pl.ds(start, chunk), :] * slope).astype(BF16)
        result[pl.ds(start, chunk), :] = dot(grad, up_ref[...], NT).astype(BF16)
        return carry

    each_chunk(tokens.shape[0] // chunk, step)
    give_back(result, mine_ref, other_ref, rows, chip, core)


def expert_forward_kernel(count, rows, *refs):
    place, up_ref, down_ref, gate_ref = refs[:4]
    row_refs = refs[4 : 4 + count]
    mine_ref, other_ref = refs[4 + count : 6 + count]
    tokens, result, sems = refs[6 + count :]
    chip, core = place[0], place[1]
    start_copies(row_refs, tokens, sems, rows, chip, core)
    wait_copies(row_refs, tokens, sems, rows, chip, core)
    chunk = 2 * rows

    def step(index, carry):
        start = chunk_start(index, chunk)
        pre = dot(tokens[pl.ds(start, chunk), :], up_ref[...])
        bend = jnp.tanh(GELU_C * pre * (1.0 + GELU_A * (pre * pre)))
        active = (0.5 * pre * (1.0 + bend)).astype(BF16)
        out = dot(active, down_ref[...])
        gate = gate_ref[pl.ds(start, chunk), :][:, :1]
        result[pl.ds(start, chunk), :] = (gate * out).astype(BF16)
        return carry

    each_chunk(tokens.shape[0] // chunk, step)
    give_back(result, mine_ref, other_ref, rows, chip, core)


def add_kernel(mine_ref, other_ref, *out_refs):
    for j, out_ref in enumerate(out_refs):
        out_ref[...] = (mine_ref[j].astype(F32) + other_ref[j].astype(F32)).astype(BF16)


def heads_backward_kernel(count, parts, depth, *refs):
    place, cot_ref, hidden_ref, proj_ref, gain_e, mask_ref = refs[:6]
    part_refs = refs[6 : 6 + parts]
    out_refs = refs[6 + parts : 6 + parts + count]
    mixed_ref, grad_ref = refs[6 + parts + count : 8 + parts + count]
    out_w, out_sems = refs[8 + parts + count :]
    chip, core = place[0], place[1]
    start_copies(out_refs, out_w, out_sems, depth, chip, core)
    grad_moe = part_refs[0][...].astype(F32)
    for part_ref in part_refs[1:]:
        grad_moe = grad_moe + part_ref[...].astype(F32)
    hidden = hidden_ref[...]
    rms_two = lax.rsqrt(mean_last(hidden * hidden) + EPS)
    normal_two = hidden * rms_two
    grad_two = grad_moe * gain_e[...]
    grad_hidden = cot_ref[...].astype(F32) + rms_two * (
        grad_two - normal_two * mean_last(grad_two * normal_two)
    )
    grad_ref[...] = grad_hidden
    wait_copies(out_refs, out_w, out_sems, depth, chip, core)
    grad_heads = dot(grad_hidden.astype(BF16), out_w[...], NT).astype(BF16)
    allowed = mask_ref[1] > 0.5
    for head in range(HEADS):
        query_hat, query_scale, key_hat, key_scale, value_bf = head_parts(proj_ref, head)
        query_bf, key_bf = query_hat.astype(BF16), key_hat.astype(BF16)
        probs = attn_probs_of(query_bf, key_bf, allowed)
        grad_out = grad_heads[:, head * HEAD_DIM : (head + 1) * HEAD_DIM]
        grad_probs = dot(grad_out, value_bf, NT)
        grad_value = dot(probs.astype(BF16), grad_out, TN)
        inner = jnp.sum(probs * grad_probs, axis=-1, keepdims=True)
        grad_scores = (probs * (grad_probs - inner) * SCORE_SCALE).astype(BF16)
        grad_qhat = dot(grad_scores, key_bf)
        grad_khat = dot(grad_scores, query_bf, TN)
        grad_query = query_scale * (grad_qhat - query_hat * mean_last(grad_qhat * query_hat))
        grad_key = key_scale * (grad_khat - key_hat * mean_last(grad_khat * key_hat))
        for index, grad in enumerate((grad_query, grad_key, grad_value)):
            start = (index * HEADS + head) * HEAD_DIM
            mixed_ref[:, start : start + HEAD_DIM] = grad.astype(BF16)


def entry_backward_kernel(count, depth, *refs):
    place, x_ref, mixed_ref, grad_ref, gain_a = refs[:5]
    mix_refs = refs[5 : 5 + count]
    result_ref = refs[5 + count]
    mix_w, mix_sems = refs[6 + count :]
    chip, core = place[0], place[1]
    start_copies(mix_refs, mix_w, mix_sems, depth, chip, core)
    wait_copies(mix_refs, mix_w, mix_sems, depth, chip, core)
    grad_normed = dot(mixed_ref[...], mix_w[...], NT)
    x = x_ref[...].astype(F32)
    rms_one = lax.rsqrt(mean_last(x * x) + EPS)
    normal_one = x * rms_one
    grad_one = grad_normed * gain_a[...]
    result = grad_ref[...] + rms_one * (grad_one - normal_one * mean_last(grad_one * normal_one))
    result_ref[...] = result.astype(BF16)


def shaped(shape, kind):
    return jax.ShapeDtypeStruct(shape, kind)


def dma(count):
    return pltpu.SemaphoreType.DMA((count,))


def call(kernel, outs, specs, out_specs, scratch, args):
    return pl.pallas_call(
        kernel,
        out_shape=outs,
        in_specs=specs,
        out_specs=out_specs,
        scratch_shapes=scratch,
        compiler_params=PARAMS,
    )(*args)


def dense_gates(routes, logits, expert_count):
    gates = jax.nn.sigmoid(logits)
    hit = routes[..., None] == jnp.arange(expert_count, dtype=jnp.int32)
    return jnp.sum(jnp.where(hit, gates[..., None], 0.0), axis=2)


def gate_columns(routes, logits, expert_count):
    gates = dense_gates(routes, logits, expert_count)
    high = lax.reduce_precision(gates, 8, 7)
    both = jnp.stack([high, gates - high], axis=1).astype(BF16)
    rows = jnp.transpose(both, (2, 0, 1, 3)).reshape(both.shape[2], -1)
    return jnp.pad(rows, ((0, 0), (0, LANES - rows.shape[1])))


def allowed_of(mask_blocks):
    frame_block = jnp.arange(FRAMES, dtype=jnp.int32) // BLOCK
    spread = (frame_block[:, None] == jnp.arange(FRAMES // BLOCK)[None, :]).astype(F32)
    eye = jnp.eye(FRAMES // BLOCK, dtype=F32)
    open_blocks = jnp.maximum((mask_blocks == 1).astype(F32), eye)
    return jnp.einsum("ib,mbc,jc->mij", spread, open_blocks, spread)


def local(
    handoff_forward,
    stashed_input,
    relay_cotangents,
    attention_gain,
    expert_gain,
    w_qkv,
    w_out,
    w_up,
    w_down,
    routes,
    gate_logits,
    block_mask,
):
    length = line_length()
    expert_count = lax.axis_size("expert")
    me = lax.axis_index("expert")
    place = jnp.stack([me // CORES, me % CORES]).astype(jnp.int32)
    tokens, width = handoff_forward.shape
    depth = w_qkv.shape[1]
    total = expert_count * tokens
    columns = w_qkv.shape[2]
    up_weight = w_up[0, 0]
    down_weight = w_down[0, 0]
    hidden_units = up_weight.shape[1]
    count = CORES * (2 * length - 1)

    mixers = with_partner(relayed(w_qkv[0]))
    outers = with_partner(relayed(w_out[0]))
    arriving = passed_along(handoff_forward, "section", 1)
    cotangent = passed_along(relay_cotangents, "section", -1)
    gates = gate_columns(routes, gate_logits, expert_count)
    cots = with_partner(relayed(jnp.concatenate([cotangent, gates], axis=1)))
    mask = allowed_of(block_mask[:, 0])

    half = count // 2
    early_mix = mixers[: half - 2] + mixers[half : count - 2]
    last_mix = mixers[half - 2 : half] + mixers[count - 2 :]
    early = len(early_mix)
    sum_fwd, sum_bwd, normed = call(
        functools.partial(early_kernel, early, depth),
        (
            shaped((tokens, columns), F32),
            shaped((tokens, columns), F32),
            shaped((2 * tokens, width), BF16),
        ),
        [SMEM] + [VMEM] * 3 + [ANY] * early,
        (VMEM,) * 3,
        [pltpu.VMEM((width, columns), BF16), dma(early)],
        [place, arriving, stashed_input, attention_gain] + early_mix,
    )
    proj_fwd, proj_bwd, hidden_bwd, expert_bwd = call(
        functools.partial(project_kernel, count, depth, length),
        (
            shaped((tokens, columns), F32),
            shaped((tokens, columns), F32),
            shaped((tokens, width), F32),
            shaped((tokens, width), BF16),
        ),
        [SMEM] + [VMEM] * 6 + [ANY] * (4 + count),
        (VMEM,) * 4,
        [
            pltpu.VMEM((CORES * depth, columns), BF16),
            pltpu.VMEM((width, width), BF16),
            pltpu.VMEM((tokens, width), BF16),
            dma(4),
            dma(count),
        ],
        [place, sum_fwd, sum_bwd, normed, stashed_input, expert_gain, mask] + last_mix + outers,
    )
    rows_bwd = with_partner(relayed(expert_bwd))

    hidden_fwd, expert_fwd = call(
        functools.partial(forward_kernel, count, depth),
        (shaped((tokens, width), F32), shaped((tokens, width), BF16)),
        [SMEM] + [VMEM] * 4 + [ANY] * count,
        (VMEM,) * 2,
        [pltpu.VMEM((width, width), BF16), pltpu.VMEM((tokens, width), BF16), dma(count)],
        [place, arriving, proj_fwd, expert_gain, mask] + outers,
    )
    rows_fwd = with_partner(relayed(expert_fwd))

    grad_act, gate_fwd = call(
        functools.partial(cotangent_kernel, count, tokens, width, expert_count),
        (shaped((total, hidden_units), F32), shaped((total, LANES), F32)),
        [SMEM, VMEM] + [ANY] * count,
        (VMEM,) * 2,
        [pltpu.VMEM((total, width + LANES), BF16), dma(count)],
        [place, down_weight] + cots,
    )

    pair = (shaped((length, tokens, width), BF16),) * 2

    def expert_scratch():
        return [pltpu.VMEM((total, width), BF16), pltpu.VMEM((total, width), BF16), dma(count)]

    def combined(mine, other):
        blocks = call(
            add_kernel,
            (shaped((tokens, width), BF16),) * length,
            [VMEM] * 2,
            (VMEM,) * length,
            [],
            [mine, swapped(other)],
        )
        return scattered(blocks)

    mine, other = call(
        functools.partial(expert_backward_kernel, count, tokens),
        pair,
        [SMEM, VMEM, VMEM] + [ANY] * count,
        (VMEM,) * 2,
        expert_scratch(),
        [place, up_weight, grad_act] + rows_bwd,
    )
    grad_parts = combined(mine, other)

    mine, other = call(
        functools.partial(expert_forward_kernel, count, tokens),
        pair,
        [SMEM, VMEM, VMEM, VMEM] + [ANY] * count,
        (VMEM,) * 2,
        expert_scratch(),
        [place, up_weight, down_weight, gate_fwd] + rows_fwd,
    )
    moe_parts = combined(mine, other)

    parts = len(grad_parts)
    grad_mixed, grad_hidden = call(
        functools.partial(heads_backward_kernel, count, parts, depth),
        (shaped((tokens, columns), BF16), shaped((tokens, width), F32)),
        [SMEM] + [VMEM] * (5 + parts) + [ANY] * count,
        (VMEM,) * 2,
        [pltpu.VMEM((width, width), BF16), dma(count)],
        [place, cotangent, hidden_bwd, proj_bwd, expert_gain, mask] + grad_parts + outers,
    )
    derivative = call(
        functools.partial(entry_backward_kernel, count, depth),
        shaped((tokens, width), BF16),
        [SMEM] + [VMEM] * 4 + [ANY] * count,
        VMEM,
        [pltpu.VMEM((width, columns), BF16), dma(count)],
        [place, stashed_input, grad_mixed, grad_hidden, attention_gain] + mixers,
    )

    layer_output = hidden_fwd
    for part in moe_parts:
        layer_output = layer_output + part.astype(F32)
    return (layer_output.astype(BF16), derivative)


def solution(mesh):
    placed = (
        P(("section", "expert"), None),
        P(("section", "expert"), None),
        P(("section", "expert"), None),
        P("section", None),
        P("section", None),
        P("section", "expert", None),
        P("section", "expert", None),
        P("section", "expert", None, None),
        P("section", "expert", None, None),
        P(None, ("section", "expert"), None),
        P(None, ("section", "expert"), None),
        P(None, ("section", "expert"), None, None),
    )

    return jax.shard_map(
        local,
        mesh=mesh,
        in_specs=placed,
        out_specs=(P(("section", "expert"), None), P(("section", "expert"), None)),
        check_vma=False,
    )
```

```python
import functools

import jax
import jax.numpy as jnp
from jax import lax
from jax.experimental import pallas as pl
from jax.experimental.pallas import tpu as pltpu
from jax.sharding import PartitionSpec as P


HEADS = 8
HEAD_DIM = 128
FRAMES = 128
BLOCK = 16
CORES = 2
LANES = 128

EPS = 1e-06
SCORE_SCALE = HEAD_DIM ** (-0.5)
GELU_C = 0.7978845608028654
GELU_A = 0.044715


F32 = jnp.float32
BF16 = jnp.bfloat16
NT = (((1,), (1,)), ((), ()))
TN = (((0,), (0,)), ((), ()))
ANY = pl.BlockSpec(memory_space=pl.ANY)
SMEM = pl.BlockSpec(memory_space=pltpu.SMEM)
VMEM = pl.BlockSpec(memory_space=pltpu.VMEM)
PARAMS = pltpu.CompilerParams(vmem_limit_bytes=56 * 1024 * 1024)


def dot(a, b, dims=(((1,), (0,)), ((), ()))):
    return lax.dot_general(a, b, dims, preferred_element_type=F32)


def mean_last(values):
    return jnp.mean(values, axis=-1, keepdims=True)


def passed_along(value, axis, steps):
    count = lax.axis_size(axis)
    pairs = [(source, (source + steps) % count) for source in range(count)]
    return lax.ppermute(value, axis, pairs)


def line_length():
    return lax.axis_size("expert") // CORES


def chip_pairs(sources, step):
    return [
        (CORES * chip + core, CORES * (chip + step) + core)
        for chip in sources
        for core in range(CORES)
    ]


def swapped(value):
    count = lax.axis_size("expert")
    return lax.ppermute(value, "expert", [(i, i ^ 1) for i in range(count)])


def hop(value, sources, move):
    return lax.ppermute(value, "expert", chip_pairs(sources, move))


def relayed(value):
    length = line_length()
    entries = [value]
    up = down = value
    for step in range(1, length):
        up = hop(up, range(step - 1, length - 1), 1)
        down = hop(down, range(1, length - step + 1), -1)
        entries += [up, down]
    return entries


def with_partner(entries):
    return entries + [swapped(block) for block in entries]


def scattered(blocks):
    length = line_length()
    up = down = None
    for step in range(1, length):
        far = length - step
        send_up, send_down = blocks[far], blocks[length - far]
        if up is not None:
            send_up = send_up + up
            send_down = send_down + down
        up = hop(send_up, range(0, step), 1)
        down = hop(send_down, range(length - step, length), -1)
    return [blocks[0], up, down]


def across(blocks):
    length = line_length()
    groups = [[CORES * chip + core for chip in range(length)] for core in range(CORES)]
    return lax.all_to_all(
        blocks, "expert", split_axis=0, concat_axis=0, axis_index_groups=groups, tiled=True
    )


def spread(value):
    copies = jnp.broadcast_to(value[None], (line_length(),) + value.shape)
    mine = across(copies)
    return [mine, swapped(mine)]


def entry_chips(hops, chip):
    length = line_length()
    listing = [(None, chip)]
    for hop in range(1, hops + 1):
        listing.append((chip - hop >= 0, chip - hop))
        listing.append((chip + hop < length, chip + hop))
    return listing


def each_copy(refs, target, sems, rows, chip, core, act):
    count = len(refs) // 2
    listing = entry_chips(count // 2, chip)
    for side in range(CORES):
        for index, (valid, origin) in enumerate(listing):
            number = side * count + index
            owner = CORES * origin + (core if side == 0 else 1 - core)

            def run(number=number, owner=owner):
                start = pl.multiple_of(owner * rows, rows)
                act(
                    pltpu.make_async_copy(
                        refs[number], target.at[pl.ds(start, rows), :], sems.at[number]
                    )
                )

            if valid is None:
                run()
            else:
                pl.when(valid)(run)


def line_copies(refs, target, sems, rows, chip, core, act):
    for side, ref in enumerate(refs):
        for origin in range(ref.shape[0]):
            owner = CORES * origin + (core if side == 0 else 1 - core)
            start = pl.multiple_of(owner * rows, rows)
            act(
                pltpu.make_async_copy(
                    ref.at[origin], target.at[pl.ds(start, rows), :], sems.at[side, origin]
                )
            )


def fetch_line(*args):
    line_copies(*args, lambda copy: copy.start())
    line_copies(*args, lambda copy: copy.wait())


def start_copies(*args):
    each_copy(*args, lambda copy: copy.start())


def wait_copies(*args):
    each_copy(*args, lambda copy: copy.wait())


def head_parts(proj_ref, head):
    def part(index):
        start = (index * HEADS + head) * HEAD_DIM
        return proj_ref[:, start : start + HEAD_DIM]

    query, key, value = part(0), part(1), part(2)
    query_scale = lax.rsqrt(mean_last(query * query) + EPS)
    key_scale = lax.rsqrt(mean_last(key * key) + EPS)
    return query * query_scale, query_scale, key * key_scale, key_scale, value.astype(BF16)


def attn_probs_of(query_bf, key_bf, allowed):
    scores = dot(query_bf, key_bf, NT) * SCORE_SCALE
    expo = jnp.where(allowed, jnp.exp(scores), 0.0)
    return expo / jnp.sum(expo, axis=-1, keepdims=True)


def attend_rows(proj_ref, mask, heads_ref):
    allowed = mask > 0.5
    for head in range(HEADS):
        query_hat, _, key_hat, _, value_bf = head_parts(proj_ref, head)
        probs = attn_probs_of(query_hat.astype(BF16), key_hat.astype(BF16), allowed)
        out = dot(probs.astype(BF16), value_bf)
        heads_ref[:, head * HEAD_DIM : (head + 1) * HEAD_DIM] = out.astype(BF16)


def finish_rows(x, heads, out_w, gain_e, hidden_ref, expert_ref):
    hidden = x.astype(F32) + dot(heads, out_w)
    hidden_ref[...] = hidden
    rms = lax.rsqrt(mean_last(hidden * hidden) + EPS)
    expert_ref[...] = (hidden * rms * gain_e).astype(BF16)


def early_kernel(count, depth, *refs):
    place, xf_ref, xb_ref, gain_a = refs[:4]
    mix_refs = refs[4 : 4 + count]
    sumf_ref, sumb_ref, normed_ref = refs[4 + count : 7 + count]
    mix_w, mix_sems = refs[7 + count :]
    chip, core = place[0], place[1]
    mix_w[...] = jnp.zeros_like(mix_w)
    start_copies(mix_refs, mix_w, mix_sems, depth, chip, core)
    rows = xf_ref.shape[0]
    for index, x_ref in enumerate((xf_ref, xb_ref)):
        x = x_ref[...].astype(F32)
        rms = lax.rsqrt(mean_last(x * x) + EPS)
        normed_ref[index * rows : (index + 1) * rows, :] = (x * rms * gain_a[...]).astype(BF16)
    wait_copies(mix_refs, mix_w, mix_sems, depth, chip, core)
    columns = mix_w.shape[1]
    chunk = 512
    for begin in range(0, columns, chunk):
        piece = dot(normed_ref[...], mix_w[:, begin : begin + chunk])
        sumf_ref[:, begin : begin + chunk] = piece[:rows]
        sumb_ref[:, begin : begin + chunk] = piece[rows:]


def last_copies(mix_refs, mix_w, sems, depth, length, chip, core, act):
    for which, end in ((0, length - 1), (1, 0)):

        @pl.when(chip == end)
        def _():
            for side in range(CORES):
                start = pl.multiple_of((core if side == 0 else 1 - core) * depth, depth)
                act(
                    pltpu.make_async_copy(
                        mix_refs[2 * side + which],
                        mix_w.at[pl.ds(start, depth), :],
                        sems.at[2 * side + which],
                    )
                )


def project_kernel(count, depth, length, *refs):
    place, sumf_ref, sumb_ref, normed_ref, xb_ref, gain_e, mask_ref = refs[:7]
    mix_refs = refs[7:11]
    out_refs = refs[11 : 11 + count]
    projf_ref, projb_ref, hidden_ref, expert_ref = refs[11 + count : 15 + count]
    mix_w, out_w, heads, mix_sems, out_sems = refs[15 + count :]
    chip, core = place[0], place[1]
    last_copies(mix_refs, mix_w, mix_sems, depth, length, chip, core, lambda copy: copy.start())
    start_copies(out_refs, out_w, out_sems, depth, chip, core)
    last_copies(mix_refs, mix_w, mix_sems, depth, length, chip, core, lambda copy: copy.wait())
    rows = xb_ref.shape[0]
    columns = mix_w.shape[1]
    chunk = 512
    block = CORES * depth
    for end in (0, length - 1):

        @pl.when(chip == end)
        def _():
            far = (length - 1 - end) * block
            for begin in range(0, columns, chunk):
                span = slice(begin, begin + chunk)
                piece = dot(normed_ref[:, far : far + block], mix_w[:, span])
                projf_ref[:, span] = sumf_ref[:, span] + piece[:rows]
                projb_ref[:, span] = sumb_ref[:, span] + piece[rows:]

    @pl.when((chip > 0) & (chip < length - 1))
    def _():
        projf_ref[...] = sumf_ref[...]
        projb_ref[...] = sumb_ref[...]

    attend_rows(projb_ref, mask_ref[1], heads)
    wait_copies(out_refs, out_w, out_sems, depth, chip, core)
    finish_rows(xb_ref[...], heads[...], out_w[...], gain_e[...], hidden_ref, expert_ref)


def forward_kernel(count, depth, *refs):
    place, x_ref, proj_ref, gain_e, mask_ref = refs[:5]
    out_refs = refs[5 : 5 + count]
    hidden_ref, expert_ref = refs[5 + count : 7 + count]
    out_w, heads, out_sems = refs[7 + count :]
    chip, core = place[0], place[1]
    start_copies(out_refs, out_w, out_sems, depth, chip, core)
    attend_rows(proj_ref, mask_ref[0], heads)
    wait_copies(out_refs, out_w, out_sems, depth, chip, core)
    finish_rows(x_ref[...], heads[...], out_w[...], gain_e[...], hidden_ref, expert_ref)


def picked_gate(gates, me, expert_count, micro):
    lane = lax.broadcasted_iota(jnp.int32, gates.shape, 1)
    first = 2 * micro * expert_count + me
    hit = (lane == first) | (lane == first + expert_count)
    return jnp.sum(jnp.where(hit, gates, 0.0), axis=-1, keepdims=True)


def cotangent_kernel(rows, width, expert_count, *refs):
    place, down_ref, mine, other, act_ref, gate_ref, cot, sems = refs
    chip, core = place[0], place[1]
    me = CORES * chip + core
    fetch_line((mine, other), cot, sems, rows, chip, core)
    chunk = 2 * rows

    def step(index, carry):
        start = chunk_start(index, chunk)
        block = cot[pl.ds(start, chunk), :]
        gates = block[:, width:].astype(F32)
        grad_act = dot(block[:, :width], down_ref[...], NT)
        act_ref[pl.ds(start, chunk), :] = grad_act * picked_gate(gates, me, expert_count, 1)
        gate_ref[pl.ds(start, chunk), :] = jnp.broadcast_to(
            picked_gate(gates, me, expert_count, 0), (chunk, LANES)
        )
        return carry

    each_chunk(expert_count * rows // chunk, step)


def each_chunk(number, step):
    if number <= 4:
        for index in range(number):
            step(index, 0)
    else:
        lax.fori_loop(0, number, step, 0)


def chunk_start(index, chunk):
    return index * chunk if isinstance(index, int) else pl.multiple_of(index * chunk, chunk)


def give_back(result, mine_ref, other_ref, rows, core):
    for owner in range(mine_ref.shape[0]):
        for out_ref, side in ((mine_ref, core), (other_ref, 1 - core)):
            start = pl.multiple_of((CORES * owner + side) * rows, rows)
            out_ref[owner] = result[pl.ds(start, rows), :]


def expert_backward_kernel(rows, *refs):
    place, up_ref, act_ref = refs[:3]
    row_refs = refs[3:5]
    mine_ref, other_ref, tokens, result, sems = refs[5:]
    chip, core = place[0], place[1]
    fetch_line(row_refs, tokens, sems, rows, chip, core)
    chunk = 2 * rows

    def step(index, carry):
        start = chunk_start(index, chunk)
        pre = dot(tokens[pl.ds(start, chunk), :], up_ref[...])
        square = pre * pre
        bend = jnp.tanh(GELU_C * pre * (1.0 + GELU_A * square))
        slope = 0.5 * (1.0 + bend) + 0.5 * pre * (1.0 - bend * bend) * (
            GELU_C * (1.0 + 3.0 * GELU_A * square)
        )
        grad = (act_ref[pl.ds(start, chunk), :] * slope).astype(BF16)
        result[pl.ds(start, chunk), :] = dot(grad, up_ref[...], NT).astype(BF16)
        return carry

    each_chunk(tokens.shape[0] // chunk, step)
    give_back(result, mine_ref, other_ref, rows, core)


def expert_forward_kernel(count, rows, *refs):
    place, up_ref, down_ref, gate_ref = refs[:4]
    row_refs = refs[4 : 4 + count]
    mine_ref, other_ref, tokens, result, sems = refs[4 + count :]
    chip, core = place[0], place[1]
    start_copies(row_refs, tokens, sems, rows, chip, core)
    wait_copies(row_refs, tokens, sems, rows, chip, core)
    chunk = 2 * rows

    def step(index, carry):
        start = chunk_start(index, chunk)
        pre = dot(tokens[pl.ds(start, chunk), :], up_ref[...])
        bend = jnp.tanh(GELU_C * pre * (1.0 + GELU_A * (pre * pre)))
        active = (0.5 * pre * (1.0 + bend)).astype(BF16)
        out = dot(active, down_ref[...])
        gate = gate_ref[pl.ds(start, chunk), :][:, :1]
        result[pl.ds(start, chunk), :] = (gate * out).astype(BF16)
        return carry

    each_chunk(tokens.shape[0] // chunk, step)
    give_back(result, mine_ref, other_ref, rows, core)


def add_kernel(mine_ref, other_ref, out_ref):
    out_ref[...] = (mine_ref[...].astype(F32) + other_ref[...].astype(F32)).astype(BF16)


def add_apart_kernel(place, mine_ref, other_ref, *out_refs):
    for j, out_ref in enumerate(out_refs):
        owner = lax.rem(place[0] + j, len(out_refs))
        out_ref[...] = (mine_ref[owner].astype(F32) + other_ref[owner].astype(F32)).astype(BF16)


def heads_backward_kernel(count, depth, *refs):
    place, cot_ref, hidden_ref, proj_ref, gain_e, mask_ref, part_ref = refs[:7]
    out_refs = refs[7 : 7 + count]
    mixed_ref, grad_ref, out_w, out_sems = refs[7 + count :]
    chip, core = place[0], place[1]
    start_copies(out_refs, out_w, out_sems, depth, chip, core)
    grad_moe = part_ref[0].astype(F32)
    for index in range(1, part_ref.shape[0]):
        grad_moe = grad_moe + part_ref[index].astype(F32)
    hidden = hidden_ref[...]
    rms_two = lax.rsqrt(mean_last(hidden * hidden) + EPS)
    normal_two = hidden * rms_two
    grad_two = grad_moe * gain_e[...]
    grad_hidden = cot_ref[...].astype(F32) + rms_two * (
        grad_two - normal_two * mean_last(grad_two * normal_two)
    )
    grad_ref[...] = grad_hidden
    wait_copies(out_refs, out_w, out_sems, depth, chip, core)
    grad_heads = dot(grad_hidden.astype(BF16), out_w[...], NT).astype(BF16)
    allowed = mask_ref[1] > 0.5
    for head in range(HEADS):
        query_hat, query_scale, key_hat, key_scale, value_bf = head_parts(proj_ref, head)
        query_bf, key_bf = query_hat.astype(BF16), key_hat.astype(BF16)
        probs = attn_probs_of(query_bf, key_bf, allowed)
        grad_out = grad_heads[:, head * HEAD_DIM : (head + 1) * HEAD_DIM]
        grad_probs = dot(grad_out, value_bf, NT)
        grad_value = dot(probs.astype(BF16), grad_out, TN)
        inner = jnp.sum(probs * grad_probs, axis=-1, keepdims=True)
        grad_scores = (probs * (grad_probs - inner) * SCORE_SCALE).astype(BF16)
        grad_qhat = dot(grad_scores, key_bf)
        grad_khat = dot(grad_scores, query_bf, TN)
        grad_query = query_scale * (grad_qhat - query_hat * mean_last(grad_qhat * query_hat))
        grad_key = key_scale * (grad_khat - key_hat * mean_last(grad_khat * key_hat))
        for index, grad in enumerate((grad_query, grad_key, grad_value)):
            start = (index * HEADS + head) * HEAD_DIM
            mixed_ref[:, start : start + HEAD_DIM] = grad.astype(BF16)


def entry_backward_kernel(count, depth, *refs):
    place, x_ref, mixed_ref, grad_ref, gain_a = refs[:5]
    mix_refs = refs[5 : 5 + count]
    result_ref = refs[5 + count]
    mix_w, mix_sems = refs[6 + count :]
    chip, core = place[0], place[1]
    start_copies(mix_refs, mix_w, mix_sems, depth, chip, core)
    wait_copies(mix_refs, mix_w, mix_sems, depth, chip, core)
    grad_normed = dot(mixed_ref[...], mix_w[...], NT)
    x = x_ref[...].astype(F32)
    rms_one = lax.rsqrt(mean_last(x * x) + EPS)
    normal_one = x * rms_one
    grad_one = grad_normed * gain_a[...]
    result = grad_ref[...] + rms_one * (grad_one - normal_one * mean_last(grad_one * normal_one))
    result_ref[...] = result.astype(BF16)


def shaped(shape, kind):
    return jax.ShapeDtypeStruct(shape, kind)


def dma(count):
    return pltpu.SemaphoreType.DMA(count if isinstance(count, tuple) else (count,))


def call(kernel, outs, specs, out_specs, scratch, args):
    return pl.pallas_call(
        kernel,
        out_shape=outs,
        in_specs=specs,
        out_specs=out_specs,
        scratch_shapes=scratch,
        compiler_params=PARAMS,
    )(*args)


def dense_gates(routes, logits, expert_count):
    gates = jax.nn.sigmoid(logits)
    hit = routes[..., None] == jnp.arange(expert_count, dtype=jnp.int32)
    return jnp.sum(jnp.where(hit, gates[..., None], 0.0), axis=2)


def gate_columns(routes, logits, expert_count):
    gates = dense_gates(routes, logits, expert_count)
    high = lax.reduce_precision(gates, 8, 7)
    both = jnp.stack([high, gates - high], axis=1).astype(BF16)
    rows = jnp.transpose(both, (2, 0, 1, 3)).reshape(both.shape[2], -1)
    return jnp.pad(rows, ((0, 0), (0, LANES - rows.shape[1])))


def allowed_of(mask_blocks):
    frame_block = jnp.arange(FRAMES, dtype=jnp.int32) // BLOCK
    spread = (frame_block[:, None] == jnp.arange(FRAMES // BLOCK)[None, :]).astype(F32)
    eye = jnp.eye(FRAMES // BLOCK, dtype=F32)
    open_blocks = jnp.maximum((mask_blocks == 1).astype(F32), eye)
    return jnp.einsum("ib,mbc,jc->mij", spread, open_blocks, spread)


def local(
    handoff_forward,
    stashed_input,
    relay_cotangents,
    attention_gain,
    expert_gain,
    w_qkv,
    w_out,
    w_up,
    w_down,
    routes,
    gate_logits,
    block_mask,
):
    length = line_length()
    expert_count = lax.axis_size("expert")
    me = lax.axis_index("expert")
    place = jnp.stack([me // CORES, me % CORES]).astype(jnp.int32)
    tokens, width = handoff_forward.shape
    depth = w_qkv.shape[1]
    total = expert_count * tokens
    columns = w_qkv.shape[2]
    up_weight = w_up[0, 0]
    down_weight = w_down[0, 0]
    hidden_units = up_weight.shape[1]
    count = CORES * (2 * length - 1)

    mixers = with_partner(relayed(w_qkv[0]))
    outers = with_partner(relayed(w_out[0]))
    arriving = passed_along(handoff_forward, "section", 1)
    cotangent = passed_along(relay_cotangents, "section", -1)
    gates = gate_columns(routes, gate_logits, expert_count)
    cots = spread(jnp.concatenate([cotangent, gates], axis=1))
    mask = allowed_of(block_mask[:, 0])

    half = count // 2
    early_mix = mixers[: half - 2] + mixers[half : count - 2]
    last_mix = mixers[half - 2 : half] + mixers[count - 2 :]
    early = len(early_mix)
    sum_fwd, sum_bwd, normed = call(
        functools.partial(early_kernel, early, depth),
        (
            shaped((tokens, columns), F32),
            shaped((tokens, columns), F32),
            shaped((2 * tokens, width), BF16),
        ),
        [SMEM] + [VMEM] * 3 + [ANY] * early,
        (VMEM,) * 3,
        [pltpu.VMEM((width, columns), BF16), dma(early)],
        [place, arriving, stashed_input, attention_gain] + early_mix,
    )
    proj_fwd, proj_bwd, hidden_bwd, expert_bwd = call(
        functools.partial(project_kernel, count, depth, length),
        (
            shaped((tokens, columns), F32),
            shaped((tokens, columns), F32),
            shaped((tokens, width), F32),
            shaped((tokens, width), BF16),
        ),
        [SMEM] + [VMEM] * 6 + [ANY] * (4 + count),
        (VMEM,) * 4,
        [
            pltpu.VMEM((CORES * depth, columns), BF16),
            pltpu.VMEM((width, width), BF16),
            pltpu.VMEM((tokens, width), BF16),
            dma(4),
            dma(count),
        ],
        [place, sum_fwd, sum_bwd, normed, stashed_input, expert_gain, mask] + last_mix + outers,
    )
    rows_bwd = spread(expert_bwd)

    hidden_fwd, expert_fwd = call(
        functools.partial(forward_kernel, count, depth),
        (shaped((tokens, width), F32), shaped((tokens, width), BF16)),
        [SMEM] + [VMEM] * 4 + [ANY] * count,
        (VMEM,) * 2,
        [pltpu.VMEM((width, width), BF16), pltpu.VMEM((tokens, width), BF16), dma(count)],
        [place, arriving, proj_fwd, expert_gain, mask] + outers,
    )
    rows_fwd = with_partner(relayed(expert_fwd))

    grad_act, gate_fwd = call(
        functools.partial(cotangent_kernel, tokens, width, expert_count),
        (shaped((total, hidden_units), F32), shaped((total, LANES), F32)),
        [SMEM, VMEM] + [ANY] * 2,
        (VMEM,) * 2,
        [pltpu.VMEM((total, width + LANES), BF16), dma((CORES, length))],
        [place, down_weight] + cots,
    )

    pair = (shaped((length, tokens, width), BF16),) * 2

    def expert_scratch(sems):
        return [pltpu.VMEM((total, width), BF16), pltpu.VMEM((total, width), BF16), dma(sems)]

    mine, other = call(
        functools.partial(expert_backward_kernel, tokens),
        pair,
        [SMEM, VMEM, VMEM] + [ANY] * 2,
        (VMEM,) * 2,
        expert_scratch((CORES, length)),
        [place, up_weight, grad_act] + rows_bwd,
    )
    grad_parts = across(call(add_kernel, pair[0], [VMEM] * 2, VMEM, [], [mine, swapped(other)]))

    mine, other = call(
        functools.partial(expert_forward_kernel, count, tokens),
        pair,
        [SMEM, VMEM, VMEM, VMEM] + [ANY] * count,
        (VMEM,) * 2,
        expert_scratch(count),
        [place, up_weight, down_weight, gate_fwd] + rows_fwd,
    )
    moe_parts = scattered(
        call(
            add_apart_kernel,
            (shaped((tokens, width), BF16),) * length,
            [SMEM] + [VMEM] * 2,
            (VMEM,) * length,
            [],
            [place, mine, swapped(other)],
        ),
    )

    grad_mixed, grad_hidden = call(
        functools.partial(heads_backward_kernel, count, depth),
        (shaped((tokens, columns), BF16), shaped((tokens, width), F32)),
        [SMEM] + [VMEM] * 6 + [ANY] * count,
        (VMEM,) * 2,
        [pltpu.VMEM((width, width), BF16), dma(count)],
        [place, cotangent, hidden_bwd, proj_bwd, expert_gain, mask, grad_parts]
        + outers,
    )
    derivative = call(
        functools.partial(entry_backward_kernel, count, depth),
        shaped((tokens, width), BF16),
        [SMEM] + [VMEM] * 4 + [ANY] * count,
        VMEM,
        [pltpu.VMEM((width, columns), BF16), dma(count)],
        [place, stashed_input, grad_mixed, grad_hidden, attention_gain] + mixers,
    )

    layer_output = hidden_fwd
    for part in moe_parts:
        layer_output = layer_output + part.astype(F32)
    return (layer_output.astype(BF16), derivative)


def solution(mesh):
    placed = (
        P(("section", "expert"), None),
        P(("section", "expert"), None),
        P(("section", "expert"), None),
        P("section", None),
        P("section", None),
        P("section", "expert", None),
        P("section", "expert", None),
        P("section", "expert", None, None),
        P("section", "expert", None, None),
        P(None, ("section", "expert"), None),
        P(None, ("section", "expert"), None),
        P(None, ("section", "expert"), None, None),
    )

    return jax.shard_map(
        local,
        mesh=mesh,
        in_specs=placed,
        out_specs=(P(("section", "expert"), None), P(("section", "expert"), None)),
        check_vma=False,
    )
```

```python
import functools

import jax
import jax.numpy as jnp
from jax import lax
from jax.experimental import pallas as pl
from jax.experimental.pallas import tpu as pltpu
from jax.sharding import PartitionSpec as P


HEADS = 8
HEAD_DIM = 128
FRAMES = 128
BLOCK = 16
CORES = 2
LANES = 128

EPS = 1e-06
SCORE_SCALE = HEAD_DIM ** (-0.5)
GELU_C = 0.7978845608028654
GELU_A = 0.044715


F32 = jnp.float32
BF16 = jnp.bfloat16
NT = (((1,), (1,)), ((), ()))
TN = (((0,), (0,)), ((), ()))
ANY = pl.BlockSpec(memory_space=pl.ANY)
SMEM = pl.BlockSpec(memory_space=pltpu.SMEM)
VMEM = pl.BlockSpec(memory_space=pltpu.VMEM)
PARAMS = pltpu.CompilerParams(vmem_limit_bytes=56 * 1024 * 1024)


def dot(a, b, dims=(((1,), (0,)), ((), ()))):
    return lax.dot_general(a, b, dims, preferred_element_type=F32)


def mean_last(values):
    return jnp.mean(values, axis=-1, keepdims=True)


def passed_along(value, axis, steps):
    count = lax.axis_size(axis)
    pairs = [(source, (source + steps) % count) for source in range(count)]
    return lax.ppermute(value, axis, pairs)


def line_length():
    return lax.axis_size("expert") // CORES


def chip_pairs(sources, step):
    return [
        (CORES * chip + core, CORES * (chip + step) + core)
        for chip in sources
        for core in range(CORES)
    ]


def swapped(value):
    count = lax.axis_size("expert")
    return lax.ppermute(value, "expert", [(i, i ^ 1) for i in range(count)])


def hop(value, sources, move):
    return lax.ppermute(value, "expert", chip_pairs(sources, move))


def relayed(value):
    length = line_length()
    entries = [value]
    up = down = value
    for step in range(1, length):
        up = hop(up, range(step - 1, length - 1), 1)
        down = hop(down, range(1, length - step + 1), -1)
        entries += [up, down]
    return entries


def with_partner(entries):
    return entries + [swapped(block) for block in entries]


def scattered(blocks):
    length = line_length()
    up = down = None
    for step in range(1, length):
        far = length - step
        send_up, send_down = blocks[far], blocks[length - far]
        if up is not None:
            send_up = send_up + up
            send_down = send_down + down
        up = hop(send_up, range(0, step), 1)
        down = hop(send_down, range(length - step, length), -1)
    return [blocks[0], up, down]


def across(blocks):
    length = line_length()
    groups = [[CORES * chip + core for chip in range(length)] for core in range(CORES)]
    return lax.all_to_all(
        blocks, "expert", split_axis=0, concat_axis=0, axis_index_groups=groups, tiled=True
    )


def spread(copies):
    mine = across(copies)
    return [mine, swapped(mine)]


def entry_chips(hops, chip):
    length = line_length()
    listing = [(None, chip)]
    for hop in range(1, hops + 1):
        listing.append((chip - hop >= 0, chip - hop))
        listing.append((chip + hop < length, chip + hop))
    return listing


def each_copy(refs, target, sems, rows, chip, core, act):
    count = len(refs) // 2
    listing = entry_chips(count // 2, chip)
    for side in range(CORES):
        for index, (valid, origin) in enumerate(listing):
            number = side * count + index
            owner = CORES * origin + (core if side == 0 else 1 - core)

            def run(number=number, owner=owner):
                start = pl.multiple_of(owner * rows, rows)
                act(
                    pltpu.make_async_copy(
                        refs[number], target.at[pl.ds(start, rows), :], sems.at[number]
                    )
                )

            if valid is None:
                run()
            else:
                pl.when(valid)(run)


def line_copies(refs, target, sems, rows, chip, core, act):
    for side, ref in enumerate(refs):
        for origin in range(ref.shape[0]):
            owner = CORES * origin + (core if side == 0 else 1 - core)
            start = pl.multiple_of(owner * rows, rows)
            act(
                pltpu.make_async_copy(
                    ref.at[origin], target.at[pl.ds(start, rows), :], sems.at[side, origin]
                )
            )


def fetch_line(*args):
    line_copies(*args, lambda copy: copy.start())
    line_copies(*args, lambda copy: copy.wait())


def start_copies(*args):
    each_copy(*args, lambda copy: copy.start())


def wait_copies(*args):
    each_copy(*args, lambda copy: copy.wait())


def head_parts(proj_ref, head):
    def part(index):
        start = (index * HEADS + head) * HEAD_DIM
        return proj_ref[:, start : start + HEAD_DIM]

    query, key, value = part(0), part(1), part(2)
    query_scale = lax.rsqrt(mean_last(query * query) + EPS)
    key_scale = lax.rsqrt(mean_last(key * key) + EPS)
    return query * query_scale, query_scale, key * key_scale, key_scale, value.astype(BF16)


def attn_probs_of(query_bf, key_bf, allowed):
    scores = dot(query_bf, key_bf, NT) * SCORE_SCALE
    expo = jnp.where(allowed, jnp.exp(scores), 0.0)
    return expo / jnp.sum(expo, axis=-1, keepdims=True)


def attend_rows(proj_ref, mask, heads_ref):
    allowed = mask > 0.5
    for head in range(HEADS):
        query_hat, _, key_hat, _, value_bf = head_parts(proj_ref, head)
        probs = attn_probs_of(query_hat.astype(BF16), key_hat.astype(BF16), allowed)
        out = dot(probs.astype(BF16), value_bf)
        heads_ref[:, head * HEAD_DIM : (head + 1) * HEAD_DIM] = out.astype(BF16)


def finish_rows(x, heads, out_w, gain_e, hidden_ref, expert_ref):
    hidden = x.astype(F32) + dot(heads, out_w)
    hidden_ref[...] = hidden
    rms = lax.rsqrt(mean_last(hidden * hidden) + EPS)
    expert_ref[...] = jnp.broadcast_to((hidden * rms * gain_e).astype(BF16), expert_ref.shape)


def early_kernel(count, depth, *refs):
    place, xf_ref, xb_ref, gain_a = refs[:4]
    mix_refs = refs[4 : 4 + count]
    sumf_ref, sumb_ref, normed_ref = refs[4 + count : 7 + count]
    mix_w, mix_sems = refs[7 + count :]
    chip, core = place[0], place[1]
    mix_w[...] = jnp.zeros_like(mix_w)
    start_copies(mix_refs, mix_w, mix_sems, depth, chip, core)
    rows = xf_ref.shape[0]
    for index, x_ref in enumerate((xf_ref, xb_ref)):
        x = x_ref[...].astype(F32)
        rms = lax.rsqrt(mean_last(x * x) + EPS)
        normed_ref[index * rows : (index + 1) * rows, :] = (x * rms * gain_a[...]).astype(BF16)
    wait_copies(mix_refs, mix_w, mix_sems, depth, chip, core)
    columns = mix_w.shape[1]
    chunk = 512
    for begin in range(0, columns, chunk):
        piece = dot(normed_ref[...], mix_w[:, begin : begin + chunk])
        sumf_ref[:, begin : begin + chunk] = piece[:rows]
        sumb_ref[:, begin : begin + chunk] = piece[rows:]


def last_copies(mix_refs, mix_w, sems, depth, length, chip, core, act):
    for which, end in ((0, length - 1), (1, 0)):

        @pl.when(chip == end)
        def _():
            for side in range(CORES):
                start = pl.multiple_of((core if side == 0 else 1 - core) * depth, depth)
                act(
                    pltpu.make_async_copy(
                        mix_refs[2 * side + which],
                        mix_w.at[pl.ds(start, depth), :],
                        sems.at[2 * side + which],
                    )
                )


def project_kernel(count, depth, length, *refs):
    place, sumf_ref, sumb_ref, normed_ref, xb_ref, gain_e, mask_ref = refs[:7]
    mix_refs = refs[7:11]
    out_refs = refs[11 : 11 + count]
    projf_ref, projb_ref, hidden_ref, expert_ref = refs[11 + count : 15 + count]
    mix_w, out_w, heads, mix_sems, out_sems = refs[15 + count :]
    chip, core = place[0], place[1]
    last_copies(mix_refs, mix_w, mix_sems, depth, length, chip, core, lambda copy: copy.start())
    start_copies(out_refs, out_w, out_sems, depth, chip, core)
    last_copies(mix_refs, mix_w, mix_sems, depth, length, chip, core, lambda copy: copy.wait())
    rows = xb_ref.shape[0]
    columns = mix_w.shape[1]
    chunk = 512
    block = CORES * depth
    for end in (0, length - 1):

        @pl.when(chip == end)
        def _():
            far = (length - 1 - end) * block
            for begin in range(0, columns, chunk):
                span = slice(begin, begin + chunk)
                piece = dot(normed_ref[:, far : far + block], mix_w[:, span])
                projf_ref[:, span] = sumf_ref[:, span] + piece[:rows]
                projb_ref[:, span] = sumb_ref[:, span] + piece[rows:]

    @pl.when((chip > 0) & (chip < length - 1))
    def _():
        projf_ref[...] = sumf_ref[...]
        projb_ref[...] = sumb_ref[...]

    attend_rows(projb_ref, mask_ref[1], heads)
    wait_copies(out_refs, out_w, out_sems, depth, chip, core)
    finish_rows(xb_ref[...], heads[...], out_w[...], gain_e[...], hidden_ref, expert_ref)


def forward_kernel(count, depth, *refs):
    place, x_ref, proj_ref, gain_e, mask_ref = refs[:5]
    out_refs = refs[5 : 5 + count]
    hidden_ref, expert_ref = refs[5 + count : 7 + count]
    out_w, heads, out_sems = refs[7 + count :]
    chip, core = place[0], place[1]
    start_copies(out_refs, out_w, out_sems, depth, chip, core)
    attend_rows(proj_ref, mask_ref[0], heads)
    wait_copies(out_refs, out_w, out_sems, depth, chip, core)
    finish_rows(x_ref[...], heads[...], out_w[...], gain_e[...], hidden_ref, expert_ref)


def picked_gate(gates, me, expert_count, micro):
    lane = lax.broadcasted_iota(jnp.int32, gates.shape, 1)
    first = 2 * micro * expert_count + me
    hit = (lane == first) | (lane == first + expert_count)
    return jnp.sum(jnp.where(hit, gates, 0.0), axis=-1, keepdims=True)


def cotangent_kernel(rows, width, expert_count, *refs):
    place, down_ref, mine, other, act_ref, gate_ref, cot, sems = refs
    chip, core = place[0], place[1]
    me = CORES * chip + core
    fetch_line((mine, other), cot, sems, rows, chip, core)
    chunk = 2 * rows

    def step(index, carry):
        start = chunk_start(index, chunk)
        block = cot[pl.ds(start, chunk), :]
        gates = block[:, width:].astype(F32)
        grad_act = dot(block[:, :width], down_ref[...], NT)
        act_ref[pl.ds(start, chunk), :] = grad_act * picked_gate(gates, me, expert_count, 1)
        gate_ref[pl.ds(start, chunk), :] = jnp.broadcast_to(
            picked_gate(gates, me, expert_count, 0), (chunk, LANES)
        )
        return carry

    each_chunk(expert_count * rows // chunk, step)


def each_chunk(number, step):
    if number <= 4:
        for index in range(number):
            step(index, 0)
    else:
        lax.fori_loop(0, number, step, 0)


def chunk_start(index, chunk):
    return index * chunk if isinstance(index, int) else pl.multiple_of(index * chunk, chunk)


def give_back(result, mine_ref, other_ref, rows, core):
    for owner in range(mine_ref.shape[0]):
        for out_ref, side in ((mine_ref, core), (other_ref, 1 - core)):
            start = pl.multiple_of((CORES * owner + side) * rows, rows)
            out_ref[owner] = result[pl.ds(start, rows), :]


def expert_backward_kernel(rows, *refs):
    place, up_ref, act_ref = refs[:3]
    row_refs = refs[3:5]
    mine_ref, other_ref, tokens, result, sems = refs[5:]
    chip, core = place[0], place[1]
    fetch_line(row_refs, tokens, sems, rows, chip, core)
    chunk = 2 * rows

    def step(index, carry):
        start = chunk_start(index, chunk)
        pre = dot(tokens[pl.ds(start, chunk), :], up_ref[...])
        square = pre * pre
        bend = jnp.tanh(GELU_C * pre * (1.0 + GELU_A * square))
        slope = 0.5 * (1.0 + bend) + 0.5 * pre * (1.0 - bend * bend) * (
            GELU_C * (1.0 + 3.0 * GELU_A * square)
        )
        grad = (act_ref[pl.ds(start, chunk), :] * slope).astype(BF16)
        result[pl.ds(start, chunk), :] = dot(grad, up_ref[...], NT).astype(BF16)
        return carry

    each_chunk(tokens.shape[0] // chunk, step)
    give_back(result, mine_ref, other_ref, rows, core)


def expert_forward_kernel(count, rows, *refs):
    place, up_ref, down_ref, gate_ref = refs[:4]
    row_refs = refs[4 : 4 + count]
    mine_ref, other_ref, tokens, result, sems = refs[4 + count :]
    chip, core = place[0], place[1]
    start_copies(row_refs, tokens, sems, rows, chip, core)
    wait_copies(row_refs, tokens, sems, rows, chip, core)
    chunk = 2 * rows

    def step(index, carry):
        start = chunk_start(index, chunk)
        pre = dot(tokens[pl.ds(start, chunk), :], up_ref[...])
        bend = jnp.tanh(GELU_C * pre * (1.0 + GELU_A * (pre * pre)))
        active = (0.5 * pre * (1.0 + bend)).astype(BF16)
        out = dot(active, down_ref[...])
        gate = gate_ref[pl.ds(start, chunk), :][:, :1]
        result[pl.ds(start, chunk), :] = (gate * out).astype(BF16)
        return carry

    each_chunk(tokens.shape[0] // chunk, step)
    give_back(result, mine_ref, other_ref, rows, core)


def add_apart_kernel(place, mine_ref, other_ref, *out_refs):
    for j, out_ref in enumerate(out_refs):
        owner = lax.rem(place[0] + j, len(out_refs))
        out_ref[...] = (mine_ref[owner].astype(F32) + other_ref[owner].astype(F32)).astype(BF16)


def heads_backward_kernel(count, depth, *refs):
    place, cot_ref, hidden_ref, proj_ref, gain_e, mask_ref, part_ref = refs[:7]
    out_refs = refs[7 : 7 + count]
    mixed_ref, grad_ref, out_w, out_sems = refs[7 + count :]
    chip, core = place[0], place[1]
    start_copies(out_refs, out_w, out_sems, depth, chip, core)
    grad_moe = part_ref[0].astype(F32)
    for index in range(1, part_ref.shape[0]):
        grad_moe = grad_moe + part_ref[index].astype(F32)
    hidden = hidden_ref[...]
    rms_two = lax.rsqrt(mean_last(hidden * hidden) + EPS)
    normal_two = hidden * rms_two
    grad_two = grad_moe * gain_e[...]
    grad_hidden = cot_ref[...].astype(F32) + rms_two * (
        grad_two - normal_two * mean_last(grad_two * normal_two)
    )
    grad_ref[...] = grad_hidden
    wait_copies(out_refs, out_w, out_sems, depth, chip, core)
    grad_heads = dot(grad_hidden.astype(BF16), out_w[...], NT).astype(BF16)
    allowed = mask_ref[1] > 0.5
    for head in range(HEADS):
        query_hat, query_scale, key_hat, key_scale, value_bf = head_parts(proj_ref, head)
        query_bf, key_bf = query_hat.astype(BF16), key_hat.astype(BF16)
        probs = attn_probs_of(query_bf, key_bf, allowed)
        grad_out = grad_heads[:, head * HEAD_DIM : (head + 1) * HEAD_DIM]
        grad_probs = dot(grad_out, value_bf, NT)
        grad_value = dot(probs.astype(BF16), grad_out, TN)
        inner = jnp.sum(probs * grad_probs, axis=-1, keepdims=True)
        grad_scores = (probs * (grad_probs - inner) * SCORE_SCALE).astype(BF16)
        grad_qhat = dot(grad_scores, key_bf)
        grad_khat = dot(grad_scores, query_bf, TN)
        grad_query = query_scale * (grad_qhat - query_hat * mean_last(grad_qhat * query_hat))
        grad_key = key_scale * (grad_khat - key_hat * mean_last(grad_khat * key_hat))
        for index, grad in enumerate((grad_query, grad_key, grad_value)):
            start = (index * HEADS + head) * HEAD_DIM
            mixed_ref[:, start : start + HEAD_DIM] = grad.astype(BF16)


def entry_backward_kernel(count, depth, *refs):
    place, x_ref, mixed_ref, grad_ref, gain_a = refs[:5]
    mix_refs = refs[5 : 5 + count]
    result_ref = refs[5 + count]
    mix_w, mix_sems = refs[6 + count :]
    chip, core = place[0], place[1]
    start_copies(mix_refs, mix_w, mix_sems, depth, chip, core)
    wait_copies(mix_refs, mix_w, mix_sems, depth, chip, core)
    grad_normed = dot(mixed_ref[...], mix_w[...], NT)
    x = x_ref[...].astype(F32)
    rms_one = lax.rsqrt(mean_last(x * x) + EPS)
    normal_one = x * rms_one
    grad_one = grad_normed * gain_a[...]
    result = grad_ref[...] + rms_one * (grad_one - normal_one * mean_last(grad_one * normal_one))
    result_ref[...] = result.astype(BF16)


def shaped(shape, kind):
    return jax.ShapeDtypeStruct(shape, kind)


def dma(count):
    return pltpu.SemaphoreType.DMA(count if isinstance(count, tuple) else (count,))


def call(kernel, outs, specs, out_specs, scratch, args):
    return pl.pallas_call(
        kernel,
        out_shape=outs,
        in_specs=specs,
        out_specs=out_specs,
        scratch_shapes=scratch,
        compiler_params=PARAMS,
    )(*args)


def dense_gates(routes, logits, expert_count):
    gates = jax.nn.sigmoid(logits)
    hit = routes[..., None] == jnp.arange(expert_count, dtype=jnp.int32)
    return jnp.sum(jnp.where(hit, gates[..., None], 0.0), axis=2)


def gate_columns(routes, logits, expert_count):
    gates = dense_gates(routes, logits, expert_count)
    high = lax.reduce_precision(gates, 8, 7)
    both = jnp.stack([high, gates - high], axis=1).astype(BF16)
    rows = jnp.transpose(both, (2, 0, 1, 3)).reshape(both.shape[2], -1)
    return jnp.pad(rows, ((0, 0), (0, LANES - rows.shape[1])))


def allowed_of(mask_blocks):
    frame_block = jnp.arange(FRAMES, dtype=jnp.int32) // BLOCK
    spread = (frame_block[:, None] == jnp.arange(FRAMES // BLOCK)[None, :]).astype(F32)
    eye = jnp.eye(FRAMES // BLOCK, dtype=F32)
    open_blocks = jnp.maximum((mask_blocks == 1).astype(F32), eye)
    return jnp.einsum("ib,mbc,jc->mij", spread, open_blocks, spread)


def local(
    handoff_forward,
    stashed_input,
    relay_cotangents,
    attention_gain,
    expert_gain,
    w_qkv,
    w_out,
    w_up,
    w_down,
    routes,
    gate_logits,
    block_mask,
):
    length = line_length()
    expert_count = lax.axis_size("expert")
    me = lax.axis_index("expert")
    place = jnp.stack([me // CORES, me % CORES]).astype(jnp.int32)
    tokens, width = handoff_forward.shape
    depth = w_qkv.shape[1]
    total = expert_count * tokens
    columns = w_qkv.shape[2]
    up_weight = w_up[0, 0]
    down_weight = w_down[0, 0]
    hidden_units = up_weight.shape[1]
    count = CORES * (2 * length - 1)

    mixers = with_partner(relayed(w_qkv[0]))
    outers = with_partner(relayed(w_out[0]))
    arriving = passed_along(handoff_forward, "section", 1)
    cotangent = passed_along(relay_cotangents, "section", -1)
    gates = gate_columns(routes, gate_logits, expert_count)
    cot_block = jnp.concatenate([cotangent, gates], axis=1)
    cots = spread(jnp.broadcast_to(cot_block[None], (length,) + cot_block.shape))
    mask = allowed_of(block_mask[:, 0])

    half = count // 2
    early_mix = mixers[: half - 2] + mixers[half : count - 2]
    last_mix = mixers[half - 2 : half] + mixers[count - 2 :]
    early = len(early_mix)
    sum_fwd, sum_bwd, normed = call(
        functools.partial(early_kernel, early, depth),
        (
            shaped((tokens, columns), F32),
            shaped((tokens, columns), F32),
            shaped((2 * tokens, width), BF16),
        ),
        [SMEM] + [VMEM] * 3 + [ANY] * early,
        (VMEM,) * 3,
        [pltpu.VMEM((width, columns), BF16), dma(early)],
        [place, arriving, stashed_input, attention_gain] + early_mix,
    )
    proj_fwd, proj_bwd, hidden_bwd, expert_bwd = call(
        functools.partial(project_kernel, count, depth, length),
        (
            shaped((tokens, columns), F32),
            shaped((tokens, columns), F32),
            shaped((tokens, width), F32),
            shaped((length, tokens, width), BF16),
        ),
        [SMEM] + [VMEM] * 6 + [ANY] * (4 + count),
        (VMEM,) * 4,
        [
            pltpu.VMEM((CORES * depth, columns), BF16),
            pltpu.VMEM((width, width), BF16),
            pltpu.VMEM((tokens, width), BF16),
            dma(4),
            dma(count),
        ],
        [place, sum_fwd, sum_bwd, normed, stashed_input, expert_gain, mask] + last_mix + outers,
    )
    rows_bwd = spread(expert_bwd)

    hidden_fwd, expert_fwd = call(
        functools.partial(forward_kernel, count, depth),
        (shaped((tokens, width), F32), shaped((tokens, width), BF16)),
        [SMEM] + [VMEM] * 4 + [ANY] * count,
        (VMEM,) * 2,
        [pltpu.VMEM((width, width), BF16), pltpu.VMEM((tokens, width), BF16), dma(count)],
        [place, arriving, proj_fwd, expert_gain, mask] + outers,
    )
    rows_fwd = with_partner(relayed(expert_fwd))

    grad_act, gate_fwd = call(
        functools.partial(cotangent_kernel, tokens, width, expert_count),
        (shaped((total, hidden_units), F32), shaped((total, LANES), F32)),
        [SMEM, VMEM] + [ANY] * 2,
        (VMEM,) * 2,
        [pltpu.VMEM((total, width + LANES), BF16), dma((CORES, length))],
        [place, down_weight] + cots,
    )

    pair = (shaped((length, tokens, width), BF16),) * 2

    def expert_scratch(sems):
        return [pltpu.VMEM((total, width), BF16), pltpu.VMEM((total, width), BF16), dma(sems)]

    mine, other = call(
        functools.partial(expert_backward_kernel, tokens),
        pair,
        [SMEM, VMEM, VMEM] + [ANY] * 2,
        (VMEM,) * 2,
        expert_scratch((CORES, length)),
        [place, up_weight, grad_act] + rows_bwd,
    )
    grad_parts = across(mine + swapped(other))

    mine, other = call(
        functools.partial(expert_forward_kernel, count, tokens),
        pair,
        [SMEM, VMEM, VMEM, VMEM] + [ANY] * count,
        (VMEM,) * 2,
        expert_scratch(count),
        [place, up_weight, down_weight, gate_fwd] + rows_fwd,
    )
    moe_parts = scattered(
        call(
            add_apart_kernel,
            (shaped((tokens, width), BF16),) * length,
            [SMEM] + [VMEM] * 2,
            (VMEM,) * length,
            [],
            [place, mine, swapped(other)],
        ),
    )

    grad_mixed, grad_hidden = call(
        functools.partial(heads_backward_kernel, count, depth),
        (shaped((tokens, columns), BF16), shaped((tokens, width), F32)),
        [SMEM] + [VMEM] * 6 + [ANY] * count,
        (VMEM,) * 2,
        [pltpu.VMEM((width, width), BF16), dma(count)],
        [place, cotangent, hidden_bwd, proj_bwd, expert_gain, mask, grad_parts]
        + outers,
    )
    derivative = call(
        functools.partial(entry_backward_kernel, count, depth),
        shaped((tokens, width), BF16),
        [SMEM] + [VMEM] * 4 + [ANY] * count,
        VMEM,
        [pltpu.VMEM((width, columns), BF16), dma(count)],
        [place, stashed_input, grad_mixed, grad_hidden, attention_gain] + mixers,
    )

    layer_output = hidden_fwd
    for part in moe_parts:
        layer_output = layer_output + part.astype(F32)
    return (layer_output.astype(BF16), derivative)


def solution(mesh):
    placed = (
        P(("section", "expert"), None),
        P(("section", "expert"), None),
        P(("section", "expert"), None),
        P("section", None),
        P("section", None),
        P("section", "expert", None),
        P("section", "expert", None),
        P("section", "expert", None, None),
        P("section", "expert", None, None),
        P(None, ("section", "expert"), None),
        P(None, ("section", "expert"), None),
        P(None, ("section", "expert"), None, None),
    )

    return jax.shard_map(
        local,
        mesh=mesh,
        in_specs=placed,
        out_specs=(P(("section", "expert"), None), P(("section", "expert"), None)),
        check_vma=False,
    )
```

```python
import functools

import jax
import jax.numpy as jnp
from jax import lax
from jax.experimental import pallas as pl
from jax.experimental.pallas import tpu as pltpu
from jax.sharding import PartitionSpec as P


HEADS = 8
HEAD_DIM = 128
FRAMES = 128
BLOCK = 16
CORES = 2
LANES = 128

EPS = 1e-06
SCORE_SCALE = HEAD_DIM ** (-0.5)
GELU_C = 0.7978845608028654
GELU_A = 0.044715


F32 = jnp.float32
BF16 = jnp.bfloat16
NT = (((1,), (1,)), ((), ()))
TN = (((0,), (0,)), ((), ()))
ANY = pl.BlockSpec(memory_space=pl.ANY)
SMEM = pl.BlockSpec(memory_space=pltpu.SMEM)
VMEM = pl.BlockSpec(memory_space=pltpu.VMEM)
PARAMS = pltpu.CompilerParams(vmem_limit_bytes=56 * 1024 * 1024)


def dot(a, b, dims=(((1,), (0,)), ((), ()))):
    return lax.dot_general(a, b, dims, preferred_element_type=F32)


def mean_last(values):
    return jnp.mean(values, axis=-1, keepdims=True)


def passed_along(value, axis, steps):
    count = lax.axis_size(axis)
    pairs = [(source, (source + steps) % count) for source in range(count)]
    return lax.ppermute(value, axis, pairs)


def line_length():
    return lax.axis_size("expert") // CORES


def chip_pairs(sources, step):
    return [
        (CORES * chip + core, CORES * (chip + step) + core)
        for chip in sources
        for core in range(CORES)
    ]


def swapped(value):
    count = lax.axis_size("expert")
    return lax.ppermute(value, "expert", [(i, i ^ 1) for i in range(count)])


def hop(value, sources, move):
    return lax.ppermute(value, "expert", chip_pairs(sources, move))


def relayed(value):
    length = line_length()
    entries = [value]
    up = down = value
    for step in range(1, length):
        up = hop(up, range(step - 1, length - 1), 1)
        down = hop(down, range(1, length - step + 1), -1)
        entries += [up, down]
    return entries


def with_partner(entries):
    return entries + [swapped(block) for block in entries]


def scattered(blocks):
    length = line_length()
    up = down = None
    for step in range(1, length):
        far = length - step
        send_up, send_down = blocks[far], blocks[length - far]
        if up is not None:
            send_up = send_up + up
            send_down = send_down + down
        up = hop(send_up, range(0, step), 1)
        down = hop(send_down, range(length - step, length), -1)
    return [blocks[0], up, down]


def across(blocks):
    length = line_length()
    groups = [[CORES * chip + core for chip in range(length)] for core in range(CORES)]
    return lax.all_to_all(
        blocks, "expert", split_axis=0, concat_axis=0, axis_index_groups=groups, tiled=True
    )


def spread(copies):
    mine = across(copies)
    return [mine, swapped(mine)]


def entry_chips(hops, chip):
    length = line_length()
    listing = [(None, chip)]
    for hop in range(1, hops + 1):
        listing.append((chip - hop >= 0, chip - hop))
        listing.append((chip + hop < length, chip + hop))
    return listing


def each_copy(refs, target, sems, rows, chip, core, act):
    count = len(refs) // 2
    listing = entry_chips(count // 2, chip)
    for side in range(CORES):
        for index, (valid, origin) in enumerate(listing):
            number = side * count + index
            owner = CORES * origin + (core if side == 0 else 1 - core)

            def run(number=number, owner=owner):
                start = pl.multiple_of(owner * rows, rows)
                act(
                    pltpu.make_async_copy(
                        refs[number], target.at[pl.ds(start, rows), :], sems.at[owner]
                    )
                )

            if valid is None:
                run()
            else:
                pl.when(valid)(run)


def line_copies(refs, target, sems, rows, chip, core, act):
    for side, ref in enumerate(refs):
        for origin in range(ref.shape[0]):
            owner = CORES * origin + (core if side == 0 else 1 - core)
            start = pl.multiple_of(owner * rows, rows)
            act(
                pltpu.make_async_copy(
                    ref.at[origin], target.at[pl.ds(start, rows), :], sems.at[side, origin]
                )
            )


def fetch_line(*args):
    line_copies(*args, lambda copy: copy.start())
    line_copies(*args, lambda copy: copy.wait())


def start_copies(*args):
    each_copy(*args, lambda copy: copy.start())


def wait_copies(*args):
    each_copy(*args, lambda copy: copy.wait())


def wait_chip(ref, target, sems, rows, chip):
    for owner in range(CORES * chip, CORES * (chip + 1)):
        pltpu.make_async_copy(
            ref, target.at[owner * rows : (owner + 1) * rows, :], sems.at[owner]
        ).wait()


def head_parts(proj_ref, head):
    def part(index):
        start = (index * HEADS + head) * HEAD_DIM
        return proj_ref[:, start : start + HEAD_DIM]

    query, key, value = part(0), part(1), part(2)
    query_scale = lax.rsqrt(mean_last(query * query) + EPS)
    key_scale = lax.rsqrt(mean_last(key * key) + EPS)
    return query * query_scale, query_scale, key * key_scale, key_scale, value.astype(BF16)


def attn_probs_of(query_bf, key_bf, allowed):
    scores = dot(query_bf, key_bf, NT) * SCORE_SCALE
    expo = jnp.where(allowed, jnp.exp(scores), 0.0)
    return expo / jnp.sum(expo, axis=-1, keepdims=True)


def attend_rows(proj_ref, mask, heads_ref):
    allowed = mask > 0.5
    for head in range(HEADS):
        query_hat, _, key_hat, _, value_bf = head_parts(proj_ref, head)
        probs = attn_probs_of(query_hat.astype(BF16), key_hat.astype(BF16), allowed)
        out = dot(probs.astype(BF16), value_bf)
        heads_ref[:, head * HEAD_DIM : (head + 1) * HEAD_DIM] = out.astype(BF16)


def finish_rows(x, heads, out_w, gain_e, hidden_ref, expert_ref):
    hidden = x.astype(F32) + dot(heads, out_w)
    hidden_ref[...] = hidden
    rms = lax.rsqrt(mean_last(hidden * hidden) + EPS)
    expert_ref[...] = (hidden * rms * gain_e).astype(BF16)


def early_kernel(count, depth, *refs):
    place, xf_ref, xb_ref, gain_a, mask_ref = refs[:5]
    mix_refs = refs[5 : 5 + count]
    sumf_ref, sumb_ref, normed_ref, allowed_ref = refs[5 + count : 9 + count]
    mix_w, mix_sems = refs[9 + count :]
    allowed_ref[...] = mask_ref[...]
    chip, core = place[0], place[1]
    mix_w[...] = jnp.zeros_like(mix_w)
    start_copies(mix_refs, mix_w, mix_sems, depth, chip, core)
    rows = xf_ref.shape[0]
    for index, x_ref in enumerate((xf_ref, xb_ref)):
        x = x_ref[...].astype(F32)
        rms = lax.rsqrt(mean_last(x * x) + EPS)
        normed_ref[index * rows : (index + 1) * rows, :] = (x * rms * gain_a[...]).astype(BF16)
    wait_copies(mix_refs, mix_w, mix_sems, depth, chip, core)
    columns = mix_w.shape[1]
    chunk = 512
    for begin in range(0, columns, chunk):
        piece = dot(normed_ref[...], mix_w[:, begin : begin + chunk])
        sumf_ref[:, begin : begin + chunk] = piece[:rows]
        sumb_ref[:, begin : begin + chunk] = piece[rows:]


def last_copies(mix_refs, mix_w, sems, depth, length, chip, core, act):
    for which, end in ((0, length - 1), (1, 0)):

        @pl.when(chip == end)
        def _():
            for side in range(CORES):
                start = pl.multiple_of((core if side == 0 else 1 - core) * depth, depth)
                act(
                    pltpu.make_async_copy(
                        mix_refs[2 * side + which],
                        mix_w.at[pl.ds(start, depth), :],
                        sems.at[2 * side + which],
                    )
                )


def project_kernel(count, depth, length, *refs):
    place, sumf_ref, sumb_ref, normed_ref, xb_ref, gain_e, mask_ref = refs[:7]
    mix_refs = refs[7:11]
    out_refs = refs[11 : 11 + count]
    projf_ref, projb_ref, hidden_ref, expert_ref = refs[11 + count : 15 + count]
    mix_w, out_w, heads, mix_sems, out_sems = refs[15 + count :]
    chip, core = place[0], place[1]
    last_copies(mix_refs, mix_w, mix_sems, depth, length, chip, core, lambda copy: copy.start())
    start_copies(out_refs, out_w, out_sems, depth, chip, core)
    last_copies(mix_refs, mix_w, mix_sems, depth, length, chip, core, lambda copy: copy.wait())
    rows = xb_ref.shape[0]
    columns = mix_w.shape[1]
    chunk = 512
    block = CORES * depth
    for end in (0, length - 1):

        @pl.when(chip == end)
        def _():
            far = (length - 1 - end) * block
            for begin in range(0, columns, chunk):
                span = slice(begin, begin + chunk)
                piece = dot(normed_ref[:, far : far + block], mix_w[:, span])
                projf_ref[:, span] = sumf_ref[:, span] + piece[:rows]
                projb_ref[:, span] = sumb_ref[:, span] + piece[rows:]

    @pl.when((chip > 0) & (chip < length - 1))
    def _():
        projf_ref[...] = sumf_ref[...]
        projb_ref[...] = sumb_ref[...]

    attend_rows(projb_ref, mask_ref[1], heads)
    wait_copies(out_refs, out_w, out_sems, depth, chip, core)
    finish_rows(xb_ref[...], heads[...], out_w[...], gain_e[...], hidden_ref, expert_ref)


def forward_kernel(count, depth, *refs):
    place, x_ref, proj_ref, gain_e, mask_ref = refs[:5]
    out_refs = refs[5 : 5 + count]
    hidden_ref, expert_ref = refs[5 + count : 7 + count]
    out_w, heads, out_sems = refs[7 + count :]
    chip, core = place[0], place[1]
    start_copies(out_refs, out_w, out_sems, depth, chip, core)
    attend_rows(proj_ref, mask_ref[0], heads)
    wait_copies(out_refs, out_w, out_sems, depth, chip, core)
    finish_rows(x_ref[...], heads[...], out_w[...], gain_e[...], hidden_ref, expert_ref)


def picked_gate(gates, me, expert_count, micro):
    lane = lax.broadcasted_iota(jnp.int32, gates.shape, 1)
    first = 2 * micro * expert_count + me
    hit = (lane == first) | (lane == first + expert_count)
    return jnp.sum(jnp.where(hit, gates, 0.0), axis=-1, keepdims=True)


def cotangent_kernel(rows, width, expert_count, *refs):
    place, down_ref, mine, other, act_ref, gate_ref, cot, sems = refs
    chip, core = place[0], place[1]
    me = CORES * chip + core
    fetch_line((mine, other), cot, sems, rows, chip, core)
    chunk = 2 * rows

    def step(index, carry):
        start = chunk_start(index, chunk)
        block = cot[pl.ds(start, chunk), :]
        gates = block[:, width:].astype(F32)
        grad_act = dot(block[:, :width], down_ref[...], NT)
        act_ref[pl.ds(start, chunk), :] = grad_act * picked_gate(gates, me, expert_count, 1)
        gate_ref[pl.ds(start, chunk), :] = jnp.broadcast_to(
            picked_gate(gates, me, expert_count, 0), (chunk, LANES)
        )
        return carry

    each_chunk(expert_count * rows // chunk, step)


def each_chunk(number, step):
    if number <= 4:
        for index in range(number):
            step(index, 0)
    else:
        lax.fori_loop(0, number, step, 0)


def chunk_start(index, chunk):
    return index * chunk if isinstance(index, int) else pl.multiple_of(index * chunk, chunk)


def give_back(result, mine_ref, other_ref, rows, core):
    for owner in range(mine_ref.shape[0]):
        for out_ref, side in ((mine_ref, core), (other_ref, 1 - core)):
            start = pl.multiple_of((CORES * owner + side) * rows, rows)
            out_ref[owner] = result[pl.ds(start, rows), :]


def expert_backward_kernel(count, rows, *refs):
    place, up_ref, act_ref = refs[:3]
    row_refs = refs[3 : 3 + count]
    mine_ref, other_ref, tokens, result, sems = refs[3 + count :]
    chip, core = place[0], place[1]
    start_copies(row_refs, tokens, sems, rows, chip, core)
    wait_copies(row_refs, tokens, sems, rows, chip, core)
    chunk = 2 * rows

    def step(index, carry):
        start = chunk_start(index, chunk)
        pre = dot(tokens[pl.ds(start, chunk), :], up_ref[...], NT)
        square = pre * pre
        bend = jnp.tanh(GELU_C * pre * (1.0 + GELU_A * square))
        slope = 0.5 * (1.0 + bend) + 0.5 * pre * (1.0 - bend * bend) * (
            GELU_C * (1.0 + 3.0 * GELU_A * square)
        )
        grad = (act_ref[pl.ds(start, chunk), :] * slope).astype(BF16)
        result[pl.ds(start, chunk), :] = dot(grad, up_ref[...]).astype(BF16)
        return carry

    each_chunk(tokens.shape[0] // chunk, step)
    give_back(result, mine_ref, other_ref, rows, core)


def expert_forward_kernel(count, rows, *refs):
    place, up_ref, down_ref, gate_ref = refs[:4]
    row_refs = refs[4 : 4 + count]
    mine_ref, other_ref, tokens, result, sems = refs[4 + count :]
    chip, core = place[0], place[1]
    start_copies(row_refs, tokens, sems, rows, chip, core)
    wait_copies(row_refs, tokens, sems, rows, chip, core)
    chunk = 2 * rows

    def step(index, carry):
        start = chunk_start(index, chunk)
        pre = dot(tokens[pl.ds(start, chunk), :], up_ref[...], NT)
        bend = jnp.tanh(GELU_C * pre * (1.0 + GELU_A * (pre * pre)))
        active = (0.5 * pre * (1.0 + bend)).astype(BF16)
        out = dot(active, down_ref[...])
        gate = gate_ref[pl.ds(start, chunk), :][:, :1]
        result[pl.ds(start, chunk), :] = (gate * out).astype(BF16)
        return carry

    each_chunk(tokens.shape[0] // chunk, step)
    give_back(result, mine_ref, other_ref, rows, core)


def add_apart_kernel(place, mine_ref, other_ref, *out_refs):
    for j, out_ref in enumerate(out_refs):
        owner = lax.rem(place[0] + j, len(out_refs))
        out_ref[...] = (mine_ref[owner].astype(F32) + other_ref[owner].astype(F32)).astype(BF16)


def heads_backward_kernel(count, depth, *refs):
    place, cot_ref, hidden_ref, proj_ref, gain_e, mask_ref, part_ref = refs[:7]
    out_refs = refs[7 : 7 + count]
    mixed_ref, grad_ref, out_w, out_sems = refs[7 + count :]
    chip, core = place[0], place[1]
    start_copies(out_refs, out_w, out_sems, depth, chip, core)
    grad_moe = part_ref[0].astype(F32)
    for index in range(1, part_ref.shape[0]):
        grad_moe = grad_moe + part_ref[index].astype(F32)
    hidden = hidden_ref[...]
    rms_two = lax.rsqrt(mean_last(hidden * hidden) + EPS)
    normal_two = hidden * rms_two
    grad_two = grad_moe * gain_e[...]
    grad_hidden = cot_ref[...].astype(F32) + rms_two * (
        grad_two - normal_two * mean_last(grad_two * normal_two)
    )
    grad_ref[...] = grad_hidden
    wait_copies(out_refs, out_w, out_sems, depth, chip, core)
    grad_heads = dot(grad_hidden.astype(BF16), out_w[...], NT).astype(BF16)
    allowed = mask_ref[1] > 0.5
    for head in range(HEADS):
        query_hat, query_scale, key_hat, key_scale, value_bf = head_parts(proj_ref, head)
        query_bf, key_bf = query_hat.astype(BF16), key_hat.astype(BF16)
        probs = attn_probs_of(query_bf, key_bf, allowed)
        grad_out = grad_heads[:, head * HEAD_DIM : (head + 1) * HEAD_DIM]
        grad_probs = dot(grad_out, value_bf, NT)
        grad_value = dot(probs.astype(BF16), grad_out, TN)
        inner = jnp.sum(probs * grad_probs, axis=-1, keepdims=True)
        grad_scores = (probs * (grad_probs - inner) * SCORE_SCALE).astype(BF16)
        grad_qhat = dot(grad_scores, key_bf)
        grad_khat = dot(grad_scores, query_bf, TN)
        grad_query = query_scale * (grad_qhat - query_hat * mean_last(grad_qhat * query_hat))
        grad_key = key_scale * (grad_khat - key_hat * mean_last(grad_khat * key_hat))
        for index, grad in enumerate((grad_query, grad_key, grad_value)):
            start = (index * HEADS + head) * HEAD_DIM
            mixed_ref[:, start : start + HEAD_DIM] = grad.astype(BF16)


def entry_backward_kernel(count, depth, *refs):
    place, x_ref, mixed_ref, grad_ref, gain_a = refs[:5]
    mix_refs = refs[5 : 5 + count]
    result_ref = refs[5 + count]
    mix_w, normed, mix_sems = refs[6 + count :]
    chip, core = place[0], place[1]
    start_copies(mix_refs, mix_w, mix_sems, depth, chip, core)
    block = CORES * depth
    for origin in range(mix_w.shape[0] // block):
        wait_chip(mix_refs[0], mix_w, mix_sems, depth, origin)
        span = slice(origin * block, (origin + 1) * block)
        normed[:, span] = dot(mixed_ref[...], mix_w[span, :], NT)
    grad_normed = normed[...]
    x = x_ref[...].astype(F32)
    rms_one = lax.rsqrt(mean_last(x * x) + EPS)
    normal_one = x * rms_one
    grad_one = grad_normed * gain_a[...]
    result = grad_ref[...] + rms_one * (grad_one - normal_one * mean_last(grad_one * normal_one))
    result_ref[...] = result.astype(BF16)


def shaped(shape, kind):
    return jax.ShapeDtypeStruct(shape, kind)


def dma(count):
    return pltpu.SemaphoreType.DMA(count if isinstance(count, tuple) else (count,))


def call(kernel, outs, specs, out_specs, scratch, args):
    return pl.pallas_call(
        kernel,
        out_shape=outs,
        in_specs=specs,
        out_specs=out_specs,
        scratch_shapes=scratch,
        compiler_params=PARAMS,
    )(*args)


def dense_gates(routes, logits, expert_count):
    gates = jax.nn.sigmoid(logits)
    hit = routes[..., None] == jnp.arange(expert_count, dtype=jnp.int32)
    return jnp.sum(jnp.where(hit, gates[..., None], 0.0), axis=2)


def gate_columns(routes, logits, expert_count):
    gates = dense_gates(routes, logits, expert_count)
    high = lax.reduce_precision(gates, 8, 7)
    both = jnp.stack([high, gates - high], axis=1).astype(BF16)
    rows = jnp.transpose(both, (2, 0, 1, 3)).reshape(both.shape[2], -1)
    return jnp.pad(rows, ((0, 0), (0, LANES - rows.shape[1])))


def allowed_of(mask_blocks):
    frame_block = jnp.arange(FRAMES, dtype=jnp.int32) // BLOCK
    spread = (frame_block[:, None] == jnp.arange(FRAMES // BLOCK)[None, :]).astype(F32)
    eye = jnp.eye(FRAMES // BLOCK, dtype=F32)
    open_blocks = jnp.maximum((mask_blocks == 1).astype(F32), eye)
    return jnp.einsum("ib,mbc,jc->mij", spread, open_blocks, spread)


def local(
    handoff_forward,
    stashed_input,
    relay_cotangents,
    attention_gain,
    expert_gain,
    w_qkv,
    w_out,
    w_up,
    w_down,
    routes,
    gate_logits,
    block_mask,
):
    length = line_length()
    expert_count = lax.axis_size("expert")
    me = lax.axis_index("expert")
    place = jnp.stack([me // CORES, me % CORES]).astype(jnp.int32)
    tokens, width = handoff_forward.shape
    depth = w_qkv.shape[1]
    total = expert_count * tokens
    columns = w_qkv.shape[2]
    up_weight = jnp.swapaxes(w_up[0, 0], 0, 1)
    down_weight = w_down[0, 0]
    hidden_units = up_weight.shape[0]
    count = CORES * (2 * length - 1)

    mixers = with_partner(relayed(w_qkv[0]))
    outers = with_partner(relayed(w_out[0]))
    arriving = passed_along(handoff_forward, "section", 1)
    cotangent = passed_along(relay_cotangents, "section", -1)
    gates = gate_columns(routes, gate_logits, expert_count)
    cot_block = jnp.concatenate([cotangent, gates], axis=1)
    cots = spread(jnp.broadcast_to(cot_block[None], (length,) + cot_block.shape))
    mask = allowed_of(block_mask[:, 0])

    half = count // 2
    early_mix = mixers[: half - 2] + mixers[half : count - 2]
    last_mix = mixers[half - 2 : half] + mixers[count - 2 :]
    early = len(early_mix)
    sum_fwd, sum_bwd, normed, mask = call(
        functools.partial(early_kernel, early, depth),
        (
            shaped((tokens, columns), F32),
            shaped((tokens, columns), F32),
            shaped((2 * tokens, width), BF16),
            shaped(mask.shape, F32),
        ),
        [SMEM] + [VMEM] * 4 + [ANY] * early,
        (VMEM,) * 4,
        [pltpu.VMEM((width, columns), BF16), dma(expert_count)],
        [place, arriving, stashed_input, attention_gain, mask] + early_mix,
    )
    proj_fwd, proj_bwd, hidden_bwd, expert_bwd = call(
        functools.partial(project_kernel, count, depth, length),
        (
            shaped((tokens, columns), F32),
            shaped((tokens, columns), F32),
            shaped((tokens, width), F32),
            shaped((tokens, width), BF16),
        ),
        [SMEM] + [VMEM] * 6 + [ANY] * (4 + count),
        (VMEM,) * 4,
        [
            pltpu.VMEM((CORES * depth, columns), BF16),
            pltpu.VMEM((width, width), BF16),
            pltpu.VMEM((tokens, width), BF16),
            dma(4),
            dma(expert_count),
        ],
        [place, sum_fwd, sum_bwd, normed, stashed_input, expert_gain, mask] + last_mix + outers,
    )
    rows_bwd = with_partner(relayed(expert_bwd))

    hidden_fwd, expert_fwd = call(
        functools.partial(forward_kernel, count, depth),
        (shaped((tokens, width), F32), shaped((tokens, width), BF16)),
        [SMEM] + [VMEM] * 4 + [ANY] * count,
        (VMEM,) * 2,
        [pltpu.VMEM((width, width), BF16), pltpu.VMEM((tokens, width), BF16), dma(expert_count)],
        [place, arriving, proj_fwd, expert_gain, mask] + outers,
    )
    rows_fwd = with_partner(relayed(expert_fwd))

    grad_act, gate_fwd = call(
        functools.partial(cotangent_kernel, tokens, width, expert_count),
        (shaped((total, hidden_units), F32), shaped((total, LANES), F32)),
        [SMEM, VMEM] + [ANY] * 2,
        (VMEM,) * 2,
        [pltpu.VMEM((total, width + LANES), BF16), dma((CORES, length))],
        [place, down_weight] + cots,
    )

    pair = (shaped((length, tokens, width), BF16),) * 2

    def expert_scratch(sems):
        return [pltpu.VMEM((total, width), BF16), pltpu.VMEM((total, width), BF16), dma(sems)]

    mine, other = call(
        functools.partial(expert_backward_kernel, count, tokens),
        pair,
        [SMEM, VMEM, VMEM] + [ANY] * count,
        (VMEM,) * 2,
        expert_scratch(expert_count),
        [place, up_weight, grad_act] + rows_bwd,
    )
    grad_parts = across(mine + swapped(other))

    mine, other = call(
        functools.partial(expert_forward_kernel, count, tokens),
        pair,
        [SMEM, VMEM, VMEM, VMEM] + [ANY] * count,
        (VMEM,) * 2,
        expert_scratch(expert_count),
        [place, up_weight, down_weight, gate_fwd] + rows_fwd,
    )
    moe_parts = scattered(
        call(
            add_apart_kernel,
            (shaped((tokens, width), BF16),) * length,
            [SMEM] + [VMEM] * 2,
            (VMEM,) * length,
            [],
            [place, mine, swapped(other)],
        ),
    )

    grad_mixed, grad_hidden = call(
        functools.partial(heads_backward_kernel, count, depth),
        (shaped((tokens, columns), BF16), shaped((tokens, width), F32)),
        [SMEM] + [VMEM] * 6 + [ANY] * count,
        (VMEM,) * 2,
        [pltpu.VMEM((width, width), BF16), dma(expert_count)],
        [place, cotangent, hidden_bwd, proj_bwd, expert_gain, mask, grad_parts]
        + outers,
    )
    derivative = call(
        functools.partial(entry_backward_kernel, count, depth),
        shaped((tokens, width), BF16),
        [SMEM] + [VMEM] * 4 + [ANY] * count,
        VMEM,
        [
            pltpu.VMEM((width, columns), BF16),
            pltpu.VMEM((tokens, width), F32),
            dma(expert_count),
        ],
        [place, stashed_input, grad_mixed, grad_hidden, attention_gain] + mixers,
    )

    layer_output = hidden_fwd
    for part in moe_parts:
        layer_output = layer_output + part.astype(F32)
    return (layer_output.astype(BF16), derivative)


def solution(mesh):
    placed = (
        P(("section", "expert"), None),
        P(("section", "expert"), None),
        P(("section", "expert"), None),
        P("section", None),
        P("section", None),
        P("section", "expert", None),
        P("section", "expert", None),
        P("section", "expert", None, None),
        P("section", "expert", None, None),
        P(None, ("section", "expert"), None),
        P(None, ("section", "expert"), None),
        P(None, ("section", "expert"), None, None),
    )

    return jax.shard_map(
        local,
        mesh=mesh,
        in_specs=placed,
        out_specs=(P(("section", "expert"), None), P(("section", "expert"), None)),
        check_vma=False,
    )
```

```python
import functools

import jax
import jax.numpy as jnp
from jax import lax
from jax.experimental import pallas as pl
from jax.experimental.pallas import tpu as pltpu
from jax.sharding import PartitionSpec as P


HEADS = 8
HEAD_DIM = 128
FRAMES = 128
BLOCK = 16
CORES = 2
LANES = 128

EPS = 1e-06
SCORE_SCALE = HEAD_DIM ** (-0.5)
GELU_C = 0.7978845608028654
GELU_A = 0.044715


F32 = jnp.float32
BF16 = jnp.bfloat16
NT = (((1,), (1,)), ((), ()))
TN = (((0,), (0,)), ((), ()))
ANY = pl.BlockSpec(memory_space=pl.ANY)
SMEM = pl.BlockSpec(memory_space=pltpu.SMEM)
VMEM = pl.BlockSpec(memory_space=pltpu.VMEM)
PARAMS = pltpu.CompilerParams(vmem_limit_bytes=56 * 1024 * 1024)


def dot(a, b, dims=(((1,), (0,)), ((), ()))):
    return lax.dot_general(a, b, dims, preferred_element_type=F32)


def mean_last(values):
    return jnp.mean(values, axis=-1, keepdims=True)


def passed_along(value, steps):
    count = lax.axis_size("section")
    pairs = [(source, (source + steps) % count) for source in range(count)]
    return lax.ppermute(value, "section", pairs)


def line_length():
    return lax.axis_size("expert") // CORES


def chip_pairs(sources, step):
    return [
        (CORES * chip + core, CORES * (chip + step) + core)
        for chip in sources
        for core in range(CORES)
    ]


def swapped(value):
    count = lax.axis_size("expert")
    return lax.ppermute(value, "expert", [(i, i ^ 1) for i in range(count)])


def hop(value, sources, move):
    return lax.ppermute(value, "expert", chip_pairs(sources, move))


def relayed(value):
    length = line_length()
    entries = [value]
    up = down = value
    for step in range(1, length):
        up = hop(up, range(step - 1, length - 1), 1)
        down = hop(down, range(1, length - step + 1), -1)
        entries += [up, down]
    return entries


def with_partner(entries):
    return entries + [swapped(block) for block in entries]


def scattered(blocks):
    length = line_length()
    up = down = None
    for step in range(1, length):
        far = length - step
        send_up, send_down = blocks[far], blocks[length - far]
        if up is not None:
            send_up = send_up + up
            send_down = send_down + down
        up = hop(send_up, range(0, step), 1)
        down = hop(send_down, range(length - step, length), -1)
    return [blocks[0], up, down]


def across(blocks):
    length = line_length()
    groups = [[CORES * chip + core for chip in range(length)] for core in range(CORES)]
    return lax.all_to_all(
        blocks, "expert", split_axis=0, concat_axis=0, axis_index_groups=groups, tiled=True
    )


def spread(copies):
    mine = across(copies)
    return [mine, swapped(mine)]


def entry_chips(hops, chip):
    length = line_length()
    listing = [(None, chip)]
    for hop in range(1, hops + 1):
        listing.append((chip - hop >= 0, chip - hop))
        listing.append((chip + hop < length, chip + hop))
    return listing


def each_copy(refs, target, sems, rows, chip, core, act):
    count = len(refs) // 2
    listing = entry_chips(count // 2, chip)
    for side in range(CORES):
        for index, (valid, origin) in enumerate(listing):
            number = side * count + index
            owner = CORES * origin + (core if side == 0 else 1 - core)

            def run(number=number, owner=owner):
                start = pl.multiple_of(owner * rows, rows)
                act(
                    pltpu.make_async_copy(
                        refs[number], target.at[pl.ds(start, rows), :], sems.at[owner]
                    )
                )

            if valid is None:
                run()
            else:
                pl.when(valid)(run)


def line_copies(refs, target, sems, rows, chip, core, act):
    for side, ref in enumerate(refs):
        for origin in range(ref.shape[0]):
            owner = CORES * origin + (core if side == 0 else 1 - core)
            start = pl.multiple_of(owner * rows, rows)
            act(
                pltpu.make_async_copy(
                    ref.at[origin], target.at[pl.ds(start, rows), :], sems.at[side, origin]
                )
            )


def fetch_line(*args):
    line_copies(*args, lambda copy: copy.start())
    line_copies(*args, lambda copy: copy.wait())


def start_copies(*args):
    each_copy(*args, lambda copy: copy.start())


def wait_copies(*args):
    each_copy(*args, lambda copy: copy.wait())


def head_parts(proj_ref, head):
    def part(index):
        start = (index * HEADS + head) * HEAD_DIM
        return proj_ref[:, start : start + HEAD_DIM]

    query, key, value = part(0), part(1), part(2)
    query_scale = lax.rsqrt(mean_last(query * query) + EPS)
    key_scale = lax.rsqrt(mean_last(key * key) + EPS)
    return query * query_scale, query_scale, key * key_scale, key_scale, value.astype(BF16)


def attn_probs_of(query_bf, key_bf, allowed):
    scores = dot(query_bf, key_bf, NT) * SCORE_SCALE
    expo = jnp.where(allowed, jnp.exp(scores), 0.0)
    return expo / jnp.sum(expo, axis=-1, keepdims=True)


def attend_rows(proj_ref, mask, heads_ref):
    allowed = mask > 0.5
    for head in range(HEADS):
        query_hat, _, key_hat, _, value_bf = head_parts(proj_ref, head)
        probs = attn_probs_of(query_hat.astype(BF16), key_hat.astype(BF16), allowed)
        out = dot(probs.astype(BF16), value_bf)
        heads_ref[:, head * HEAD_DIM : (head + 1) * HEAD_DIM] = out.astype(BF16)


def finish_rows(x, heads, out_w, gain_e, hidden_ref, expert_ref):
    hidden = x.astype(F32) + dot(heads, out_w)
    hidden_ref[...] = hidden
    rms = lax.rsqrt(mean_last(hidden * hidden) + EPS)
    expert_ref[...] = (hidden * rms * gain_e).astype(BF16)


def early_kernel(count, depth, *refs):
    place, xf_ref, xb_ref, gain_a, mask_ref = refs[:5]
    mix_refs = refs[5 : 5 + count]
    sumf_ref, sumb_ref, normed_ref, allowed_ref = refs[5 + count : 9 + count]
    mix_w, mix_sems = refs[9 + count :]
    allowed_ref[...] = mask_ref[...]
    chip, core = place[0], place[1]
    mix_w[...] = jnp.zeros_like(mix_w)
    start_copies(mix_refs, mix_w, mix_sems, depth, chip, core)
    rows = xf_ref.shape[0]
    for index, x_ref in enumerate((xf_ref, xb_ref)):
        x = x_ref[...].astype(F32)
        rms = lax.rsqrt(mean_last(x * x) + EPS)
        normed_ref[index * rows : (index + 1) * rows, :] = (x * rms * gain_a[...]).astype(BF16)
    wait_copies(mix_refs, mix_w, mix_sems, depth, chip, core)
    columns = mix_w.shape[1]
    chunk = 512
    for begin in range(0, columns, chunk):
        piece = dot(normed_ref[...], mix_w[:, begin : begin + chunk])
        sumf_ref[:, begin : begin + chunk] = piece[:rows]
        sumb_ref[:, begin : begin + chunk] = piece[rows:]


def last_copies(mix_refs, mix_w, sems, depth, length, chip, core, act):
    for which, end in ((0, length - 1), (1, 0)):

        @pl.when(chip == end)
        def _():
            for side in range(CORES):
                start = pl.multiple_of((core if side == 0 else 1 - core) * depth, depth)
                act(
                    pltpu.make_async_copy(
                        mix_refs[2 * side + which],
                        mix_w.at[pl.ds(start, depth), :],
                        sems.at[2 * side + which],
                    )
                )


def project_kernel(count, depth, length, *refs):
    place, sumf_ref, sumb_ref, normed_ref, xb_ref, gain_e, mask_ref = refs[:7]
    mix_refs = refs[7:11]
    out_refs = refs[11 : 11 + count]
    projf_ref, projb_ref, hidden_ref, expert_ref = refs[11 + count : 15 + count]
    mix_w, out_w, heads, mix_sems, out_sems = refs[15 + count :]
    chip, core = place[0], place[1]
    last_copies(mix_refs, mix_w, mix_sems, depth, length, chip, core, lambda copy: copy.start())
    start_copies(out_refs, out_w, out_sems, depth, chip, core)
    last_copies(mix_refs, mix_w, mix_sems, depth, length, chip, core, lambda copy: copy.wait())
    rows = xb_ref.shape[0]
    columns = mix_w.shape[1]
    chunk = 512
    block = CORES * depth
    for end in (0, length - 1):

        @pl.when(chip == end)
        def _():
            far = (length - 1 - end) * block
            for begin in range(0, columns, chunk):
                span = slice(begin, begin + chunk)
                piece = dot(normed_ref[:, far : far + block], mix_w[:, span])
                projf_ref[:, span] = sumf_ref[:, span] + piece[:rows]
                projb_ref[:, span] = sumb_ref[:, span] + piece[rows:]

    @pl.when((chip > 0) & (chip < length - 1))
    def _():
        projf_ref[...] = sumf_ref[...]
        projb_ref[...] = sumb_ref[...]

    attend_rows(projb_ref, mask_ref[1], heads)
    wait_copies(out_refs, out_w, out_sems, depth, chip, core)
    finish_rows(xb_ref[...], heads[...], out_w[...], gain_e[...], hidden_ref, expert_ref)


def forward_kernel(count, depth, *refs):
    place, x_ref, proj_ref, gain_e, mask_ref = refs[:5]
    out_refs = refs[5 : 5 + count]
    hidden_ref, expert_ref = refs[5 + count : 7 + count]
    out_w, heads, out_sems = refs[7 + count :]
    chip, core = place[0], place[1]
    start_copies(out_refs, out_w, out_sems, depth, chip, core)
    attend_rows(proj_ref, mask_ref[0], heads)
    wait_copies(out_refs, out_w, out_sems, depth, chip, core)
    finish_rows(x_ref[...], heads[...], out_w[...], gain_e[...], hidden_ref, expert_ref)


def picked_gate(gates, me, expert_count, micro):
    lane = lax.broadcasted_iota(jnp.int32, gates.shape, 1)
    first = 2 * micro * expert_count + me
    hit = (lane == first) | (lane == first + expert_count)
    return jnp.sum(jnp.where(hit, gates, 0.0), axis=-1, keepdims=True)


def cotangent_kernel(rows, width, expert_count, *refs):
    place, down_ref, mine, other, act_ref, gate_ref, cot, sems = refs
    chip, core = place[0], place[1]
    me = CORES * chip + core
    fetch_line((mine, other), cot, sems, rows, chip, core)
    chunk = 2 * rows

    def step(index, carry):
        start = chunk_start(index, chunk)
        block = cot[pl.ds(start, chunk), :]
        gates = block[:, width:].astype(F32)
        grad_act = dot(block[:, :width], down_ref[...], NT)
        act_ref[pl.ds(start, chunk), :] = grad_act * picked_gate(gates, me, expert_count, 1)
        gate_ref[pl.ds(start, chunk), :] = jnp.broadcast_to(
            picked_gate(gates, me, expert_count, 0), (chunk, LANES)
        )
        return carry

    each_chunk(expert_count * rows // chunk, step)


def each_chunk(number, step):
    if number <= 4:
        for index in range(number):
            step(index, 0)
    else:
        lax.fori_loop(0, number, step, 0)


def chunk_start(index, chunk):
    return index * chunk if isinstance(index, int) else pl.multiple_of(index * chunk, chunk)


def give_back(result, mine_ref, other_ref, rows, core):
    for owner in range(mine_ref.shape[0]):
        for out_ref, side in ((mine_ref, core), (other_ref, 1 - core)):
            start = pl.multiple_of((CORES * owner + side) * rows, rows)
            out_ref[owner] = result[pl.ds(start, rows), :]


def expert_backward_kernel(count, rows, *refs):
    place, up_ref, act_ref = refs[:3]
    row_refs = refs[3 : 3 + count]
    mine_ref, other_ref, tokens, result, sems = refs[3 + count :]
    chip, core = place[0], place[1]
    start_copies(row_refs, tokens, sems, rows, chip, core)
    wait_copies(row_refs, tokens, sems, rows, chip, core)
    chunk = 2 * rows

    def step(index, carry):
        start = chunk_start(index, chunk)
        pre = dot(tokens[pl.ds(start, chunk), :], up_ref[...], NT)
        square = pre * pre
        bend = jnp.tanh(GELU_C * pre * (1.0 + GELU_A * square))
        slope = 0.5 * (1.0 + bend) + 0.5 * pre * (1.0 - bend * bend) * (
            GELU_C * (1.0 + 3.0 * GELU_A * square)
        )
        grad = (act_ref[pl.ds(start, chunk), :] * slope).astype(BF16)
        result[pl.ds(start, chunk), :] = dot(grad, up_ref[...]).astype(BF16)
        return carry

    each_chunk(tokens.shape[0] // chunk, step)
    give_back(result, mine_ref, other_ref, rows, core)


def expert_forward_kernel(count, rows, *refs):
    place, up_ref, down_ref, gate_ref = refs[:4]
    row_refs = refs[4 : 4 + count]
    mine_ref, other_ref, tokens, result, sems = refs[4 + count :]
    chip, core = place[0], place[1]
    start_copies(row_refs, tokens, sems, rows, chip, core)
    wait_copies(row_refs, tokens, sems, rows, chip, core)
    chunk = 2 * rows

    def step(index, carry):
        start = chunk_start(index, chunk)
        pre = dot(tokens[pl.ds(start, chunk), :], up_ref[...], NT)
        bend = jnp.tanh(GELU_C * pre * (1.0 + GELU_A * (pre * pre)))
        active = (0.5 * pre * (1.0 + bend)).astype(BF16)
        out = dot(active, down_ref[...])
        gate = gate_ref[pl.ds(start, chunk), :][:, :1]
        result[pl.ds(start, chunk), :] = (gate * out).astype(BF16)
        return carry

    each_chunk(tokens.shape[0] // chunk, step)
    give_back(result, mine_ref, other_ref, rows, core)


def add_apart_kernel(place, mine_ref, other_ref, *out_refs):
    for j, out_ref in enumerate(out_refs):
        owner = lax.rem(place[0] + j, len(out_refs))
        out_ref[...] = (mine_ref[owner].astype(F32) + other_ref[owner].astype(F32)).astype(BF16)


def heads_backward_kernel(count, depth, *refs):
    place, cot_ref, hidden_ref, proj_ref, gain_e, mask_ref, part_ref = refs[:7]
    out_refs = refs[7 : 7 + count]
    mixed_ref, grad_ref, out_w, out_sems = refs[7 + count :]
    chip, core = place[0], place[1]
    start_copies(out_refs, out_w, out_sems, depth, chip, core)
    grad_moe = part_ref[0].astype(F32)
    for index in range(1, part_ref.shape[0]):
        grad_moe = grad_moe + part_ref[index].astype(F32)
    hidden = hidden_ref[...]
    rms_two = lax.rsqrt(mean_last(hidden * hidden) + EPS)
    normal_two = hidden * rms_two
    grad_two = grad_moe * gain_e[...]
    grad_hidden = cot_ref[...].astype(F32) + rms_two * (
        grad_two - normal_two * mean_last(grad_two * normal_two)
    )
    grad_ref[...] = grad_hidden
    wait_copies(out_refs, out_w, out_sems, depth, chip, core)
    grad_heads = dot(grad_hidden.astype(BF16), out_w[...], NT).astype(BF16)
    allowed = mask_ref[1] > 0.5
    for head in range(HEADS):
        query_hat, query_scale, key_hat, key_scale, value_bf = head_parts(proj_ref, head)
        query_bf, key_bf = query_hat.astype(BF16), key_hat.astype(BF16)
        probs = attn_probs_of(query_bf, key_bf, allowed)
        grad_out = grad_heads[:, head * HEAD_DIM : (head + 1) * HEAD_DIM]
        grad_probs = dot(grad_out, value_bf, NT)
        grad_value = dot(probs.astype(BF16), grad_out, TN)
        inner = jnp.sum(probs * grad_probs, axis=-1, keepdims=True)
        grad_scores = (probs * (grad_probs - inner) * SCORE_SCALE).astype(BF16)
        grad_qhat = dot(grad_scores, key_bf)
        grad_khat = dot(grad_scores, query_bf, TN)
        grad_query = query_scale * (grad_qhat - query_hat * mean_last(grad_qhat * query_hat))
        grad_key = key_scale * (grad_khat - key_hat * mean_last(grad_khat * key_hat))
        for index, grad in enumerate((grad_query, grad_key, grad_value)):
            start = (index * HEADS + head) * HEAD_DIM
            mixed_ref[:, start : start + HEAD_DIM] = grad.astype(BF16)


def entry_backward_kernel(count, depth, *refs):
    place, x_ref, mixed_ref, grad_ref, gain_a = refs[:5]
    mix_refs = refs[5 : 5 + count]
    result_ref = refs[5 + count]
    mix_w, mix_sems = refs[6 + count :]
    chip, core = place[0], place[1]
    start_copies(mix_refs, mix_w, mix_sems, depth, chip, core)
    wait_copies(mix_refs, mix_w, mix_sems, depth, chip, core)
    grad_normed = dot(mixed_ref[...], mix_w[...], NT)
    x = x_ref[...].astype(F32)
    rms_one = lax.rsqrt(mean_last(x * x) + EPS)
    normal_one = x * rms_one
    grad_one = grad_normed * gain_a[...]
    result = grad_ref[...] + rms_one * (grad_one - normal_one * mean_last(grad_one * normal_one))
    result_ref[...] = result.astype(BF16)


def shaped(shape, kind):
    return jax.ShapeDtypeStruct(shape, kind)


def dma(count):
    return pltpu.SemaphoreType.DMA(count if isinstance(count, tuple) else (count,))


def call(kernel, outs, specs, out_specs, scratch, args):
    return pl.pallas_call(
        kernel,
        out_shape=outs,
        in_specs=specs,
        out_specs=out_specs,
        scratch_shapes=scratch,
        compiler_params=PARAMS,
    )(*args)


def dense_gates(routes, logits, expert_count):
    gates = jax.nn.sigmoid(logits)
    hit = routes[..., None] == jnp.arange(expert_count, dtype=jnp.int32)
    return jnp.sum(jnp.where(hit, gates[..., None], 0.0), axis=2)


def gate_columns(routes, logits, expert_count):
    gates = dense_gates(routes, logits, expert_count)
    high = lax.reduce_precision(gates, 8, 7)
    both = jnp.stack([high, gates - high], axis=1).astype(BF16)
    rows = jnp.transpose(both, (2, 0, 1, 3)).reshape(both.shape[2], -1)
    return jnp.pad(rows, ((0, 0), (0, LANES - rows.shape[1])))


def allowed_of(mask_blocks):
    frame_block = jnp.arange(FRAMES, dtype=jnp.int32) // BLOCK
    spread = (frame_block[:, None] == jnp.arange(FRAMES // BLOCK)[None, :]).astype(F32)
    eye = jnp.eye(FRAMES // BLOCK, dtype=F32)
    open_blocks = jnp.maximum((mask_blocks == 1).astype(F32), eye)
    return jnp.einsum("ib,mbc,jc->mij", spread, open_blocks, spread)


def local(
    handoff_forward,
    stashed_input,
    relay_cotangents,
    attention_gain,
    expert_gain,
    w_qkv,
    w_out,
    w_up,
    w_down,
    routes,
    gate_logits,
    block_mask,
):
    length = line_length()
    expert_count = lax.axis_size("expert")
    me = lax.axis_index("expert")
    place = jnp.stack([me // CORES, me % CORES]).astype(jnp.int32)
    tokens, width = handoff_forward.shape
    depth = w_qkv.shape[1]
    total = expert_count * tokens
    columns = w_qkv.shape[2]
    up_weight = jnp.swapaxes(w_up[0, 0], 0, 1)
    down_weight = w_down[0, 0]
    hidden_units = up_weight.shape[0]
    count = CORES * (2 * length - 1)

    mixers = with_partner(relayed(w_qkv[0]))
    outers = with_partner(relayed(w_out[0]))
    arriving = passed_along(handoff_forward, 1)
    cotangent = passed_along(relay_cotangents, -1)
    gates = gate_columns(routes, gate_logits, expert_count)
    cot_block = jnp.concatenate([cotangent, gates], axis=1)
    cots = spread(jnp.broadcast_to(cot_block[None], (length,) + cot_block.shape))
    mask = allowed_of(block_mask[:, 0])

    half = count // 2
    early_mix = mixers[: half - 2] + mixers[half : count - 2]
    last_mix = mixers[half - 2 : half] + mixers[count - 2 :]
    early = len(early_mix)
    sum_fwd, sum_bwd, normed, mask = call(
        functools.partial(early_kernel, early, depth),
        (
            shaped((tokens, columns), F32),
            shaped((tokens, columns), F32),
            shaped((2 * tokens, width), BF16),
            shaped(mask.shape, F32),
        ),
        [SMEM] + [VMEM] * 4 + [ANY] * early,
        (VMEM,) * 4,
        [pltpu.VMEM((width, columns), BF16), dma(expert_count)],
        [place, arriving, stashed_input, attention_gain, mask] + early_mix,
    )
    proj_fwd, proj_bwd, hidden_bwd, expert_bwd = call(
        functools.partial(project_kernel, count, depth, length),
        (
            shaped((tokens, columns), F32),
            shaped((tokens, columns), F32),
            shaped((tokens, width), F32),
            shaped((tokens, width), BF16),
        ),
        [SMEM] + [VMEM] * 6 + [ANY] * (4 + count),
        (VMEM,) * 4,
        [
            pltpu.VMEM((CORES * depth, columns), BF16),
            pltpu.VMEM((width, width), BF16),
            pltpu.VMEM((tokens, width), BF16),
            dma(4),
            dma(expert_count),
        ],
        [place, sum_fwd, sum_bwd, normed, stashed_input, expert_gain, mask] + last_mix + outers,
    )
    rows_bwd = with_partner(relayed(expert_bwd))

    hidden_fwd, expert_fwd = call(
        functools.partial(forward_kernel, count, depth),
        (shaped((tokens, width), F32), shaped((tokens, width), BF16)),
        [SMEM] + [VMEM] * 4 + [ANY] * count,
        (VMEM,) * 2,
        [pltpu.VMEM((width, width), BF16), pltpu.VMEM((tokens, width), BF16), dma(expert_count)],
        [place, arriving, proj_fwd, expert_gain, mask] + outers,
    )
    rows_fwd = with_partner(relayed(expert_fwd))

    grad_act, gate_fwd = call(
        functools.partial(cotangent_kernel, tokens, width, expert_count),
        (shaped((total, hidden_units), F32), shaped((total, LANES), F32)),
        [SMEM, VMEM] + [ANY] * 2,
        (VMEM,) * 2,
        [pltpu.VMEM((total, width + LANES), BF16), dma((CORES, length))],
        [place, down_weight] + cots,
    )

    pair = (shaped((length, tokens, width), BF16),) * 2

    def expert_scratch(sems):
        return [pltpu.VMEM((total, width), BF16), pltpu.VMEM((total, width), BF16), dma(sems)]

    mine, other = call(
        functools.partial(expert_backward_kernel, count, tokens),
        pair,
        [SMEM, VMEM, VMEM] + [ANY] * count,
        (VMEM,) * 2,
        expert_scratch(expert_count),
        [place, up_weight, grad_act] + rows_bwd,
    )
    grad_parts = across(mine + swapped(other))

    mine, other = call(
        functools.partial(expert_forward_kernel, count, tokens),
        pair,
        [SMEM, VMEM, VMEM, VMEM] + [ANY] * count,
        (VMEM,) * 2,
        expert_scratch(expert_count),
        [place, up_weight, down_weight, gate_fwd] + rows_fwd,
    )
    moe_parts = scattered(
        call(
            add_apart_kernel,
            (shaped((tokens, width), BF16),) * length,
            [SMEM] + [VMEM] * 2,
            (VMEM,) * length,
            [],
            [place, mine, swapped(other)],
        ),
    )

    grad_mixed, grad_hidden = call(
        functools.partial(heads_backward_kernel, count, depth),
        (shaped((tokens, columns), BF16), shaped((tokens, width), F32)),
        [SMEM] + [VMEM] * 6 + [ANY] * count,
        (VMEM,) * 2,
        [pltpu.VMEM((width, width), BF16), dma(expert_count)],
        [place, cotangent, hidden_bwd, proj_bwd, expert_gain, mask, grad_parts]
        + outers,
    )
    derivative = call(
        functools.partial(entry_backward_kernel, count, depth),
        shaped((tokens, width), BF16),
        [SMEM] + [VMEM] * 4 + [ANY] * count,
        VMEM,
        [
            pltpu.VMEM((width, columns), BF16),
            dma(expert_count),
        ],
        [place, stashed_input, grad_mixed, grad_hidden, attention_gain] + mixers,
    )

    layer_output = hidden_fwd
    for part in moe_parts:
        layer_output = layer_output + part.astype(F32)
    return (layer_output.astype(BF16), derivative)


def solution(mesh):
    placed = (
        P(("section", "expert"), None),
        P(("section", "expert"), None),
        P(("section", "expert"), None),
        P("section", None),
        P("section", None),
        P("section", "expert", None),
        P("section", "expert", None),
        P("section", "expert", None, None),
        P("section", "expert", None, None),
        P(None, ("section", "expert"), None),
        P(None, ("section", "expert"), None),
        P(None, ("section", "expert"), None, None),
    )

    return jax.shard_map(
        local,
        mesh=mesh,
        in_specs=placed,
        out_specs=(P(("section", "expert"), None), P(("section", "expert"), None)),
        check_vma=False,
    )
```

```python
import functools

import jax
import jax.numpy as jnp
from jax import lax
from jax.experimental import pallas as pl
from jax.experimental.pallas import tpu as pltpu
from jax.sharding import PartitionSpec as P


HEADS = 8
HEAD_DIM = 128
FRAMES = 128
BLOCK = 16
CORES = 2
LANES = 128

EPS = 1e-06
SCORE_SCALE = HEAD_DIM ** (-0.5)
GELU_C = 0.7978845608028654
GELU_A = 0.044715


F32 = jnp.float32
BF16 = jnp.bfloat16
NT = (((1,), (1,)), ((), ()))
TN = (((0,), (0,)), ((), ()))
ANY = pl.BlockSpec(memory_space=pl.ANY)
SMEM = pl.BlockSpec(memory_space=pltpu.SMEM)
VMEM = pl.BlockSpec(memory_space=pltpu.VMEM)
PARAMS = pltpu.CompilerParams(vmem_limit_bytes=56 * 1024 * 1024)


def dot(a, b, dims=(((1,), (0,)), ((), ()))):
    return lax.dot_general(a, b, dims, preferred_element_type=F32)


def mean_last(values):
    return jnp.mean(values, axis=-1, keepdims=True)


def passed_along(value, steps):
    count = lax.axis_size("section")
    pairs = [(source, (source + steps) % count) for source in range(count)]
    return lax.ppermute(value, "section", pairs)


def line_length():
    return lax.axis_size("expert") // CORES


def chip_pairs(sources, step):
    return [
        (CORES * chip + core, CORES * (chip + step) + core)
        for chip in sources
        for core in range(CORES)
    ]


def swapped(value):
    count = lax.axis_size("expert")
    return lax.ppermute(value, "expert", [(i, i ^ 1) for i in range(count)])


def hop(value, sources, move):
    return lax.ppermute(value, "expert", chip_pairs(sources, move))


def relayed(value):
    length = line_length()
    entries = [value]
    up = down = value
    for step in range(1, length):
        up = hop(up, range(step - 1, length - 1), 1)
        down = hop(down, range(1, length - step + 1), -1)
        entries += [up, down]
    return entries


def with_partner(entries):
    return entries + [swapped(block) for block in entries]


def scattered(blocks):
    length = line_length()
    up = down = None
    for step in range(1, length):
        far = length - step
        send_up, send_down = blocks[far], blocks[length - far]
        if up is not None:
            send_up = send_up + up
            send_down = send_down + down
        up = hop(send_up, range(0, step), 1)
        down = hop(send_down, range(length - step, length), -1)
    return [blocks[0], up, down]


def across(blocks):
    length = line_length()
    groups = [[CORES * chip + core for chip in range(length)] for core in range(CORES)]
    return lax.all_to_all(
        blocks, "expert", split_axis=0, concat_axis=0, axis_index_groups=groups, tiled=True
    )


def spread(copies):
    mine = across(copies)
    return [mine, swapped(mine)]


def entry_chips(hops, chip):
    length = line_length()
    listing = [(None, chip)]
    for hop in range(1, hops + 1):
        listing.append((chip - hop >= 0, chip - hop))
        listing.append((chip + hop < length, chip + hop))
    return listing


def each_copy(refs, target, sems, rows, chip, core, act):
    count = len(refs) // 2
    listing = entry_chips(count // 2, chip)
    for side in range(CORES):
        for index, (valid, origin) in enumerate(listing):
            number = side * count + index
            owner = CORES * origin + (core if side == 0 else 1 - core)

            def run(number=number, owner=owner):
                start = pl.multiple_of(owner * rows, rows)
                act(
                    pltpu.make_async_copy(
                        refs[number], target.at[pl.ds(start, rows), :], sems.at[owner]
                    )
                )

            if valid is None:
                run()
            else:
                pl.when(valid)(run)


def line_copies(refs, target, sems, rows, chip, core, act):
    for side, ref in enumerate(refs):
        for origin in range(ref.shape[0]):
            owner = CORES * origin + (core if side == 0 else 1 - core)
            start = pl.multiple_of(owner * rows, rows)
            act(
                pltpu.make_async_copy(
                    ref.at[origin], target.at[pl.ds(start, rows), :], sems.at[side, origin]
                )
            )


def fetch_line(*args):
    line_copies(*args, lambda copy: copy.start())
    line_copies(*args, lambda copy: copy.wait())


def start_copies(*args):
    each_copy(*args, lambda copy: copy.start())


def wait_copies(*args):
    each_copy(*args, lambda copy: copy.wait())


def head_parts(proj_ref, head):
    def part(index):
        start = (index * HEADS + head) * HEAD_DIM
        return proj_ref[:, start : start + HEAD_DIM]

    query, key, value = part(0), part(1), part(2)
    query_scale = lax.rsqrt(mean_last(query * query) + EPS)
    key_scale = lax.rsqrt(mean_last(key * key) + EPS)
    return query * query_scale, query_scale, key * key_scale, key_scale, value.astype(BF16)


def attn_probs_of(query_bf, key_bf, allowed):
    scores = dot(query_bf, key_bf, NT) * SCORE_SCALE
    expo = jnp.where(allowed, jnp.exp(scores), 0.0)
    return expo / jnp.sum(expo, axis=-1, keepdims=True)


def attend_rows(proj_ref, mask, heads_ref):
    allowed = mask > 0.5
    for head in range(HEADS):
        query_hat, _, key_hat, _, value_bf = head_parts(proj_ref, head)
        probs = attn_probs_of(query_hat.astype(BF16), key_hat.astype(BF16), allowed)
        out = dot(probs.astype(BF16), value_bf)
        heads_ref[:, head * HEAD_DIM : (head + 1) * HEAD_DIM] = out.astype(BF16)


def finish_rows(x, heads, out_w, gain_e, hidden_ref, expert_ref):
    hidden = x.astype(F32) + dot(heads, out_w)
    hidden_ref[...] = hidden
    rms = lax.rsqrt(mean_last(hidden * hidden) + EPS)
    expert_ref[...] = jnp.broadcast_to((hidden * rms * gain_e).astype(BF16), expert_ref.shape)


def early_kernel(count, depth, *refs):
    place, xf_ref, xb_ref, gain_a, mask_ref = refs[:5]
    mix_refs = refs[5 : 5 + count]
    sumf_ref, sumb_ref, normed_ref, allowed_ref = refs[5 + count : 9 + count]
    mix_w, mix_sems = refs[9 + count :]
    allowed_ref[...] = mask_ref[...]
    chip, core = place[0], place[1]
    mix_w[...] = jnp.zeros_like(mix_w)
    start_copies(mix_refs, mix_w, mix_sems, depth, chip, core)
    rows = xf_ref.shape[0]
    for index, x_ref in enumerate((xf_ref, xb_ref)):
        x = x_ref[...].astype(F32)
        rms = lax.rsqrt(mean_last(x * x) + EPS)
        normed_ref[index * rows : (index + 1) * rows, :] = (x * rms * gain_a[...]).astype(BF16)
    wait_copies(mix_refs, mix_w, mix_sems, depth, chip, core)
    columns = mix_w.shape[1]
    chunk = 512
    for begin in range(0, columns, chunk):
        piece = dot(normed_ref[...], mix_w[:, begin : begin + chunk])
        sumf_ref[:, begin : begin + chunk] = piece[:rows]
        sumb_ref[:, begin : begin + chunk] = piece[rows:]


def last_copies(mix_refs, mix_w, sems, depth, length, chip, core, act):
    for which, end in ((0, length - 1), (1, 0)):

        @pl.when(chip == end)
        def _():
            for side in range(CORES):
                start = pl.multiple_of((core if side == 0 else 1 - core) * depth, depth)
                act(
                    pltpu.make_async_copy(
                        mix_refs[2 * side + which],
                        mix_w.at[pl.ds(start, depth), :],
                        sems.at[2 * side + which],
                    )
                )


def project_kernel(count, depth, length, *refs):
    place, sumf_ref, sumb_ref, normed_ref, xb_ref, gain_e, mask_ref = refs[:7]
    mix_refs = refs[7:11]
    out_refs = refs[11 : 11 + count]
    projf_ref, projb_ref, hidden_ref, expert_ref = refs[11 + count : 15 + count]
    mix_w, out_w, heads, mix_sems, out_sems = refs[15 + count :]
    chip, core = place[0], place[1]
    last_copies(mix_refs, mix_w, mix_sems, depth, length, chip, core, lambda copy: copy.start())
    start_copies(out_refs, out_w, out_sems, depth, chip, core)
    last_copies(mix_refs, mix_w, mix_sems, depth, length, chip, core, lambda copy: copy.wait())
    rows = xb_ref.shape[0]
    columns = mix_w.shape[1]
    chunk = 512
    block = CORES * depth
    for end in (0, length - 1):

        @pl.when(chip == end)
        def _():
            far = (length - 1 - end) * block
            for begin in range(0, columns, chunk):
                span = slice(begin, begin + chunk)
                piece = dot(normed_ref[:, far : far + block], mix_w[:, span])
                projf_ref[:, span] = sumf_ref[:, span] + piece[:rows]
                projb_ref[:, span] = sumb_ref[:, span] + piece[rows:]

    @pl.when((chip > 0) & (chip < length - 1))
    def _():
        projf_ref[...] = sumf_ref[...]
        projb_ref[...] = sumb_ref[...]

    attend_rows(projb_ref, mask_ref[1], heads)
    wait_copies(out_refs, out_w, out_sems, depth, chip, core)
    finish_rows(xb_ref[...], heads[...], out_w[...], gain_e[...], hidden_ref, expert_ref)


def forward_kernel(count, depth, *refs):
    place, x_ref, proj_ref, gain_e, mask_ref = refs[:5]
    out_refs = refs[5 : 5 + count]
    hidden_ref, expert_ref = refs[5 + count : 7 + count]
    out_w, heads, out_sems = refs[7 + count :]
    chip, core = place[0], place[1]
    start_copies(out_refs, out_w, out_sems, depth, chip, core)
    attend_rows(proj_ref, mask_ref[0], heads)
    wait_copies(out_refs, out_w, out_sems, depth, chip, core)
    finish_rows(x_ref[...], heads[...], out_w[...], gain_e[...], hidden_ref, expert_ref)


def picked_gate(gates, me, expert_count, micro):
    lane = lax.broadcasted_iota(jnp.int32, gates.shape, 1)
    first = 2 * micro * expert_count + me
    hit = (lane == first) | (lane == first + expert_count)
    return jnp.sum(jnp.where(hit, gates, 0.0), axis=-1, keepdims=True)


def cotangent_kernel(rows, width, expert_count, *refs):
    place, down_ref, mine, other, act_ref, gate_ref, cot, sems = refs
    chip, core = place[0], place[1]
    me = CORES * chip + core
    fetch_line((mine, other), cot, sems, rows, chip, core)
    chunk = 2 * rows

    def step(index, carry):
        start = chunk_start(index, chunk)
        block = cot[pl.ds(start, chunk), :]
        gates = block[:, width:].astype(F32)
        grad_act = dot(block[:, :width], down_ref[...], NT)
        act_ref[pl.ds(start, chunk), :] = grad_act * picked_gate(gates, me, expert_count, 1)
        gate_ref[pl.ds(start, chunk), :] = jnp.broadcast_to(
            picked_gate(gates, me, expert_count, 0), (chunk, LANES)
        )
        return carry

    each_chunk(expert_count * rows // chunk, step)


def each_chunk(number, step):
    if number <= 4:
        for index in range(number):
            step(index, 0)
    else:
        lax.fori_loop(0, number, step, 0)


def chunk_start(index, chunk):
    return index * chunk if isinstance(index, int) else pl.multiple_of(index * chunk, chunk)


def give_back(result, mine_ref, other_ref, rows, core):
    for owner in range(mine_ref.shape[0]):
        for out_ref, side in ((mine_ref, core), (other_ref, 1 - core)):
            start = pl.multiple_of((CORES * owner + side) * rows, rows)
            out_ref[owner] = result[pl.ds(start, rows), :]


def expert_backward_kernel(rows, *refs):
    place, up_ref, act_ref = refs[:3]
    row_refs = refs[3:5]
    mine_ref, other_ref, tokens, result, sems = refs[5:]
    chip, core = place[0], place[1]
    fetch_line(row_refs, tokens, sems, rows, chip, core)
    chunk = 2 * rows

    def step(index, carry):
        start = chunk_start(index, chunk)
        pre = dot(tokens[pl.ds(start, chunk), :], up_ref[...], NT)
        square = pre * pre
        bend = jnp.tanh(GELU_C * pre * (1.0 + GELU_A * square))
        slope = 0.5 * (1.0 + bend) + 0.5 * pre * (1.0 - bend * bend) * (
            GELU_C * (1.0 + 3.0 * GELU_A * square)
        )
        grad = (act_ref[pl.ds(start, chunk), :] * slope).astype(BF16)
        result[pl.ds(start, chunk), :] = dot(grad, up_ref[...]).astype(BF16)
        return carry

    each_chunk(tokens.shape[0] // chunk, step)
    give_back(result, mine_ref, other_ref, rows, core)


def expert_forward_kernel(rows, *refs):
    place, up_ref, down_ref, gate_ref = refs[:4]
    row_refs = refs[4:6]
    mine_ref, other_ref, tokens, result, sems = refs[6:]
    chip, core = place[0], place[1]
    fetch_line(row_refs, tokens, sems, rows, chip, core)
    chunk = 2 * rows

    def step(index, carry):
        start = chunk_start(index, chunk)
        pre = dot(tokens[pl.ds(start, chunk), :], up_ref[...], NT)
        bend = jnp.tanh(GELU_C * pre * (1.0 + GELU_A * (pre * pre)))
        active = (0.5 * pre * (1.0 + bend)).astype(BF16)
        out = dot(active, down_ref[...])
        gate = gate_ref[pl.ds(start, chunk), :][:, :1]
        result[pl.ds(start, chunk), :] = (gate * out).astype(BF16)
        return carry

    each_chunk(tokens.shape[0] // chunk, step)
    give_back(result, mine_ref, other_ref, rows, core)


def add_apart_kernel(place, mine_ref, other_ref, *out_refs):
    for j, out_ref in enumerate(out_refs):
        owner = lax.rem(place[0] + j, len(out_refs))
        out_ref[...] = (mine_ref[owner].astype(F32) + other_ref[owner].astype(F32)).astype(BF16)


def heads_backward_kernel(count, depth, *refs):
    place, cot_ref, hidden_ref, proj_ref, gain_e, mask_ref, part_ref = refs[:7]
    out_refs = refs[7 : 7 + count]
    mixed_ref, grad_ref, out_w, out_sems = refs[7 + count :]
    chip, core = place[0], place[1]
    start_copies(out_refs, out_w, out_sems, depth, chip, core)
    grad_moe = part_ref[0].astype(F32)
    for index in range(1, part_ref.shape[0]):
        grad_moe = grad_moe + part_ref[index].astype(F32)
    hidden = hidden_ref[...]
    rms_two = lax.rsqrt(mean_last(hidden * hidden) + EPS)
    normal_two = hidden * rms_two
    grad_two = grad_moe * gain_e[...]
    grad_hidden = cot_ref[...].astype(F32) + rms_two * (
        grad_two - normal_two * mean_last(grad_two * normal_two)
    )
    grad_ref[...] = grad_hidden
    wait_copies(out_refs, out_w, out_sems, depth, chip, core)
    grad_heads = dot(grad_hidden.astype(BF16), out_w[...], NT).astype(BF16)
    allowed = mask_ref[1] > 0.5
    for head in range(HEADS):
        query_hat, query_scale, key_hat, key_scale, value_bf = head_parts(proj_ref, head)
        query_bf, key_bf = query_hat.astype(BF16), key_hat.astype(BF16)
        probs = attn_probs_of(query_bf, key_bf, allowed)
        grad_out = grad_heads[:, head * HEAD_DIM : (head + 1) * HEAD_DIM]
        grad_probs = dot(grad_out, value_bf, NT)
        grad_value = dot(probs.astype(BF16), grad_out, TN)
        inner = jnp.sum(probs * grad_probs, axis=-1, keepdims=True)
        grad_scores = (probs * (grad_probs - inner) * SCORE_SCALE).astype(BF16)
        grad_qhat = dot(grad_scores, key_bf)
        grad_khat = dot(grad_scores, query_bf, TN)
        grad_query = query_scale * (grad_qhat - query_hat * mean_last(grad_qhat * query_hat))
        grad_key = key_scale * (grad_khat - key_hat * mean_last(grad_khat * key_hat))
        for index, grad in enumerate((grad_query, grad_key, grad_value)):
            start = (index * HEADS + head) * HEAD_DIM
            mixed_ref[:, start : start + HEAD_DIM] = grad.astype(BF16)


def entry_backward_kernel(count, depth, *refs):
    place, x_ref, mixed_ref, grad_ref, gain_a = refs[:5]
    mix_refs = refs[5 : 5 + count]
    result_ref = refs[5 + count]
    mix_w, mix_sems = refs[6 + count :]
    chip, core = place[0], place[1]
    start_copies(mix_refs, mix_w, mix_sems, depth, chip, core)
    wait_copies(mix_refs, mix_w, mix_sems, depth, chip, core)
    grad_normed = dot(mixed_ref[...], mix_w[...], NT)
    x = x_ref[...].astype(F32)
    rms_one = lax.rsqrt(mean_last(x * x) + EPS)
    normal_one = x * rms_one
    grad_one = grad_normed * gain_a[...]
    result = grad_ref[...] + rms_one * (grad_one - normal_one * mean_last(grad_one * normal_one))
    result_ref[...] = result.astype(BF16)


def shaped(shape, kind):
    return jax.ShapeDtypeStruct(shape, kind)


def dma(count):
    return pltpu.SemaphoreType.DMA(count if isinstance(count, tuple) else (count,))


def call(kernel, outs, specs, out_specs, scratch, args):
    return pl.pallas_call(
        kernel,
        out_shape=outs,
        in_specs=specs,
        out_specs=out_specs,
        scratch_shapes=scratch,
        compiler_params=PARAMS,
    )(*args)


def dense_gates(routes, logits, expert_count):
    gates = jax.nn.sigmoid(logits)
    hit = routes[..., None] == jnp.arange(expert_count, dtype=jnp.int32)
    return jnp.sum(jnp.where(hit, gates[..., None], 0.0), axis=2)


def gate_columns(routes, logits, expert_count):
    gates = dense_gates(routes, logits, expert_count)
    high = lax.reduce_precision(gates, 8, 7)
    both = jnp.stack([high, gates - high], axis=1).astype(BF16)
    rows = jnp.transpose(both, (2, 0, 1, 3)).reshape(both.shape[2], -1)
    return jnp.pad(rows, ((0, 0), (0, LANES - rows.shape[1])))


def allowed_of(mask_blocks):
    frame_block = jnp.arange(FRAMES, dtype=jnp.int32) // BLOCK
    spread = (frame_block[:, None] == jnp.arange(FRAMES // BLOCK)[None, :]).astype(F32)
    eye = jnp.eye(FRAMES // BLOCK, dtype=F32)
    open_blocks = jnp.maximum((mask_blocks == 1).astype(F32), eye)
    return jnp.einsum("ib,mbc,jc->mij", spread, open_blocks, spread)


def local(
    handoff_forward,
    stashed_input,
    relay_cotangents,
    attention_gain,
    expert_gain,
    w_qkv,
    w_out,
    w_up,
    w_down,
    routes,
    gate_logits,
    block_mask,
):
    length = line_length()
    expert_count = lax.axis_size("expert")
    me = lax.axis_index("expert")
    place = jnp.stack([me // CORES, me % CORES]).astype(jnp.int32)
    tokens, width = handoff_forward.shape
    depth = w_qkv.shape[1]
    total = expert_count * tokens
    columns = w_qkv.shape[2]
    up_weight = jnp.swapaxes(w_up[0, 0], 0, 1)
    down_weight = w_down[0, 0]
    hidden_units = up_weight.shape[0]
    count = CORES * (2 * length - 1)

    mixers = with_partner(relayed(w_qkv[0]))
    outers = with_partner(relayed(w_out[0]))
    arriving = passed_along(handoff_forward, 1)
    cotangent = passed_along(relay_cotangents, -1)
    gates = gate_columns(routes, gate_logits, expert_count)
    cot_block = jnp.concatenate([cotangent, gates], axis=1)
    cots = spread(jnp.broadcast_to(cot_block[None], (length,) + cot_block.shape))
    mask = allowed_of(block_mask[:, 0])

    half = count // 2
    early_mix = mixers[: half - 2] + mixers[half : count - 2]
    last_mix = mixers[half - 2 : half] + mixers[count - 2 :]
    early = len(early_mix)
    sum_fwd, sum_bwd, normed, mask = call(
        functools.partial(early_kernel, early, depth),
        (
            shaped((tokens, columns), F32),
            shaped((tokens, columns), F32),
            shaped((2 * tokens, width), BF16),
            shaped(mask.shape, F32),
        ),
        [SMEM] + [VMEM] * 4 + [ANY] * early,
        (VMEM,) * 4,
        [pltpu.VMEM((width, columns), BF16), dma(expert_count)],
        [place, arriving, stashed_input, attention_gain, mask] + early_mix,
    )
    proj_fwd, proj_bwd, hidden_bwd, expert_bwd = call(
        functools.partial(project_kernel, count, depth, length),
        (
            shaped((tokens, columns), F32),
            shaped((tokens, columns), F32),
            shaped((tokens, width), F32),
            shaped((length, tokens, width), BF16),
        ),
        [SMEM] + [VMEM] * 6 + [ANY] * (4 + count),
        (VMEM,) * 4,
        [
            pltpu.VMEM((CORES * depth, columns), BF16),
            pltpu.VMEM((width, width), BF16),
            pltpu.VMEM((tokens, width), BF16),
            dma(4),
            dma(expert_count),
        ],
        [place, sum_fwd, sum_bwd, normed, stashed_input, expert_gain, mask] + last_mix + outers,
    )
    rows_bwd = spread(expert_bwd)

    hidden_fwd, expert_fwd = call(
        functools.partial(forward_kernel, count, depth),
        (shaped((tokens, width), F32), shaped((length, tokens, width), BF16)),
        [SMEM] + [VMEM] * 4 + [ANY] * count,
        (VMEM,) * 2,
        [pltpu.VMEM((width, width), BF16), pltpu.VMEM((tokens, width), BF16), dma(expert_count)],
        [place, arriving, proj_fwd, expert_gain, mask] + outers,
    )
    rows_fwd = spread(expert_fwd)

    grad_act, gate_fwd = call(
        functools.partial(cotangent_kernel, tokens, width, expert_count),
        (shaped((total, hidden_units), F32), shaped((total, LANES), F32)),
        [SMEM, VMEM] + [ANY] * 2,
        (VMEM,) * 2,
        [pltpu.VMEM((total, width + LANES), BF16), dma((CORES, length))],
        [place, down_weight] + cots,
    )

    pair = (shaped((length, tokens, width), BF16),) * 2

    def expert_scratch(sems):
        return [pltpu.VMEM((total, width), BF16), pltpu.VMEM((total, width), BF16), dma(sems)]

    mine, other = call(
        functools.partial(expert_backward_kernel, tokens),
        pair,
        [SMEM, VMEM, VMEM] + [ANY] * 2,
        (VMEM,) * 2,
        expert_scratch((CORES, length)),
        [place, up_weight, grad_act] + rows_bwd,
    )
    grad_parts = across(mine + swapped(other))

    mine, other = call(
        functools.partial(expert_forward_kernel, tokens),
        pair,
        [SMEM, VMEM, VMEM, VMEM] + [ANY] * 2,
        (VMEM,) * 2,
        expert_scratch((CORES, length)),
        [place, up_weight, down_weight, gate_fwd] + rows_fwd,
    )
    moe_parts = scattered(
        call(
            add_apart_kernel,
            (shaped((tokens, width), BF16),) * length,
            [SMEM] + [VMEM] * 2,
            (VMEM,) * length,
            [],
            [place, mine, swapped(other)],
        ),
    )

    grad_mixed, grad_hidden = call(
        functools.partial(heads_backward_kernel, count, depth),
        (shaped((tokens, columns), BF16), shaped((tokens, width), F32)),
        [SMEM] + [VMEM] * 6 + [ANY] * count,
        (VMEM,) * 2,
        [pltpu.VMEM((width, width), BF16), dma(expert_count)],
        [place, cotangent, hidden_bwd, proj_bwd, expert_gain, mask, grad_parts]
        + outers,
    )
    derivative = call(
        functools.partial(entry_backward_kernel, count, depth),
        shaped((tokens, width), BF16),
        [SMEM] + [VMEM] * 4 + [ANY] * count,
        VMEM,
        [
            pltpu.VMEM((width, columns), BF16),
            dma(expert_count),
        ],
        [place, stashed_input, grad_mixed, grad_hidden, attention_gain] + mixers,
    )

    layer_output = hidden_fwd
    for part in moe_parts:
        layer_output = layer_output + part.astype(F32)
    return (layer_output.astype(BF16), derivative)


def solution(mesh):
    placed = (
        P(("section", "expert"), None),
        P(("section", "expert"), None),
        P(("section", "expert"), None),
        P("section", None),
        P("section", None),
        P("section", "expert", None),
        P("section", "expert", None),
        P("section", "expert", None, None),
        P("section", "expert", None, None),
        P(None, ("section", "expert"), None),
        P(None, ("section", "expert"), None),
        P(None, ("section", "expert"), None, None),
    )

    return jax.shard_map(
        local,
        mesh=mesh,
        in_specs=placed,
        out_specs=(P(("section", "expert"), None), P(("section", "expert"), None)),
        check_vma=False,
    )
```

```python
import functools

import jax
import jax.numpy as jnp
from jax import lax
from jax.experimental import pallas as pl
from jax.experimental.pallas import tpu as pltpu
from jax.sharding import PartitionSpec as P


HEADS = 8
HEAD_DIM = 128
FRAMES = 128
BLOCK = 16
CORES = 2
LANES = 128

EPS = 1e-06
SCORE_SCALE = HEAD_DIM ** (-0.5)
GELU_C = 0.7978845608028654
GELU_A = 0.044715


F32 = jnp.float32
BF16 = jnp.bfloat16
NT = (((1,), (1,)), ((), ()))
TN = (((0,), (0,)), ((), ()))
ANY = pl.BlockSpec(memory_space=pltpu.HBM)
SMEM = pl.BlockSpec(memory_space=pltpu.SMEM)
VMEM = pl.BlockSpec(memory_space=pltpu.VMEM)
PARAMS = pltpu.CompilerParams(vmem_limit_bytes=56 * 1024 * 1024)


def dot(a, b, dims=(((1,), (0,)), ((), ()))):
    return lax.dot_general(a, b, dims, preferred_element_type=F32)


def mean_last(values):
    return jnp.mean(values, axis=-1, keepdims=True)


def passed_along(value, steps):
    count = lax.axis_size("section")
    pairs = [(source, (source + steps) % count) for source in range(count)]
    return lax.ppermute(value, "section", pairs)


def line_length():
    return lax.axis_size("expert") // CORES


def chip_pairs(sources, step):
    return [
        (CORES * chip + core, CORES * (chip + step) + core)
        for chip in sources
        for core in range(CORES)
    ]


def swapped(value):
    count = lax.axis_size("expert")
    return lax.ppermute(value, "expert", [(i, i ^ 1) for i in range(count)])


def hop(value, sources, move):
    return lax.ppermute(value, "expert", chip_pairs(sources, move))


def relayed(value):
    length = line_length()
    entries = [value]
    up = down = value
    for step in range(1, length):
        up = hop(up, range(step - 1, length - 1), 1)
        down = hop(down, range(1, length - step + 1), -1)
        entries += [up, down]
    return entries


def with_partner(entries):
    return entries + [swapped(block) for block in entries]


def across(blocks):
    length = line_length()
    groups = [[CORES * chip + core for chip in range(length)] for core in range(CORES)]
    return lax.all_to_all(
        blocks, "expert", split_axis=0, concat_axis=0, axis_index_groups=groups, tiled=True
    )


def spread(copies):
    mine = across(copies)
    return [mine, swapped(mine)]


def entry_chips(hops, chip):
    length = line_length()
    listing = [(None, chip)]
    for hop in range(1, hops + 1):
        listing.append((chip - hop >= 0, chip - hop))
        listing.append((chip + hop < length, chip + hop))
    return listing


def each_copy(refs, target, sems, rows, chip, core, act):
    count = len(refs) // 2
    listing = entry_chips(count // 2, chip)
    for side in range(CORES):
        for index, (valid, origin) in enumerate(listing):
            number = side * count + index
            owner = CORES * origin + (core if side == 0 else 1 - core)

            def run(number=number, owner=owner):
                start = pl.multiple_of(owner * rows, rows)
                act(
                    pltpu.make_async_copy(
                        refs[number], target.at[pl.ds(start, rows), :], sems.at[owner]
                    )
                )

            if valid is None:
                run()
            else:
                pl.when(valid)(run)


def line_copies(refs, target, sems, rows, chip, core, act):
    for side, ref in enumerate(refs):
        for origin in range(ref.shape[0]):
            owner = CORES * origin + (core if side == 0 else 1 - core)
            start = pl.multiple_of(owner * rows, rows)
            act(
                pltpu.make_async_copy(
                    ref.at[origin], target.at[pl.ds(start, rows), :], sems.at[side, origin]
                )
            )


def fetch_line(*args):
    line_copies(*args, lambda copy: copy.start())
    line_copies(*args, lambda copy: copy.wait())


def start_copies(*args):
    each_copy(*args, lambda copy: copy.start())


def wait_copies(*args):
    each_copy(*args, lambda copy: copy.wait())


def head_parts(proj_ref, head):
    def part(index):
        start = (index * HEADS + head) * HEAD_DIM
        return proj_ref[:, start : start + HEAD_DIM]

    query, key, value = part(0), part(1), part(2)
    query_scale = lax.rsqrt(mean_last(query * query) + EPS)
    key_scale = lax.rsqrt(mean_last(key * key) + EPS)
    return query * query_scale, query_scale, key * key_scale, key_scale, value.astype(BF16)


def attn_probs_of(query_bf, key_bf, allowed):
    scores = dot(query_bf, key_bf, NT) * SCORE_SCALE
    expo = jnp.where(allowed, jnp.exp(scores), 0.0)
    return expo / jnp.sum(expo, axis=-1, keepdims=True)


def attend_rows(proj_ref, mask, heads_ref):
    allowed = mask > 0.5
    for head in range(HEADS):
        query_hat, _, key_hat, _, value_bf = head_parts(proj_ref, head)
        probs = attn_probs_of(query_hat.astype(BF16), key_hat.astype(BF16), allowed)
        out = dot(probs.astype(BF16), value_bf)
        heads_ref[:, head * HEAD_DIM : (head + 1) * HEAD_DIM] = out.astype(BF16)


def finish_rows(x, heads, out_w, gain_e, hidden_ref, expert_ref):
    hidden = x.astype(F32) + dot(heads, out_w)
    hidden_ref[...] = hidden
    rms = lax.rsqrt(mean_last(hidden * hidden) + EPS)
    expert_ref[...] = jnp.broadcast_to((hidden * rms * gain_e).astype(BF16), expert_ref.shape)


def early_kernel(count, depth, *refs):
    place, xf_ref, xb_ref, gain_a, mask_ref = refs[:5]
    mix_refs = refs[5 : 5 + count]
    sumf_ref, sumb_ref, normedf_ref, normedb_ref, allowed_ref = refs[5 + count : 10 + count]
    mix_w, normed, mix_sems = refs[10 + count :]
    allowed_ref[...] = mask_ref[...]
    chip, core = place[0], place[1]
    mix_w[...] = jnp.zeros_like(mix_w)
    start_copies(mix_refs, mix_w, mix_sems, depth, chip, core)
    rows = xf_ref.shape[0]
    for index, x_ref in enumerate((xf_ref, xb_ref)):
        x = x_ref[...].astype(F32)
        rms = lax.rsqrt(mean_last(x * x) + EPS)
        normed[index * rows : (index + 1) * rows, :] = (x * rms * gain_a[...]).astype(BF16)
    normedf_ref[...] = normed[:rows, :]
    normedb_ref[...] = normed[rows:, :]
    wait_copies(mix_refs, mix_w, mix_sems, depth, chip, core)
    columns = mix_w.shape[1]
    chunk = 512
    for begin in range(0, columns, chunk):
        piece = dot(normed[...], mix_w[:, begin : begin + chunk])
        sumf_ref[:, begin : begin + chunk] = piece[:rows]
        sumb_ref[:, begin : begin + chunk] = piece[rows:]


def last_copies(mix_refs, mix_w, sems, depth, length, chip, core, act):
    for which, end in ((0, length - 1), (1, 0)):

        @pl.when(chip == end)
        def _():
            for side in range(CORES):
                start = pl.multiple_of((core if side == 0 else 1 - core) * depth, depth)
                act(
                    pltpu.make_async_copy(
                        mix_refs[2 * side + which],
                        mix_w.at[pl.ds(start, depth), :],
                        sems.at[2 * side + which],
                    )
                )


def add_last(sum_ref, normed_ref, mix_w, proj_ref, chip, length):
    columns = mix_w.shape[1]
    block = mix_w.shape[0]
    chunk = 512
    for end in (0, length - 1):

        @pl.when(chip == end)
        def _():
            far = (length - 1 - end) * block
            for begin in range(0, columns, chunk):
                span = slice(begin, begin + chunk)
                piece = dot(normed_ref[:, far : far + block], mix_w[:, span])
                proj_ref[:, span] = sum_ref[:, span] + piece

    @pl.when((chip > 0) & (chip < length - 1))
    def _():
        proj_ref[...] = sum_ref[...]


def project_kernel(count, depth, length, micro, *refs):
    place, x_ref, sum_ref, normed_ref, gain_e, mask_ref = refs[:6]
    mix_refs = refs[6:10]
    out_refs = refs[10 : 10 + count]
    proj_ref, hidden_ref, expert_ref = refs[10 + count : 13 + count]
    mix_w, out_w, heads, mix_sems, out_sems = refs[13 + count :]
    chip, core = place[0], place[1]
    last_copies(mix_refs, mix_w, mix_sems, depth, length, chip, core, lambda copy: copy.start())
    start_copies(out_refs, out_w, out_sems, depth, chip, core)
    last_copies(mix_refs, mix_w, mix_sems, depth, length, chip, core, lambda copy: copy.wait())
    add_last(sum_ref, normed_ref, mix_w, proj_ref, chip, length)
    attend_rows(proj_ref, mask_ref[micro], heads)
    wait_copies(out_refs, out_w, out_sems, depth, chip, core)
    finish_rows(x_ref[...], heads[...], out_w[...], gain_e[...], hidden_ref, expert_ref)


def picked_gate(gates, me, expert_count, micro):
    lane = lax.broadcasted_iota(jnp.int32, gates.shape, 1)
    first = 2 * micro * expert_count + me
    hit = (lane == first) | (lane == first + expert_count)
    return jnp.sum(jnp.where(hit, gates, 0.0), axis=-1, keepdims=True)


def cotangent_kernel(rows, width, expert_count, *refs):
    place, down_ref, mine, other, act_ref, gate_ref, cot, sems = refs
    chip, core = place[0], place[1]
    me = CORES * chip + core
    fetch_line((mine, other), cot, sems, rows, chip, core)
    chunk = 2 * rows

    def step(index, carry):
        start = chunk_start(index, chunk)
        block = cot[pl.ds(start, chunk), :]
        gates = block[:, width:].astype(F32)
        grad_act = dot(block[:, :width], down_ref[...], NT)
        act_ref[pl.ds(start, chunk), :] = grad_act * picked_gate(gates, me, expert_count, 1)
        gate_ref[pl.ds(start, chunk), :] = jnp.broadcast_to(
            picked_gate(gates, me, expert_count, 0), (chunk, LANES)
        )
        return carry

    each_chunk(expert_count * rows // chunk, step)


def each_chunk(number, step):
    if number <= 4:
        for index in range(number):
            step(index, 0)
    else:
        lax.fori_loop(0, number, step, 0)


def chunk_start(index, chunk):
    return index * chunk if isinstance(index, int) else pl.multiple_of(index * chunk, chunk)


def give_back(result, mine_ref, other_ref, rows, core):
    for owner in range(mine_ref.shape[0]):
        for out_ref, side in ((mine_ref, core), (other_ref, 1 - core)):
            start = pl.multiple_of((CORES * owner + side) * rows, rows)
            out_ref[owner] = result[pl.ds(start, rows), :]


def expert_backward_kernel(count, rows, *refs):
    place, up_ref, act_ref = refs[:3]
    row_refs = refs[3 : 3 + count]
    mine_ref, other_ref, tokens, result, sems = refs[3 + count :]
    chip, core = place[0], place[1]
    start_copies(row_refs, tokens, sems, rows, chip, core)
    wait_copies(row_refs, tokens, sems, rows, chip, core)
    chunk = 2 * rows

    def step(index, carry):
        start = chunk_start(index, chunk)
        pre = dot(tokens[pl.ds(start, chunk), :], up_ref[...], NT)
        square = pre * pre
        bend = jnp.tanh(GELU_C * pre * (1.0 + GELU_A * square))
        slope = 0.5 * (1.0 + bend) + 0.5 * pre * (1.0 - bend * bend) * (
            GELU_C * (1.0 + 3.0 * GELU_A * square)
        )
        grad = (act_ref[pl.ds(start, chunk), :] * slope).astype(BF16)
        result[pl.ds(start, chunk), :] = dot(grad, up_ref[...]).astype(BF16)
        return carry

    each_chunk(tokens.shape[0] // chunk, step)
    give_back(result, mine_ref, other_ref, rows, core)


def expert_forward_kernel(rows, *refs):
    place, up_ref, down_ref, gate_ref = refs[:4]
    row_refs = refs[4:6]
    mine_ref, other_ref, tokens, result, sems = refs[6:]
    chip, core = place[0], place[1]
    fetch_line(row_refs, tokens, sems, rows, chip, core)
    chunk = 2 * rows

    def step(index, carry):
        start = chunk_start(index, chunk)
        pre = dot(tokens[pl.ds(start, chunk), :], up_ref[...], NT)
        bend = jnp.tanh(GELU_C * pre * (1.0 + GELU_A * (pre * pre)))
        active = (0.5 * pre * (1.0 + bend)).astype(BF16)
        out = dot(active, down_ref[...])
        gate = gate_ref[pl.ds(start, chunk), :][:, :1]
        result[pl.ds(start, chunk), :] = (gate * out).astype(BF16)
        return carry

    each_chunk(tokens.shape[0] // chunk, step)
    give_back(result, mine_ref, other_ref, rows, core)


def heads_backward_kernel(count, depth, *refs):
    place, cot_ref, hidden_ref, proj_ref, gain_e, mask_ref, part_ref = refs[:7]
    out_refs = refs[7 : 7 + count]
    mixed_ref, grad_ref, out_w, out_sems = refs[7 + count :]
    chip, core = place[0], place[1]
    start_copies(out_refs, out_w, out_sems, depth, chip, core)
    grad_moe = part_ref[0].astype(F32)
    for index in range(1, part_ref.shape[0]):
        grad_moe = grad_moe + part_ref[index].astype(F32)
    hidden = hidden_ref[...]
    rms_two = lax.rsqrt(mean_last(hidden * hidden) + EPS)
    normal_two = hidden * rms_two
    grad_two = grad_moe * gain_e[...]
    grad_hidden = cot_ref[...].astype(F32) + rms_two * (
        grad_two - normal_two * mean_last(grad_two * normal_two)
    )
    grad_ref[...] = grad_hidden
    wait_copies(out_refs, out_w, out_sems, depth, chip, core)
    grad_heads = dot(grad_hidden.astype(BF16), out_w[...], NT).astype(BF16)
    allowed = mask_ref[1] > 0.5
    for head in range(HEADS):
        query_hat, query_scale, key_hat, key_scale, value_bf = head_parts(proj_ref, head)
        query_bf, key_bf = query_hat.astype(BF16), key_hat.astype(BF16)
        probs = attn_probs_of(query_bf, key_bf, allowed)
        grad_out = grad_heads[:, head * HEAD_DIM : (head + 1) * HEAD_DIM]
        grad_probs = dot(grad_out, value_bf, NT)
        grad_value = dot(probs.astype(BF16), grad_out, TN)
        inner = jnp.sum(probs * grad_probs, axis=-1, keepdims=True)
        grad_scores = (probs * (grad_probs - inner) * SCORE_SCALE).astype(BF16)
        grad_qhat = dot(grad_scores, key_bf)
        grad_khat = dot(grad_scores, query_bf, TN)
        grad_query = query_scale * (grad_qhat - query_hat * mean_last(grad_qhat * query_hat))
        grad_key = key_scale * (grad_khat - key_hat * mean_last(grad_khat * key_hat))
        for index, grad in enumerate((grad_query, grad_key, grad_value)):
            start = (index * HEADS + head) * HEAD_DIM
            mixed_ref[:, start : start + HEAD_DIM] = grad.astype(BF16)


def entry_backward_kernel(count, depth, *refs):
    place, x_ref, mixed_ref, grad_ref, gain_a = refs[:5]
    mix_refs = refs[5 : 5 + count]
    result_ref = refs[5 + count]
    mix_w, mix_sems = refs[6 + count :]
    chip, core = place[0], place[1]
    start_copies(mix_refs, mix_w, mix_sems, depth, chip, core)
    wait_copies(mix_refs, mix_w, mix_sems, depth, chip, core)
    grad_normed = dot(mixed_ref[...], mix_w[...], NT)
    x = x_ref[...].astype(F32)
    rms_one = lax.rsqrt(mean_last(x * x) + EPS)
    normal_one = x * rms_one
    grad_one = grad_normed * gain_a[...]
    result = grad_ref[...] + rms_one * (grad_one - normal_one * mean_last(grad_one * normal_one))
    result_ref[...] = result.astype(BF16)


def shaped(shape, kind):
    return jax.ShapeDtypeStruct(shape, kind)


def dma(count):
    return pltpu.SemaphoreType.DMA(count if isinstance(count, tuple) else (count,))


def call(kernel, outs, specs, out_specs, scratch, args):
    return pl.pallas_call(
        kernel,
        out_shape=outs,
        in_specs=specs,
        out_specs=out_specs,
        scratch_shapes=scratch,
        compiler_params=PARAMS,
    )(*args)


def dense_gates(routes, logits, expert_count):
    gates = jax.nn.sigmoid(logits)
    hit = routes[..., None] == jnp.arange(expert_count, dtype=jnp.int32)
    return jnp.sum(jnp.where(hit, gates[..., None], 0.0), axis=2)


def gate_columns(routes, logits, expert_count):
    gates = dense_gates(routes, logits, expert_count)
    high = lax.reduce_precision(gates, 8, 7)
    both = jnp.stack([high, gates - high], axis=1).astype(BF16)
    rows = jnp.transpose(both, (2, 0, 1, 3)).reshape(both.shape[2], -1)
    return jnp.pad(rows, ((0, 0), (0, LANES - rows.shape[1])))


def allowed_of(mask_blocks):
    frame_block = jnp.arange(FRAMES, dtype=jnp.int32) // BLOCK
    spread = (frame_block[:, None] == jnp.arange(FRAMES // BLOCK)[None, :]).astype(F32)
    eye = jnp.eye(FRAMES // BLOCK, dtype=F32)
    open_blocks = jnp.maximum((mask_blocks == 1).astype(F32), eye)
    return jnp.einsum("ib,mbc,jc->mij", spread, open_blocks, spread)


def local(
    handoff_forward,
    stashed_input,
    relay_cotangents,
    attention_gain,
    expert_gain,
    w_qkv,
    w_out,
    w_up,
    w_down,
    routes,
    gate_logits,
    block_mask,
):
    length = line_length()
    expert_count = lax.axis_size("expert")
    me = lax.axis_index("expert")
    place = jnp.stack([me // CORES, me % CORES]).astype(jnp.int32)
    tokens, width = handoff_forward.shape
    depth = w_qkv.shape[1]
    total = expert_count * tokens
    columns = w_qkv.shape[2]
    up_weight = jnp.swapaxes(w_up[0, 0], 0, 1)
    down_weight = w_down[0, 0]
    hidden_units = up_weight.shape[0]
    count = CORES * (2 * length - 1)

    mixers = with_partner(relayed(w_qkv[0]))
    outers = with_partner(relayed(w_out[0]))
    arriving = passed_along(handoff_forward, 1)
    cotangent = passed_along(relay_cotangents, -1)
    gates = gate_columns(routes, gate_logits, expert_count)
    cot_block = jnp.concatenate([cotangent, gates], axis=1)
    cots = spread(jnp.broadcast_to(cot_block[None], (length,) + cot_block.shape))
    mask = allowed_of(block_mask[:, 0])

    half = count // 2
    early_mix = mixers[: half - 2] + mixers[half : count - 2]
    last_mix = mixers[half - 2 : half] + mixers[count - 2 :]
    early = len(early_mix)
    sum_fwd, sum_bwd, normed_fwd, normed_bwd, mask = call(
        functools.partial(early_kernel, early, depth),
        (
            shaped((tokens, columns), F32),
            shaped((tokens, columns), F32),
            shaped((tokens, width), BF16),
            shaped((tokens, width), BF16),
            shaped(mask.shape, F32),
        ),
        [SMEM] + [VMEM] * 4 + [ANY] * early,
        (VMEM,) * 5,
        [
            pltpu.VMEM((width, columns), BF16),
            pltpu.VMEM((2 * tokens, width), BF16),
            dma(expert_count),
        ],
        [place, arriving, stashed_input, attention_gain, mask] + early_mix,
    )

    def attended(micro, x, sums, normed, block):
        return call(
            functools.partial(project_kernel, count, depth, length, micro),
            (
                shaped((tokens, columns), F32),
                shaped((tokens, width), F32),
                shaped(block, BF16),
            ),
            [SMEM] + [VMEM] * 5 + [ANY] * (4 + count),
            (VMEM,) * 3,
            [
                pltpu.VMEM((CORES * depth, columns), BF16),
                pltpu.VMEM((width, width), BF16),
                pltpu.VMEM((tokens, width), BF16),
                dma(4),
                dma(expert_count),
            ],
            [place, x, sums, normed, expert_gain, mask] + last_mix + outers,
        )

    proj_bwd, hidden_bwd, expert_bwd = attended(
        1, stashed_input, sum_bwd, normed_bwd, (tokens, width)
    )
    rows_bwd = with_partner(relayed(expert_bwd))

    _, hidden_fwd, expert_fwd = attended(0, arriving, sum_fwd, normed_fwd, (length, tokens, width))
    rows_fwd = spread(expert_fwd)

    grad_act, gate_fwd = call(
        functools.partial(cotangent_kernel, tokens, width, expert_count),
        (shaped((total, hidden_units), F32), shaped((total, LANES), F32)),
        [SMEM, VMEM] + [ANY] * 2,
        (VMEM,) * 2,
        [pltpu.VMEM((total, width + LANES), BF16), dma((CORES, length))],
        [place, down_weight] + cots,
    )

    pair = (shaped((length, tokens, width), BF16),) * 2

    def expert_scratch(sems):
        return [pltpu.VMEM((total, width), BF16), pltpu.VMEM((total, width), BF16), dma(sems)]

    mine, other = call(
        functools.partial(expert_backward_kernel, count, tokens),
        pair,
        [SMEM, VMEM, VMEM] + [ANY] * count,
        (VMEM,) * 2,
        expert_scratch(expert_count),
        [place, up_weight, grad_act] + rows_bwd,
    )
    grad_parts = across(mine + swapped(other))

    mine, other = call(
        functools.partial(expert_forward_kernel, tokens),
        pair,
        [SMEM, VMEM, VMEM, VMEM] + [ANY] * 2,
        (VMEM,) * 2,
        expert_scratch((CORES, length)),
        [place, up_weight, down_weight, gate_fwd] + rows_fwd,
    )
    moe_parts = across(mine + swapped(other))

    grad_mixed, grad_hidden = call(
        functools.partial(heads_backward_kernel, count, depth),
        (shaped((tokens, columns), BF16), shaped((tokens, width), F32)),
        [SMEM] + [VMEM] * 6 + [ANY] * count,
        (VMEM,) * 2,
        [pltpu.VMEM((width, width), BF16), dma(expert_count)],
        [place, cotangent, hidden_bwd, proj_bwd, expert_gain, mask, grad_parts]
        + outers,
    )
    derivative = call(
        functools.partial(entry_backward_kernel, count, depth),
        shaped((tokens, width), BF16),
        [SMEM] + [VMEM] * 4 + [ANY] * count,
        VMEM,
        [
            pltpu.VMEM((width, columns), BF16),
            dma(expert_count),
        ],
        [place, stashed_input, grad_mixed, grad_hidden, attention_gain] + mixers,
    )

    layer_output = hidden_fwd + jnp.sum(moe_parts.astype(F32), axis=0)
    return (layer_output.astype(BF16), derivative)


def solution(mesh):
    placed = (
        P(("section", "expert"), None),
        P(("section", "expert"), None),
        P(("section", "expert"), None),
        P("section", None),
        P("section", None),
        P("section", "expert", None),
        P("section", "expert", None),
        P("section", "expert", None, None),
        P("section", "expert", None, None),
        P(None, ("section", "expert"), None),
        P(None, ("section", "expert"), None),
        P(None, ("section", "expert"), None, None),
    )

    return jax.shard_map(
        local,
        mesh=mesh,
        in_specs=placed,
        out_specs=(P(("section", "expert"), None), P(("section", "expert"), None)),
        check_vma=False,
    )
```

```python
import functools

import jax
import jax.numpy as jnp
from jax import lax
from jax.experimental import pallas as pl
from jax.experimental.pallas import tpu as pltpu
from jax.sharding import PartitionSpec as P


HEADS = 8
HEAD_DIM = 128
FRAMES = 128
BLOCK = 16
CORES = 2
LANES = 128

EPS = 1e-06
SCORE_SCALE = HEAD_DIM ** (-0.5)
GELU_C = 0.7978845608028654
GELU_A = 0.044715


F32 = jnp.float32
BF16 = jnp.bfloat16
NT = (((1,), (1,)), ((), ()))
TN = (((0,), (0,)), ((), ()))
ANY = pl.BlockSpec(memory_space=pltpu.HBM)
SMEM = pl.BlockSpec(memory_space=pltpu.SMEM)
VMEM = pl.BlockSpec(memory_space=pltpu.VMEM)
PARAMS = pltpu.CompilerParams(vmem_limit_bytes=56 * 1024 * 1024)


def dot(a, b, dims=(((1,), (0,)), ((), ()))):
    return lax.dot_general(a, b, dims, preferred_element_type=F32)


def mean_last(values):
    return jnp.mean(values, axis=-1, keepdims=True)


def passed_along(value, steps):
    count = lax.axis_size("section")
    pairs = [(source, (source + steps) % count) for source in range(count)]
    return lax.ppermute(value, "section", pairs)


def line_length():
    return lax.axis_size("expert") // CORES


def chip_pairs(sources, step):
    return [
        (CORES * chip + core, CORES * (chip + step) + core)
        for chip in sources
        for core in range(CORES)
    ]


def swapped(value):
    count = lax.axis_size("expert")
    return lax.ppermute(value, "expert", [(i, i ^ 1) for i in range(count)])


def hop(value, sources, move):
    return lax.ppermute(value, "expert", chip_pairs(sources, move))


def relayed(value):
    length = line_length()
    entries = [value]
    up = down = value
    for step in range(1, length):
        up = hop(up, range(step - 1, length - 1), 1)
        down = hop(down, range(1, length - step + 1), -1)
        entries += [up, down]
    return entries


def with_partner(entries):
    return entries + [swapped(block) for block in entries]


def across(blocks):
    length = line_length()
    groups = [[CORES * chip + core for chip in range(length)] for core in range(CORES)]
    return lax.all_to_all(
        blocks, "expert", split_axis=0, concat_axis=0, axis_index_groups=groups, tiled=True
    )


def spread(copies):
    mine = across(copies)
    return [mine, swapped(mine)]


def entry_chips(hops, chip):
    length = line_length()
    listing = [(None, chip)]
    for hop in range(1, hops + 1):
        listing.append((chip - hop >= 0, chip - hop))
        listing.append((chip + hop < length, chip + hop))
    return listing


def each_copy(refs, target, sems, rows, chip, core, act):
    count = len(refs) // 2
    listing = entry_chips(count // 2, chip)
    for side in range(CORES):
        for index, (valid, origin) in enumerate(listing):
            number = side * count + index
            owner = CORES * origin + (core if side == 0 else 1 - core)

            def run(number=number, owner=owner):
                start = pl.multiple_of(owner * rows, rows)
                act(
                    pltpu.make_async_copy(
                        refs[number], target.at[pl.ds(start, rows), :], sems.at[owner]
                    )
                )

            if valid is None:
                run()
            else:
                pl.when(valid)(run)


def line_copies(refs, target, sems, rows, chip, core, act):
    for side, ref in enumerate(refs):
        for origin in range(ref.shape[0]):
            owner = CORES * origin + (core if side == 0 else 1 - core)
            start = pl.multiple_of(owner * rows, rows)
            act(
                pltpu.make_async_copy(
                    ref.at[origin], target.at[pl.ds(start, rows), :], sems.at[side, origin]
                )
            )


def fetch_line(*args):
    line_copies(*args, lambda copy: copy.start())
    line_copies(*args, lambda copy: copy.wait())


def start_copies(*args):
    each_copy(*args, lambda copy: copy.start())


def wait_copies(*args):
    each_copy(*args, lambda copy: copy.wait())


def head_parts(proj_ref, head):
    def part(index):
        start = (index * HEADS + head) * HEAD_DIM
        return proj_ref[:, start : start + HEAD_DIM]

    query, key, value = part(0), part(1), part(2)
    query_scale = lax.rsqrt(mean_last(query * query) + EPS)
    key_scale = lax.rsqrt(mean_last(key * key) + EPS)
    return query * query_scale, query_scale, key * key_scale, key_scale, value.astype(BF16)


def attn_probs_of(query_bf, key_bf, allowed):
    scores = dot(query_bf, key_bf, NT) * SCORE_SCALE
    expo = jnp.where(allowed, jnp.exp(scores), 0.0)
    return expo / jnp.sum(expo, axis=-1, keepdims=True)


def attend_rows(proj_ref, mask, heads_ref):
    allowed = mask > 0.5
    for head in range(HEADS):
        query_hat, _, key_hat, _, value_bf = head_parts(proj_ref, head)
        probs = attn_probs_of(query_hat.astype(BF16), key_hat.astype(BF16), allowed)
        out = dot(probs.astype(BF16), value_bf)
        heads_ref[:, head * HEAD_DIM : (head + 1) * HEAD_DIM] = out.astype(BF16)


def finish_rows(x, heads, out_w, gain_e, hidden_ref, expert_ref):
    hidden = x.astype(F32) + dot(heads, out_w)
    hidden_ref[...] = hidden
    rms = lax.rsqrt(mean_last(hidden * hidden) + EPS)
    expert_ref[...] = jnp.broadcast_to((hidden * rms * gain_e).astype(BF16), expert_ref.shape)


def early_kernel(count, depth, *refs):
    place, xf_ref, xb_ref, gain_a, mask_ref = refs[:5]
    mix_refs = refs[5 : 5 + count]
    sumf_ref, sumb_ref, normedf_ref, normedb_ref, allowed_ref = refs[5 + count : 10 + count]
    mix_w, normed, mix_sems = refs[10 + count :]
    allowed_ref[...] = mask_ref[...]
    chip, core = place[0], place[1]
    mix_w[...] = jnp.zeros_like(mix_w)
    start_copies(mix_refs, mix_w, mix_sems, depth, chip, core)
    rows = xf_ref.shape[0]
    for index, x_ref in enumerate((xf_ref, xb_ref)):
        x = x_ref[...].astype(F32)
        rms = lax.rsqrt(mean_last(x * x) + EPS)
        normed[index * rows : (index + 1) * rows, :] = (x * rms * gain_a[...]).astype(BF16)
    normedf_ref[...] = normed[:rows, :]
    normedb_ref[...] = normed[rows:, :]
    wait_copies(mix_refs, mix_w, mix_sems, depth, chip, core)
    columns = mix_w.shape[1]
    chunk = 512
    for begin in range(0, columns, chunk):
        piece = dot(normed[...], mix_w[:, begin : begin + chunk])
        sumf_ref[:, begin : begin + chunk] = piece[:rows]
        sumb_ref[:, begin : begin + chunk] = piece[rows:]


def last_copies(mix_refs, mix_w, sems, depth, length, chip, core, act):
    for which, end in ((0, length - 1), (1, 0)):

        @pl.when(chip == end)
        def _():
            for side in range(CORES):
                start = pl.multiple_of((core if side == 0 else 1 - core) * depth, depth)
                act(
                    pltpu.make_async_copy(
                        mix_refs[2 * side + which],
                        mix_w.at[pl.ds(start, depth), :],
                        sems.at[2 * side + which],
                    )
                )


def add_last(sum_ref, normed_ref, mix_w, proj_ref, chip, length):
    columns = mix_w.shape[1]
    block = mix_w.shape[0]
    chunk = 512
    for end in (0, length - 1):

        @pl.when(chip == end)
        def _():
            far = (length - 1 - end) * block
            for begin in range(0, columns, chunk):
                span = slice(begin, begin + chunk)
                piece = dot(normed_ref[:, far : far + block], mix_w[:, span])
                proj_ref[:, span] = sum_ref[:, span] + piece

    @pl.when((chip > 0) & (chip < length - 1))
    def _():
        proj_ref[...] = sum_ref[...]


def project_kernel(count, depth, length, micro, *refs):
    place, x_ref, sum_ref, normed_ref, gain_e, mask_ref = refs[:6]
    mix_refs = refs[6:10]
    out_refs = refs[10 : 10 + count]
    proj_ref, hidden_ref, expert_ref = refs[10 + count : 13 + count]
    mix_w, out_w, heads, mix_sems, out_sems = refs[13 + count :]
    chip, core = place[0], place[1]
    last_copies(mix_refs, mix_w, mix_sems, depth, length, chip, core, lambda copy: copy.start())
    start_copies(out_refs, out_w, out_sems, depth, chip, core)
    last_copies(mix_refs, mix_w, mix_sems, depth, length, chip, core, lambda copy: copy.wait())
    add_last(sum_ref, normed_ref, mix_w, proj_ref, chip, length)
    attend_rows(proj_ref, mask_ref[micro], heads)
    wait_copies(out_refs, out_w, out_sems, depth, chip, core)
    finish_rows(x_ref[...], heads[...], out_w[...], gain_e[...], hidden_ref, expert_ref)


def picked_gate(gates, me, expert_count, micro):
    lane = lax.broadcasted_iota(jnp.int32, gates.shape, 1)
    first = 2 * micro * expert_count + me
    hit = (lane == first) | (lane == first + expert_count)
    return jnp.sum(jnp.where(hit, gates, 0.0), axis=-1, keepdims=True)


def cotangent_kernel(rows, width, expert_count, *refs):
    place, down_ref, mine, other, act_ref, gate_ref, cot, sems = refs
    chip, core = place[0], place[1]
    me = CORES * chip + core
    fetch_line((mine, other), cot, sems, rows, chip, core)
    chunk = 2 * rows

    def step(index, carry):
        start = chunk_start(index, chunk)
        block = cot[pl.ds(start, chunk), :]
        gates = block[:, width:].astype(F32)
        grad_act = dot(block[:, :width], down_ref[...], NT)
        act_ref[pl.ds(start, chunk), :] = grad_act * picked_gate(gates, me, expert_count, 1)
        gate_ref[pl.ds(start, chunk), :] = jnp.broadcast_to(
            picked_gate(gates, me, expert_count, 0), (chunk, LANES)
        )
        return carry

    each_chunk(expert_count * rows // chunk, step)


def each_chunk(number, step):
    if number <= 4:
        for index in range(number):
            step(index, 0)
    else:
        lax.fori_loop(0, number, step, 0)


def chunk_start(index, chunk):
    return index * chunk if isinstance(index, int) else pl.multiple_of(index * chunk, chunk)


def give_back(result, mine_ref, other_ref, rows, core):
    for owner in range(mine_ref.shape[0]):
        for out_ref, side in ((mine_ref, core), (other_ref, 1 - core)):
            start = pl.multiple_of((CORES * owner + side) * rows, rows)
            out_ref[owner] = result[pl.ds(start, rows), :]


def expert_backward_kernel(rows, *refs):
    place, up_ref, act_ref = refs[:3]
    row_refs = refs[3:5]
    mine_ref, other_ref, tokens, result, sems = refs[5:]
    chip, core = place[0], place[1]
    fetch_line(row_refs, tokens, sems, rows, chip, core)
    chunk = 2 * rows

    def step(index, carry):
        start = chunk_start(index, chunk)
        pre = dot(tokens[pl.ds(start, chunk), :], up_ref[...], NT)
        square = pre * pre
        bend = jnp.tanh(GELU_C * pre * (1.0 + GELU_A * square))
        slope = 0.5 * (1.0 + bend) + 0.5 * pre * (1.0 - bend * bend) * (
            GELU_C * (1.0 + 3.0 * GELU_A * square)
        )
        grad = (act_ref[pl.ds(start, chunk), :] * slope).astype(BF16)
        result[pl.ds(start, chunk), :] = dot(grad, up_ref[...]).astype(BF16)
        return carry

    each_chunk(tokens.shape[0] // chunk, step)
    give_back(result, mine_ref, other_ref, rows, core)


def expert_forward_kernel(rows, *refs):
    place, up_ref, down_ref, gate_ref = refs[:4]
    row_refs = refs[4:6]
    mine_ref, other_ref, tokens, result, sems = refs[6:]
    chip, core = place[0], place[1]
    fetch_line(row_refs, tokens, sems, rows, chip, core)
    chunk = 2 * rows

    def step(index, carry):
        start = chunk_start(index, chunk)
        pre = dot(tokens[pl.ds(start, chunk), :], up_ref[...], NT)
        bend = jnp.tanh(GELU_C * pre * (1.0 + GELU_A * (pre * pre)))
        active = (0.5 * pre * (1.0 + bend)).astype(BF16)
        out = dot(active, down_ref[...])
        gate = gate_ref[pl.ds(start, chunk), :][:, :1]
        result[pl.ds(start, chunk), :] = (gate * out).astype(BF16)
        return carry

    each_chunk(tokens.shape[0] // chunk, step)
    give_back(result, mine_ref, other_ref, rows, core)


def heads_backward_kernel(count, depth, *refs):
    place, cot_ref, hidden_ref, proj_ref, gain_e, mask_ref, part_ref = refs[:7]
    out_refs = refs[7 : 7 + count]
    mixed_ref, grad_ref, out_w, out_sems = refs[7 + count :]
    chip, core = place[0], place[1]
    start_copies(out_refs, out_w, out_sems, depth, chip, core)
    grad_moe = part_ref[0].astype(F32)
    for index in range(1, part_ref.shape[0]):
        grad_moe = grad_moe + part_ref[index].astype(F32)
    hidden = hidden_ref[...]
    rms_two = lax.rsqrt(mean_last(hidden * hidden) + EPS)
    normal_two = hidden * rms_two
    grad_two = grad_moe * gain_e[...]
    grad_hidden = cot_ref[...].astype(F32) + rms_two * (
        grad_two - normal_two * mean_last(grad_two * normal_two)
    )
    grad_ref[...] = grad_hidden
    wait_copies(out_refs, out_w, out_sems, depth, chip, core)
    grad_heads = dot(grad_hidden.astype(BF16), out_w[...], NT).astype(BF16)
    allowed = mask_ref[1] > 0.5
    for head in range(HEADS):
        query_hat, query_scale, key_hat, key_scale, value_bf = head_parts(proj_ref, head)
        query_bf, key_bf = query_hat.astype(BF16), key_hat.astype(BF16)
        probs = attn_probs_of(query_bf, key_bf, allowed)
        grad_out = grad_heads[:, head * HEAD_DIM : (head + 1) * HEAD_DIM]
        grad_probs = dot(grad_out, value_bf, NT)
        grad_value = dot(probs.astype(BF16), grad_out, TN)
        inner = jnp.sum(probs * grad_probs, axis=-1, keepdims=True)
        grad_scores = (probs * (grad_probs - inner) * SCORE_SCALE).astype(BF16)
        grad_qhat = dot(grad_scores, key_bf)
        grad_khat = dot(grad_scores, query_bf, TN)
        grad_query = query_scale * (grad_qhat - query_hat * mean_last(grad_qhat * query_hat))
        grad_key = key_scale * (grad_khat - key_hat * mean_last(grad_khat * key_hat))
        for index, grad in enumerate((grad_query, grad_key, grad_value)):
            start = (index * HEADS + head) * HEAD_DIM
            mixed_ref[:, start : start + HEAD_DIM] = grad.astype(BF16)


def entry_backward_kernel(count, depth, *refs):
    place, x_ref, mixed_ref, grad_ref, gain_a = refs[:5]
    mix_refs = refs[5 : 5 + count]
    result_ref = refs[5 + count]
    mix_w, mix_sems = refs[6 + count :]
    chip, core = place[0], place[1]
    start_copies(mix_refs, mix_w, mix_sems, depth, chip, core)
    wait_copies(mix_refs, mix_w, mix_sems, depth, chip, core)
    grad_normed = dot(mixed_ref[...], mix_w[...], NT)
    x = x_ref[...].astype(F32)
    rms_one = lax.rsqrt(mean_last(x * x) + EPS)
    normal_one = x * rms_one
    grad_one = grad_normed * gain_a[...]
    result = grad_ref[...] + rms_one * (grad_one - normal_one * mean_last(grad_one * normal_one))
    result_ref[...] = result.astype(BF16)


def shaped(shape, kind):
    return jax.ShapeDtypeStruct(shape, kind)


def dma(count):
    return pltpu.SemaphoreType.DMA(count if isinstance(count, tuple) else (count,))


def call(kernel, outs, specs, out_specs, scratch, args):
    return pl.pallas_call(
        kernel,
        out_shape=outs,
        in_specs=specs,
        out_specs=out_specs,
        scratch_shapes=scratch,
        compiler_params=PARAMS,
    )(*args)


def dense_gates(routes, logits, expert_count):
    gates = jax.nn.sigmoid(logits)
    hit = routes[..., None] == jnp.arange(expert_count, dtype=jnp.int32)
    return jnp.sum(jnp.where(hit, gates[..., None], 0.0), axis=2)


def gate_columns(routes, logits, expert_count):
    gates = dense_gates(routes, logits, expert_count)
    high = lax.reduce_precision(gates, 8, 7)
    both = jnp.stack([high, gates - high], axis=1).astype(BF16)
    rows = jnp.transpose(both, (2, 0, 1, 3)).reshape(both.shape[2], -1)
    return jnp.pad(rows, ((0, 0), (0, LANES - rows.shape[1])))


def allowed_of(mask_blocks):
    frame_block = jnp.arange(FRAMES, dtype=jnp.int32) // BLOCK
    spread = (frame_block[:, None] == jnp.arange(FRAMES // BLOCK)[None, :]).astype(F32)
    eye = jnp.eye(FRAMES // BLOCK, dtype=F32)
    open_blocks = jnp.maximum((mask_blocks == 1).astype(F32), eye)
    return jnp.einsum("ib,mbc,jc->mij", spread, open_blocks, spread)


def local(
    handoff_forward,
    stashed_input,
    relay_cotangents,
    attention_gain,
    expert_gain,
    w_qkv,
    w_out,
    w_up,
    w_down,
    routes,
    gate_logits,
    block_mask,
):
    length = line_length()
    expert_count = lax.axis_size("expert")
    me = lax.axis_index("expert")
    place = jnp.stack([me // CORES, me % CORES]).astype(jnp.int32)
    tokens, width = handoff_forward.shape
    depth = w_qkv.shape[1]
    total = expert_count * tokens
    columns = w_qkv.shape[2]
    up_weight = jnp.swapaxes(w_up[0, 0], 0, 1)
    down_weight = w_down[0, 0]
    hidden_units = up_weight.shape[0]
    count = CORES * (2 * length - 1)

    mixers = with_partner(relayed(w_qkv[0]))
    outers = with_partner(relayed(w_out[0]))
    arriving = passed_along(handoff_forward, 1)
    cotangent = passed_along(relay_cotangents, -1)
    gates = gate_columns(routes, gate_logits, expert_count)
    cot_block = jnp.concatenate([cotangent, gates], axis=1)
    cots = spread(jnp.broadcast_to(cot_block[None], (length,) + cot_block.shape))
    mask = allowed_of(block_mask[:, 0])

    half = count // 2
    early_mix = mixers[: half - 2] + mixers[half : count - 2]
    last_mix = mixers[half - 2 : half] + mixers[count - 2 :]
    early = len(early_mix)
    sum_fwd, sum_bwd, normed_fwd, normed_bwd, mask = call(
        functools.partial(early_kernel, early, depth),
        (
            shaped((tokens, columns), F32),
            shaped((tokens, columns), F32),
            shaped((tokens, width), BF16),
            shaped((tokens, width), BF16),
            shaped(mask.shape, F32),
        ),
        [SMEM] + [VMEM] * 4 + [ANY] * early,
        (VMEM,) * 5,
        [
            pltpu.VMEM((width, columns), BF16),
            pltpu.VMEM((2 * tokens, width), BF16),
            dma(expert_count),
        ],
        [place, arriving, stashed_input, attention_gain, mask] + early_mix,
    )

    def attended(micro, x, sums, normed):
        return call(
            functools.partial(project_kernel, count, depth, length, micro),
            (
                shaped((tokens, columns), F32),
                shaped((tokens, width), F32),
                shaped((length, tokens, width), BF16),
            ),
            [SMEM] + [VMEM] * 5 + [ANY] * (4 + count),
            (VMEM,) * 3,
            [
                pltpu.VMEM((CORES * depth, columns), BF16),
                pltpu.VMEM((width, width), BF16),
                pltpu.VMEM((tokens, width), BF16),
                dma(4),
                dma(expert_count),
            ],
            [place, x, sums, normed, expert_gain, mask] + last_mix + outers,
        )

    proj_bwd, hidden_bwd, expert_bwd = attended(1, stashed_input, sum_bwd, normed_bwd)
    rows_bwd = spread(expert_bwd)

    _, hidden_fwd, expert_fwd = attended(0, arriving, sum_fwd, normed_fwd)
    rows_fwd = spread(expert_fwd)

    grad_act, gate_fwd = call(
        functools.partial(cotangent_kernel, tokens, width, expert_count),
        (shaped((total, hidden_units), F32), shaped((total, LANES), F32)),
        [SMEM, VMEM] + [ANY] * 2,
        (VMEM,) * 2,
        [pltpu.VMEM((total, width + LANES), BF16), dma((CORES, length))],
        [place, down_weight] + cots,
    )

    pair = (shaped((length, tokens, width), BF16),) * 2

    def expert_scratch(sems):
        return [pltpu.VMEM((total, width), BF16), pltpu.VMEM((total, width), BF16), dma(sems)]

    mine, other = call(
        functools.partial(expert_backward_kernel, tokens),
        pair,
        [SMEM, VMEM, VMEM] + [ANY] * 2,
        (VMEM,) * 2,
        expert_scratch((CORES, length)),
        [place, up_weight, grad_act] + rows_bwd,
    )
    grad_parts = across(mine + swapped(other))

    mine, other = call(
        functools.partial(expert_forward_kernel, tokens),
        pair,
        [SMEM, VMEM, VMEM, VMEM] + [ANY] * 2,
        (VMEM,) * 2,
        expert_scratch((CORES, length)),
        [place, up_weight, down_weight, gate_fwd] + rows_fwd,
    )
    moe_parts = across(mine + swapped(other))

    grad_mixed, grad_hidden = call(
        functools.partial(heads_backward_kernel, count, depth),
        (shaped((tokens, columns), BF16), shaped((tokens, width), F32)),
        [SMEM] + [VMEM] * 6 + [ANY] * count,
        (VMEM,) * 2,
        [pltpu.VMEM((width, width), BF16), dma(expert_count)],
        [place, cotangent, hidden_bwd, proj_bwd, expert_gain, mask, grad_parts]
        + outers,
    )
    derivative = call(
        functools.partial(entry_backward_kernel, count, depth),
        shaped((tokens, width), BF16),
        [SMEM] + [VMEM] * 4 + [ANY] * count,
        VMEM,
        [
            pltpu.VMEM((width, columns), BF16),
            dma(expert_count),
        ],
        [place, stashed_input, grad_mixed, grad_hidden, attention_gain] + mixers,
    )

    layer_output = hidden_fwd + jnp.sum(moe_parts.astype(F32), axis=0)
    return (layer_output.astype(BF16), derivative)


def solution(mesh):
    placed = (
        P(("section", "expert"), None),
        P(("section", "expert"), None),
        P(("section", "expert"), None),
        P("section", None),
        P("section", None),
        P("section", "expert", None),
        P("section", "expert", None),
        P("section", "expert", None, None),
        P("section", "expert", None, None),
        P(None, ("section", "expert"), None),
        P(None, ("section", "expert"), None),
        P(None, ("section", "expert"), None, None),
    )

    return jax.shard_map(
        local,
        mesh=mesh,
        in_specs=placed,
        out_specs=(P(("section", "expert"), None), P(("section", "expert"), None)),
        check_vma=False,
    )
```

```python
import functools

import jax
import jax.numpy as jnp
from jax import lax
from jax.experimental import pallas as pl
from jax.experimental.pallas import tpu as pltpu
from jax.sharding import PartitionSpec as P


HEADS = 8
HEAD_DIM = 128
FRAMES = 128
BLOCK = 16
CORES = 2
LANES = 128

EPS = 1e-06
SCORE_SCALE = HEAD_DIM ** (-0.5)
GELU_C = 0.7978845608028654
GELU_A = 0.044715


F32 = jnp.float32
BF16 = jnp.bfloat16
NT = (((1,), (1,)), ((), ()))
TN = (((0,), (0,)), ((), ()))
ANY = pl.BlockSpec(memory_space=pltpu.HBM)
SMEM = pl.BlockSpec(memory_space=pltpu.SMEM)
VMEM = pl.BlockSpec(memory_space=pltpu.VMEM)
PARAMS = pltpu.CompilerParams(vmem_limit_bytes=56 * 1024 * 1024)


def dot(a, b, dims=(((1,), (0,)), ((), ()))):
    return lax.dot_general(a, b, dims, preferred_element_type=F32)


def mean_last(values):
    return jnp.mean(values, axis=-1, keepdims=True)


def passed_along(value, steps):
    count = lax.axis_size("section")
    pairs = [(source, (source + steps) % count) for source in range(count)]
    return lax.ppermute(value, "section", pairs)


def line_length():
    return lax.axis_size("expert") // CORES


def chip_pairs(sources, step):
    return [
        (CORES * chip + core, CORES * (chip + step) + core)
        for chip in sources
        for core in range(CORES)
    ]


def swapped(value):
    count = lax.axis_size("expert")
    return lax.ppermute(value, "expert", [(i, i ^ 1) for i in range(count)])


def hop(value, sources, move):
    return lax.ppermute(value, "expert", chip_pairs(sources, move))


def relayed(value):
    length = line_length()
    entries = [value]
    up = down = value
    for step in range(1, length):
        up = hop(up, range(step - 1, length - 1), 1)
        down = hop(down, range(1, length - step + 1), -1)
        entries += [up, down]
    return entries


def with_partner(entries):
    return entries + [swapped(block) for block in entries]


def across(blocks):
    length = line_length()
    groups = [[CORES * chip + core for chip in range(length)] for core in range(CORES)]
    return lax.all_to_all(
        blocks, "expert", split_axis=0, concat_axis=0, axis_index_groups=groups, tiled=True
    )


def spread(copies):
    mine = across(copies)
    return [mine, swapped(mine)]


def entry_chips(hops, chip):
    length = line_length()
    listing = [(None, chip)]
    for hop in range(1, hops + 1):
        listing.append((chip - hop >= 0, chip - hop))
        listing.append((chip + hop < length, chip + hop))
    return listing


def each_copy(refs, target, sems, rows, chip, core, act):
    count = len(refs) // 2
    listing = entry_chips(count // 2, chip)
    for side in range(CORES):
        for index, (valid, origin) in enumerate(listing):
            number = side * count + index
            owner = CORES * origin + (core if side == 0 else 1 - core)

            def run(number=number, owner=owner):
                start = pl.multiple_of(owner * rows, rows)
                act(
                    pltpu.make_async_copy(
                        refs[number], target.at[pl.ds(start, rows), :], sems.at[owner]
                    )
                )

            if valid is None:
                run()
            else:
                pl.when(valid)(run)


def line_copies(refs, target, sems, rows, chip, core, act):
    for side, ref in enumerate(refs):
        for origin in range(ref.shape[0]):
            owner = CORES * origin + (core if side == 0 else 1 - core)
            start = pl.multiple_of(owner * rows, rows)
            act(
                pltpu.make_async_copy(
                    ref.at[origin], target.at[pl.ds(start, rows), :], sems.at[side, origin]
                )
            )


def fetch_line(*args):
    line_copies(*args, lambda copy: copy.start())
    line_copies(*args, lambda copy: copy.wait())


def start_copies(*args):
    each_copy(*args, lambda copy: copy.start())


def wait_copies(*args):
    each_copy(*args, lambda copy: copy.wait())


def head_parts(proj_ref, head):
    def part(index):
        start = (index * HEADS + head) * HEAD_DIM
        return proj_ref[:, start : start + HEAD_DIM]

    query, key, value = part(0), part(1), part(2)
    query_scale = lax.rsqrt(mean_last(query * query) + EPS)
    key_scale = lax.rsqrt(mean_last(key * key) + EPS)
    return query * query_scale, query_scale, key * key_scale, key_scale, value.astype(BF16)


def attn_probs_of(query_bf, key_bf, allowed):
    scores = dot(query_bf, key_bf, NT) * SCORE_SCALE
    expo = jnp.where(allowed, jnp.exp(scores), 0.0)
    return expo / jnp.sum(expo, axis=-1, keepdims=True)


def attend_rows(proj_ref, mask, heads_ref):
    allowed = mask > 0.5
    for head in range(HEADS):
        query_hat, _, key_hat, _, value_bf = head_parts(proj_ref, head)
        probs = attn_probs_of(query_hat.astype(BF16), key_hat.astype(BF16), allowed)
        out = dot(probs.astype(BF16), value_bf)
        heads_ref[:, head * HEAD_DIM : (head + 1) * HEAD_DIM] = out.astype(BF16)


def finish_rows(x, heads, out_w, gain_e, hidden_ref, expert_ref):
    hidden = x.astype(F32) + dot(heads, out_w)
    hidden_ref[...] = hidden
    rms = lax.rsqrt(mean_last(hidden * hidden) + EPS)
    expert_ref[...] = jnp.broadcast_to((hidden * rms * gain_e).astype(BF16), expert_ref.shape)


def early_kernel(count, depth, *refs):
    place, xf_ref, xb_ref, gain_a, mask_ref = refs[:5]
    mix_refs = refs[5 : 5 + count]
    sumf_ref, sumb_ref, normedf_ref, normedb_ref, allowed_ref = refs[5 + count : 10 + count]
    mix_w, normed, mix_sems = refs[10 + count :]
    allowed_ref[...] = mask_ref[...]
    chip, core = place[0], place[1]
    mix_w[...] = jnp.zeros_like(mix_w)
    start_copies(mix_refs, mix_w, mix_sems, depth, chip, core)
    rows = xf_ref.shape[0]
    for index, x_ref in enumerate((xf_ref, xb_ref)):
        x = x_ref[...].astype(F32)
        rms = lax.rsqrt(mean_last(x * x) + EPS)
        normed[index * rows : (index + 1) * rows, :] = (x * rms * gain_a[...]).astype(BF16)
    normedf_ref[...] = normed[:rows, :]
    normedb_ref[...] = normed[rows:, :]
    wait_copies(mix_refs, mix_w, mix_sems, depth, chip, core)
    columns = mix_w.shape[1]
    chunk = 512
    for begin in range(0, columns, chunk):
        piece = dot(normed[...], mix_w[:, begin : begin + chunk])
        sumf_ref[:, begin : begin + chunk] = piece[:rows]
        sumb_ref[:, begin : begin + chunk] = piece[rows:]


def last_copies(mix_refs, mix_w, sems, depth, length, chip, core, act):
    for which, end in ((0, length - 1), (1, 0)):

        @pl.when(chip == end)
        def _():
            for side in range(CORES):
                start = pl.multiple_of((core if side == 0 else 1 - core) * depth, depth)
                act(
                    pltpu.make_async_copy(
                        mix_refs[2 * side + which],
                        mix_w.at[pl.ds(start, depth), :],
                        sems.at[2 * side + which],
                    )
                )


def add_last(sum_ref, normed_ref, mix_w, proj_ref, chip, length):
    columns = mix_w.shape[1]
    block = mix_w.shape[0]
    chunk = 512
    for end in (0, length - 1):

        @pl.when(chip == end)
        def _():
            far = (length - 1 - end) * block
            for begin in range(0, columns, chunk):
                span = slice(begin, begin + chunk)
                piece = dot(normed_ref[:, far : far + block], mix_w[:, span])
                proj_ref[:, span] = sum_ref[:, span] + piece

    @pl.when((chip > 0) & (chip < length - 1))
    def _():
        proj_ref[...] = sum_ref[...]


def project_kernel(count, depth, length, micro, *refs):
    place, x_ref, sum_ref, normed_ref, gain_e, mask_ref = refs[:6]
    mix_refs = refs[6:10]
    out_refs = refs[10 : 10 + count]
    proj_ref, hidden_ref, expert_ref = refs[10 + count : 13 + count]
    mix_w, out_w, heads, mix_sems, out_sems = refs[13 + count :]
    chip, core = place[0], place[1]
    last_copies(mix_refs, mix_w, mix_sems, depth, length, chip, core, lambda copy: copy.start())
    start_copies(out_refs, out_w, out_sems, depth, chip, core)
    last_copies(mix_refs, mix_w, mix_sems, depth, length, chip, core, lambda copy: copy.wait())
    add_last(sum_ref, normed_ref, mix_w, proj_ref, chip, length)
    attend_rows(proj_ref, mask_ref[micro], heads)
    wait_copies(out_refs, out_w, out_sems, depth, chip, core)
    finish_rows(x_ref[...], heads[...], out_w[...], gain_e[...], hidden_ref, expert_ref)


def picked_gate(gates, me, expert_count, micro):
    lane = lax.broadcasted_iota(jnp.int32, gates.shape, 1)
    first = 2 * micro * expert_count + me
    hit = (lane == first) | (lane == first + expert_count)
    return jnp.sum(jnp.where(hit, gates, 0.0), axis=-1, keepdims=True)


def cotangent_kernel(rows, expert_count, *refs):
    place, down_ref = refs[:2]
    act_ref, gate_ref, cot, columns, sems, gate_sems = refs[6:]
    chip, core = place[0], place[1]
    me = CORES * chip + core
    fetch_line(refs[4:6], columns, gate_sems, rows, chip, core)
    fetch_line(refs[2:4], cot, sems, rows, chip, core)
    chunk = 2 * rows

    def step(index, carry):
        start = chunk_start(index, chunk)
        gates = columns[pl.ds(start, chunk), :].astype(F32)
        grad_act = dot(cot[pl.ds(start, chunk), :], down_ref[...], NT)
        act_ref[pl.ds(start, chunk), :] = grad_act * picked_gate(gates, me, expert_count, 1)
        gate_ref[pl.ds(start, chunk), :] = jnp.broadcast_to(
            picked_gate(gates, me, expert_count, 0), (chunk, LANES)
        )
        return carry

    each_chunk(expert_count * rows // chunk, step)


def each_chunk(number, step):
    if number <= 4:
        for index in range(number):
            step(index, 0)
    else:
        lax.fori_loop(0, number, step, 0)


def chunk_start(index, chunk):
    return index * chunk if isinstance(index, int) else pl.multiple_of(index * chunk, chunk)


def give_back(result, mine_ref, other_ref, rows, core):
    for owner in range(mine_ref.shape[0]):
        for out_ref, side in ((mine_ref, core), (other_ref, 1 - core)):
            start = pl.multiple_of((CORES * owner + side) * rows, rows)
            out_ref[owner] = result[pl.ds(start, rows), :]


def expert_backward_kernel(rows, *refs):
    place, up_ref, act_ref = refs[:3]
    row_refs = refs[3:5]
    mine_ref, other_ref, tokens, result, sems = refs[5:]
    chip, core = place[0], place[1]
    fetch_line(row_refs, tokens, sems, rows, chip, core)
    chunk = 2 * rows

    def step(index, carry):
        start = chunk_start(index, chunk)
        pre = dot(tokens[pl.ds(start, chunk), :], up_ref[...], NT)
        square = pre * pre
        bend = jnp.tanh(GELU_C * pre * (1.0 + GELU_A * square))
        slope = 0.5 * (1.0 + bend) + 0.5 * pre * (1.0 - bend * bend) * (
            GELU_C * (1.0 + 3.0 * GELU_A * square)
        )
        grad = (act_ref[pl.ds(start, chunk), :] * slope).astype(BF16)
        result[pl.ds(start, chunk), :] = dot(grad, up_ref[...]).astype(BF16)
        return carry

    each_chunk(tokens.shape[0] // chunk, step)
    give_back(result, mine_ref, other_ref, rows, core)


def expert_forward_kernel(rows, *refs):
    place, up_ref, down_ref, gate_ref = refs[:4]
    row_refs = refs[4:6]
    mine_ref, other_ref, tokens, result, sems = refs[6:]
    chip, core = place[0], place[1]
    fetch_line(row_refs, tokens, sems, rows, chip, core)
    chunk = 2 * rows

    def step(index, carry):
        start = chunk_start(index, chunk)
        pre = dot(tokens[pl.ds(start, chunk), :], up_ref[...], NT)
        bend = jnp.tanh(GELU_C * pre * (1.0 + GELU_A * (pre * pre)))
        active = (0.5 * pre * (1.0 + bend)).astype(BF16)
        out = dot(active, down_ref[...])
        gate = gate_ref[pl.ds(start, chunk), :][:, :1]
        result[pl.ds(start, chunk), :] = (gate * out).astype(BF16)
        return carry

    each_chunk(tokens.shape[0] // chunk, step)
    give_back(result, mine_ref, other_ref, rows, core)


def heads_backward_kernel(count, depth, *refs):
    place, cot_ref, hidden_ref, proj_ref, gain_e, mask_ref, part_ref = refs[:7]
    out_refs = refs[7 : 7 + count]
    mixed_ref, grad_ref, out_w, out_sems = refs[7 + count :]
    chip, core = place[0], place[1]
    start_copies(out_refs, out_w, out_sems, depth, chip, core)
    grad_moe = part_ref[0].astype(F32)
    for index in range(1, part_ref.shape[0]):
        grad_moe = grad_moe + part_ref[index].astype(F32)
    hidden = hidden_ref[...]
    rms_two = lax.rsqrt(mean_last(hidden * hidden) + EPS)
    normal_two = hidden * rms_two
    grad_two = grad_moe * gain_e[...]
    grad_hidden = cot_ref[...].astype(F32) + rms_two * (
        grad_two - normal_two * mean_last(grad_two * normal_two)
    )
    grad_ref[...] = grad_hidden
    wait_copies(out_refs, out_w, out_sems, depth, chip, core)
    grad_heads = dot(grad_hidden.astype(BF16), out_w[...], NT).astype(BF16)
    allowed = mask_ref[1] > 0.5
    for head in range(HEADS):
        query_hat, query_scale, key_hat, key_scale, value_bf = head_parts(proj_ref, head)
        query_bf, key_bf = query_hat.astype(BF16), key_hat.astype(BF16)
        probs = attn_probs_of(query_bf, key_bf, allowed)
        grad_out = grad_heads[:, head * HEAD_DIM : (head + 1) * HEAD_DIM]
        grad_probs = dot(grad_out, value_bf, NT)
        grad_value = dot(probs.astype(BF16), grad_out, TN)
        inner = jnp.sum(probs * grad_probs, axis=-1, keepdims=True)
        grad_scores = (probs * (grad_probs - inner) * SCORE_SCALE).astype(BF16)
        grad_qhat = dot(grad_scores, key_bf)
        grad_khat = dot(grad_scores, query_bf, TN)
        grad_query = query_scale * (grad_qhat - query_hat * mean_last(grad_qhat * query_hat))
        grad_key = key_scale * (grad_khat - key_hat * mean_last(grad_khat * key_hat))
        for index, grad in enumerate((grad_query, grad_key, grad_value)):
            start = (index * HEADS + head) * HEAD_DIM
            mixed_ref[:, start : start + HEAD_DIM] = grad.astype(BF16)


def entry_backward_kernel(count, depth, *refs):
    place, x_ref, mixed_ref, grad_ref, gain_a = refs[:5]
    mix_refs = refs[5 : 5 + count]
    result_ref = refs[5 + count]
    mix_w, mix_sems = refs[6 + count :]
    chip, core = place[0], place[1]
    start_copies(mix_refs, mix_w, mix_sems, depth, chip, core)
    wait_copies(mix_refs, mix_w, mix_sems, depth, chip, core)
    grad_normed = dot(mixed_ref[...], mix_w[...], NT)
    x = x_ref[...].astype(F32)
    rms_one = lax.rsqrt(mean_last(x * x) + EPS)
    normal_one = x * rms_one
    grad_one = grad_normed * gain_a[...]
    result = grad_ref[...] + rms_one * (grad_one - normal_one * mean_last(grad_one * normal_one))
    result_ref[...] = result.astype(BF16)


def shaped(shape, kind):
    return jax.ShapeDtypeStruct(shape, kind)


def dma(count):
    return pltpu.SemaphoreType.DMA(count if isinstance(count, tuple) else (count,))


def call(kernel, outs, specs, out_specs, scratch, args):
    return pl.pallas_call(
        kernel,
        out_shape=outs,
        in_specs=specs,
        out_specs=out_specs,
        scratch_shapes=scratch,
        compiler_params=PARAMS,
    )(*args)


def dense_gates(routes, logits, expert_count):
    gates = jax.nn.sigmoid(logits)
    hit = routes[..., None] == jnp.arange(expert_count, dtype=jnp.int32)
    return jnp.sum(jnp.where(hit, gates[..., None], 0.0), axis=2)


def gate_columns(routes, logits, expert_count):
    gates = dense_gates(routes, logits, expert_count)
    high = lax.reduce_precision(gates, 8, 7)
    both = jnp.stack([high, gates - high], axis=1).astype(BF16)
    rows = jnp.transpose(both, (2, 0, 1, 3)).reshape(both.shape[2], -1)
    return jnp.pad(rows, ((0, 0), (0, LANES - rows.shape[1])))


def allowed_of(mask_blocks):
    frame_block = jnp.arange(FRAMES, dtype=jnp.int32) // BLOCK
    spread = (frame_block[:, None] == jnp.arange(FRAMES // BLOCK)[None, :]).astype(F32)
    eye = jnp.eye(FRAMES // BLOCK, dtype=F32)
    open_blocks = jnp.maximum((mask_blocks == 1).astype(F32), eye)
    return jnp.einsum("ib,mbc,jc->mij", spread, open_blocks, spread)


def local(
    handoff_forward,
    stashed_input,
    relay_cotangents,
    attention_gain,
    expert_gain,
    w_qkv,
    w_out,
    w_up,
    w_down,
    routes,
    gate_logits,
    block_mask,
):
    length = line_length()
    expert_count = lax.axis_size("expert")
    me = lax.axis_index("expert")
    place = jnp.stack([me // CORES, me % CORES]).astype(jnp.int32)
    tokens, width = handoff_forward.shape
    depth = w_qkv.shape[1]
    total = expert_count * tokens
    columns = w_qkv.shape[2]
    up_weight = jnp.swapaxes(w_up[0, 0], 0, 1)
    down_weight = w_down[0, 0]
    hidden_units = up_weight.shape[0]
    count = CORES * (2 * length - 1)

    mixers = with_partner(relayed(w_qkv[0]))
    outers = with_partner(relayed(w_out[0]))
    arriving = passed_along(handoff_forward, 1)
    cotangent = passed_along(relay_cotangents, -1)
    gates = gate_columns(routes, gate_logits, expert_count)
    cots = spread(jnp.broadcast_to(cotangent[None], (length,) + cotangent.shape))
    gate_blocks = spread(jnp.broadcast_to(gates[None], (length,) + gates.shape))
    mask = allowed_of(block_mask[:, 0])

    half = count // 2
    early_mix = mixers[: half - 2] + mixers[half : count - 2]
    last_mix = mixers[half - 2 : half] + mixers[count - 2 :]
    early = len(early_mix)
    sum_fwd, sum_bwd, normed_fwd, normed_bwd, mask = call(
        functools.partial(early_kernel, early, depth),
        (
            shaped((tokens, columns), F32),
            shaped((tokens, columns), F32),
            shaped((tokens, width), BF16),
            shaped((tokens, width), BF16),
            shaped(mask.shape, F32),
        ),
        [SMEM] + [VMEM] * 4 + [ANY] * early,
        (VMEM,) * 5,
        [
            pltpu.VMEM((width, columns), BF16),
            pltpu.VMEM((2 * tokens, width), BF16),
            dma(expert_count),
        ],
        [place, arriving, stashed_input, attention_gain, mask] + early_mix,
    )

    def attended(micro, x, sums, normed):
        return call(
            functools.partial(project_kernel, count, depth, length, micro),
            (
                shaped((tokens, columns), F32),
                shaped((tokens, width), F32),
                shaped((length, tokens, width), BF16),
            ),
            [SMEM] + [VMEM] * 5 + [ANY] * (4 + count),
            (VMEM,) * 3,
            [
                pltpu.VMEM((CORES * depth, columns), BF16),
                pltpu.VMEM((width, width), BF16),
                pltpu.VMEM((tokens, width), BF16),
                dma(4),
                dma(expert_count),
            ],
            [place, x, sums, normed, expert_gain, mask] + last_mix + outers,
        )

    proj_bwd, hidden_bwd, expert_bwd = attended(1, stashed_input, sum_bwd, normed_bwd)
    rows_bwd = spread(expert_bwd)

    _, hidden_fwd, expert_fwd = attended(0, arriving, sum_fwd, normed_fwd)
    rows_fwd = spread(expert_fwd)

    grad_act, gate_fwd = call(
        functools.partial(cotangent_kernel, tokens, expert_count),
        (shaped((total, hidden_units), F32), shaped((total, LANES), F32)),
        [SMEM, VMEM] + [ANY] * 4,
        (VMEM,) * 2,
        [
            pltpu.VMEM((total, width), BF16),
            pltpu.VMEM((total, LANES), BF16),
            dma((CORES, length)),
            dma((CORES, length)),
        ],
        [place, down_weight] + cots + gate_blocks,
    )

    pair = (shaped((length, tokens, width), BF16),) * 2

    def expert_scratch(sems):
        return [pltpu.VMEM((total, width), BF16), pltpu.VMEM((total, width), BF16), dma(sems)]

    mine, other = call(
        functools.partial(expert_backward_kernel, tokens),
        pair,
        [SMEM, VMEM, VMEM] + [ANY] * 2,
        (VMEM,) * 2,
        expert_scratch((CORES, length)),
        [place, up_weight, grad_act] + rows_bwd,
    )
    grad_parts = across(mine + swapped(other))

    mine, other = call(
        functools.partial(expert_forward_kernel, tokens),
        pair,
        [SMEM, VMEM, VMEM, VMEM] + [ANY] * 2,
        (VMEM,) * 2,
        expert_scratch((CORES, length)),
        [place, up_weight, down_weight, gate_fwd] + rows_fwd,
    )
    moe_parts = across(mine + swapped(other))

    grad_mixed, grad_hidden = call(
        functools.partial(heads_backward_kernel, count, depth),
        (shaped((tokens, columns), BF16), shaped((tokens, width), F32)),
        [SMEM] + [VMEM] * 6 + [ANY] * count,
        (VMEM,) * 2,
        [pltpu.VMEM((width, width), BF16), dma(expert_count)],
        [place, cotangent, hidden_bwd, proj_bwd, expert_gain, mask, grad_parts]
        + outers,
    )
    derivative = call(
        functools.partial(entry_backward_kernel, count, depth),
        shaped((tokens, width), BF16),
        [SMEM] + [VMEM] * 4 + [ANY] * count,
        VMEM,
        [
            pltpu.VMEM((width, columns), BF16),
            dma(expert_count),
        ],
        [place, stashed_input, grad_mixed, grad_hidden, attention_gain] + mixers,
    )

    layer_output = hidden_fwd + jnp.sum(moe_parts.astype(F32), axis=0)
    return (layer_output.astype(BF16), derivative)


def solution(mesh):
    placed = (
        P(("section", "expert"), None),
        P(("section", "expert"), None),
        P(("section", "expert"), None),
        P("section", None),
        P("section", None),
        P("section", "expert", None),
        P("section", "expert", None),
        P("section", "expert", None, None),
        P("section", "expert", None, None),
        P(None, ("section", "expert"), None),
        P(None, ("section", "expert"), None),
        P(None, ("section", "expert"), None, None),
    )

    return jax.shard_map(
        local,
        mesh=mesh,
        in_specs=placed,
        out_specs=(P(("section", "expert"), None), P(("section", "expert"), None)),
        check_vma=False,
    )
```
